256 devices in a mesh: gx: 16 (over z_hi, x), gy: 16 (over z_lo, y, core).
Axes of the slice: x: 4, y: 4, z: 8 (z_hi: 4, z_lo: 2; z = z_hi * 2 + z_lo), core: 2. Of those that a mesh axis runs over, the one named last changes fastest.
Arguments:
- features: bfloat16 [16, 16, 16, 48, 512], P('gx', 'gy'), may hold values from -6 to 6
- block_slots: int32 [16, 16, 16], P('gx', 'gy'), may hold values from 0 to 15, as said below
- block_count: int32 [16, 16], P('gx', 'gy'), may hold values from 2 to 16
- cotangent: bfloat16 [16, 16, 16, 48, 512], P('gx', 'gy'), may hold values from -6 to 6
- fine_weight: bfloat16 [48, 27, 48], replicated, may hold values from -0.15625 to 0.15625
- down_weight: bfloat16 [48, 8, 48], replicated, may hold values from -0.3125 to 0.3125
- coarse_weight: bfloat16 [48, 27, 48], replicated, may hold values from -0.15625 to 0.15625
- up_weight: bfloat16 [8, 48, 48], replicated, may hold values from -0.875 to 0.875
Outputs:
- output: bfloat16 [16, 16, 16, 48, 512], P('gx', 'gy')
- input_grad: bfloat16 [16, 16, 16, 48, 512], P('gx', 'gy')
- fine_weight_grad: float32 [48, 27, 48], replicated
- down_weight_grad: float32 [48, 8, 48], replicated
- coarse_weight_grad: float32 [48, 27, 48], replicated
- up_weight_grad: float32 [8, 48, 48], replicated
The draws below stay inside these ranges and needn't reach their ends.
Inputs may be any that keep to these rules, and one draw needn't show every extreme that they name: `block_slots`: on each device the 16 entries are distinct, so every block position of the region appears once.
All inputs are finite; a program needn't handle non-finite values.
Results may differ from the reference program's by a relative error of at most 0.008.
Values may be sent and summed in bfloat16 or wider, within the bound.
A program may use at most 192 MiB of HBM per device.

```python
import math
import jax
import jax.numpy as jnp
from jax import lax

C = 48
BLOCK = 8
VOX = 512
KVOL = 27
SUB = 8
BX = 1
SLOTS = 16
BY = 16
N_GX = 16
N_GY = 16


def draw_block_slots(key, part):
    count_dev = N_GX * N_GY
    keys = jax.random.split(jax.random.fold_in(key, 5), count_dev)
    orders = jax.vmap(lambda single: jax.random.permutation(single, SLOTS))(keys)
    return orders.reshape(N_GX, N_GY, SLOTS).astype(jnp.int32)


def draw_block_count(key, part):
    count_dev = N_GX * N_GY
    least = max(1, SLOTS // 8)
    counts = jax.random.randint(jax.random.fold_in(key, 11), (count_dev,), least, SLOTS + 1)
    busiest = jax.random.randint(jax.random.fold_in(key, 12), (), 0, count_dev)
    counts = jnp.where(jnp.arange(count_dev) == busiest, SLOTS, counts)
    return counts.reshape(N_GX, N_GY).astype(jnp.int32)


def steps_of(own_key, extent, shards, low, top_value):
    gain = 1.0
    for dim, shards_of in shards:
        heights = jax.random.uniform(jax.random.fold_in(jax.random.fold_in(own_key, 6), dim), (shards_of,), jnp.float32, low / len(shards), top_value / len(shards))
        gain = gain * jnp.repeat(jnp.exp(heights), extent[dim] // shards_of).reshape((-1,) + (1,) * (len(extent) - 1 - dim))
    return gain


def scatter_about(rng, extent, spread, most, cuts=(), kind=jnp.bfloat16):
    gain = steps_of(rng, extent, cuts, -0.22, 0.18) if cuts else 1.0
    values = jax.random.normal(rng, extent, jnp.float32) * spread * gain
    return jnp.minimum(jnp.maximum(values, -most), most).astype(kind)


def setup_inputs(seed: int = 0) -> dict:
    seeds = jax.random.split(jax.random.key(seed), 9)
    features = scatter_about(seeds[0], (N_GX, N_GY, SLOTS, C, VOX), 1.0, 6.0, ((0, 16), (1, 16)))
    block_slots = draw_block_slots(jax.random.fold_in(seeds[8], 71), 0)
    block_count = draw_block_count(jax.random.fold_in(seeds[8], 71), 0)
    cotangent = scatter_about(seeds[3], (N_GX, N_GY, SLOTS, C, VOX), 1.0, 6.0, ((0, 16), (1, 16)))
    fine_weight = scatter_about(seeds[4], (C, KVOL, C), (KVOL * C) ** -0.5, 0.15625)
    down_weight = scatter_about(seeds[5], (C, SUB, C), (SUB * C) ** -0.5, 0.3125)
    coarse_weight = scatter_about(seeds[6], (C, KVOL, C), (KVOL * C) ** -0.5, 0.15625)
    up_weight = scatter_about(seeds[7], (SUB, C, C), C ** -0.5, 0.875)
    return dict(features=features, block_slots=block_slots, block_count=block_count, cotangent=cotangent, fine_weight=fine_weight, down_weight=down_weight, coarse_weight=coarse_weight, up_weight=up_weight)


def offset_columns(window, edge, flipped):
    pieces = []
    for depth in range(3):
        for across in range(3):
            for along in range(3):
                if flipped:
                    first = (2 - depth, 2 - across, 2 - along)
                else:
                    first = (depth, across, along)
                piece = window[..., first[0]:first[0] + edge, first[1]:first[1] + edge, first[2]:first[2] + edge]
                pieces.append(piece.reshape(piece.shape[:-3] + (edge ** 3,)))
    return jnp.stack(pieces, axis=-3)

def split_parity(fine):
    lead = fine.shape[:-2]
    chans = fine.shape[-2]
    count = len(lead)
    shaped = fine.reshape(lead + (chans, 4, 2, 4, 2, 4, 2))
    order = tuple(range(count)) + (count + 2, count + 4, count + 6, count, count + 1, count + 3, count + 5)
    return shaped.transpose(order).reshape(lead + (8, chans, 64))

def join_parity(parts):
    lead = parts.shape[:-3]
    chans = parts.shape[-2]
    count = len(lead)
    shaped = parts.reshape(lead + (2, 2, 2, chans, 4, 4, 4))
    order = tuple(range(count)) + (count + 3, count + 4, count, count + 5, count + 1, count + 6, count + 2)
    return shaped.transpose(order).reshape(lead + (chans, 512))

def smooth_gate(value):
    return value * jax.nn.sigmoid(value)

def gate_slope(value):
    sigma = jax.nn.sigmoid(value)
    return sigma * (1.0 + value * (1.0 - sigma))

def global_grid(blocks, places, edge):
    count_dev = blocks.shape[0]
    chans = blocks.shape[2]
    owner = jnp.arange(count_dev, dtype=jnp.int32)[:, None]
    dense = jnp.zeros((count_dev, BX * BY, chans, edge ** 3), blocks.dtype).at[owner, places].set(blocks)
    dense = dense.reshape(N_GX, N_GY, BX, BY, chans, edge, edge, edge)
    dense = dense.transpose(4, 5, 0, 2, 6, 1, 3, 7)
    dense = dense.reshape(chans, edge, N_GX * BX * edge, N_GY * BY * edge)
    return jnp.pad(dense, ((0, 0), (1, 1), (1, 1), (1, 1)))

def device_windows(padded, device, places, edge):
    row = places[device]
    start_x = ((device // N_GY * BX + row // BY) * edge).astype(jnp.int32)
    start_y = ((device % N_GY * BY + row % BY) * edge).astype(jnp.int32)
    zero = jnp.zeros((), jnp.int32)

    def single(first_x, first_y):
        return lax.dynamic_slice(padded, (zero, zero, first_x, first_y), (padded.shape[0], edge + 2, edge + 2, edge + 2))
    return jax.vmap(single)(start_x, start_y)

def reference(features, block_slots, block_count, cotangent, fine_weight, down_weight, coarse_weight, up_weight):
    count_dev = N_GX * N_GY
    half = BLOCK // 2
    places = block_slots.reshape(count_dev, SLOTS).astype(jnp.int32)
    live = jnp.arange(SLOTS, dtype=jnp.int32)[None, :] < block_count.reshape(count_dev, 1)
    live_blocks = live[:, :, None, None]
    zero_half = jnp.zeros((), jnp.bfloat16)
    inputs = jnp.where(live_blocks, features.reshape(count_dev, SLOTS, C, VOX), zero_half)
    grad_out = jnp.where(live_blocks, cotangent.reshape(count_dev, SLOTS, C, VOX), zero_half)
    fine_w = fine_weight.astype(jnp.float32)
    down_w = down_weight.astype(jnp.float32)
    coarse_w = coarse_weight.astype(jnp.float32)
    up_w = up_weight.astype(jnp.float32)
    devices = jnp.arange(count_dev, dtype=jnp.int32)
    fine_pad = global_grid(inputs, places, BLOCK)

    def forward_fine(device):
        columns = offset_columns(device_windows(fine_pad, device, places, BLOCK), BLOCK, False).astype(jnp.float32)
        hidden = jnp.einsum('okc,skcv->sov', fine_w, columns)
        hidden = jnp.where(live_blocks[device], hidden, 0.0)
        active = smooth_gate(hidden).astype(jnp.bfloat16)
        lowered = jnp.einsum('oqc,sqcv->sov', down_w, split_parity(active).astype(jnp.float32))
        lowered = jnp.where(live_blocks[device], lowered, 0.0).astype(jnp.bfloat16)
        return (hidden, active, lowered)
    hidden, active, lowered = lax.map(forward_fine, devices)
    coarse_pad = global_grid(lowered, places, half)

    def coarse_section(device):
        columns = offset_columns(device_windows(coarse_pad, device, places, half), half, False).astype(jnp.float32)
        coarse = jnp.einsum('okc,skcv->sov', coarse_w, columns)
        rect = smooth_gate(coarse).astype(jnp.bfloat16)
        rect_wide = rect.astype(jnp.float32)
        upward = join_parity(jnp.einsum('qoc,scv->sqov', up_w, rect_wide))
        output = jnp.where(live_blocks[device], hidden[device] + upward, 0.0).astype(jnp.bfloat16)
        parts = split_parity(grad_out[device]).astype(jnp.float32)
        grad_rect = jnp.einsum('qoc,sqov->scv', up_w, parts)
        grad_coarse = jnp.where(live_blocks[device], grad_rect * gate_slope(coarse), 0.0).astype(jnp.bfloat16)
        up_term = jnp.einsum('sqov,scv->qoc', parts, rect_wide)
        coarse_term = jnp.einsum('sov,skcv->okc', grad_coarse.astype(jnp.float32), columns)
        return (output, grad_coarse, up_term, coarse_term)
    output, grad_coarse, up_terms, coarse_terms = lax.map(coarse_section, devices)
    grad_coarse_pad = global_grid(grad_coarse, places, half)

    def down_section(device):
        back = offset_columns(device_windows(grad_coarse_pad, device, places, half), half, True).astype(jnp.float32)
        grad_down = jnp.einsum('okc,skov->scv', coarse_w, back)
        grad_down = jnp.where(live_blocks[device], grad_down, 0.0).astype(jnp.bfloat16)
        grad_wide = grad_down.astype(jnp.float32)
        down_term = jnp.einsum('sov,sqcv->oqc', grad_wide, split_parity(active[device]).astype(jnp.float32))
        grad_act = join_parity(jnp.einsum('oqc,sov->sqcv', down_w, grad_wide))
        grad_hidden = grad_out[device].astype(jnp.float32) + grad_act * gate_slope(hidden[device])
        grad_hidden = jnp.where(live_blocks[device], grad_hidden, 0.0).astype(jnp.bfloat16)
        return (grad_hidden, down_term)
    grad_hidden, down_terms = lax.map(down_section, devices)
    grad_hidden_pad = global_grid(grad_hidden, places, BLOCK)

    def fine_section(device):
        fore = offset_columns(device_windows(fine_pad, device, places, BLOCK), BLOCK, False).astype(jnp.float32)
        back = offset_columns(device_windows(grad_hidden_pad, device, places, BLOCK), BLOCK, True).astype(jnp.float32)
        fine_term = jnp.einsum('sov,skcv->okc', grad_hidden[device].astype(jnp.float32), fore)
        input_grad = jnp.einsum('okc,skov->scv', fine_w, back)
        input_grad = jnp.where(live_blocks[device], input_grad, 0.0).astype(jnp.bfloat16)
        return (input_grad, fine_term)
    input_grad, fine_terms = lax.map(fine_section, devices)
    scale = 1.0 / math.sqrt(SLOTS * VOX * count_dev)
    shape_out = (N_GX, N_GY, SLOTS, C, VOX)
    return (output.reshape(shape_out), input_grad.reshape(shape_out), lax.optimization_barrier(jnp.sum(fine_terms, axis=0)) * scale, lax.optimization_barrier(jnp.sum(down_terms, axis=0)) * scale, lax.optimization_barrier(jnp.sum(coarse_terms, axis=0)) * scale, lax.optimization_barrier(jnp.sum(up_terms, axis=0)) * scale)
```

```python
import math

import jax
import jax.numpy as jnp
from jax import lax
from jax.experimental import pallas as pl
from jax.experimental.pallas import tpu as pltpu
from jax.sharding import PartitionSpec as P

C = 48
SLOTS = 16
LANE = 128
NX = 16
NY = 16
ROWS = 1536
CHUNK = ROWS // NX
F32 = jnp.float32
BF16 = jnp.bfloat16
MESH = pl.DeviceIdType.MESH


def dot(a, b):
    return jnp.dot(a, b, preferred_element_type=F32)


def dot_t(a, b):
    return lax.dot_general(a, b, (((1,), (1,)), ((), ())), preferred_element_type=F32)


def iota(shape, dim):
    return lax.broadcasted_iota(jnp.int32, shape, dim)


def one_hot(cond):
    return jnp.where(cond, 1.0, 0.0).astype(BF16)


def build_shift(s_ref, count, last):
    row = iota((256, 256), 0)
    col = iota((256, 256), 1)
    lane = col % LANE
    right = col >= LANE
    if last == 127:
        before = jnp.where(lane < 64, lane + 63, lane - 64)
        after = jnp.where(lane < 64, lane + 64, lane - 63)
        before = jnp.where(lane == 0, -1, before)
        after = jnp.where(lane == 127, -1, after)
    else:
        before = jnp.where((lane == 0) | (lane > last), -1, lane - 1)
        after = jnp.where(lane >= last, -1, lane + 1)
    source = jnp.where(right, after, before)
    place = jnp.where(lane == jnp.where(right, last, 0), jnp.where(right, LANE + 8, LANE), -512)

    @pl.loop(0, count)
    def _(x):
        s_ref[x] = one_hot((row == source) | (row == place + x))


def build_edge(t_ref, length, last):
    row = iota((length, LANE), 0)
    col = iota((length, LANE), 1)
    lane = row % LANE
    x = row // LANE
    t_ref[...] = one_hot(((lane == last) & (col == x)) | ((lane == 0) & (col == x + 8)))


def build_places(e_ref, slots_ref, live_count):
    e_ref[...] = jnp.zeros_like(e_ref)
    row = iota((16, 256), 0)
    col = iota((16, 256), 1)
    y = row % 8
    own = (row // 8) == (col // LANE)
    spot = col % LANE - 64 * (y % 2) - y // 2

    @pl.loop(0, SLOTS)
    def _(s):
        place = jnp.where(s < live_count, slots_ref[0, s], 4096)
        tile = one_hot(own & (spot == 4 * place))
        for j in range(4):
            e_ref[pl.ds(pl.multiple_of(64 * s + 16 * j, 16), 16), 256 * j : 256 * j + 256] = tile


def live_lanes(slots_ref, live_count):
    spot = (iota((8, LANE), 1) % 64) // 4

    def step(s, total):
        place = jnp.where(s < live_count, slots_ref[0, s], 4096)
        return total + jnp.where(spot == place, 1.0, 0.0)

    return lax.fori_loop(0, SLOTS, step, jnp.zeros((8, LANE), F32))


def to_grid(blocks, work, e_ref, grid):
    @pl.loop(0, 8)
    def _(t):
        lanes = pl.ds(pl.multiple_of(t * LANE, LANE), LANE)
        for pair in range(4):
            one = blocks[2 * t, :, pair * LANE : (pair + 1) * LANE]
            two = blocks[2 * t + 1, :, pair * LANE : (pair + 1) * LANE]
            work[2 * pair, :, lanes] = jnp.concatenate([one[:, :64], two[:, :64]], axis=1)
            work[2 * pair + 1, :, lanes] = jnp.concatenate([one[:, 64:], two[:, 64:]], axis=1)

    @pl.loop(0, 4)
    def _(n):
        lanes = pl.ds(pl.multiple_of(n * 256, 256), 256)
        moved = dot(work[...].reshape(8 * C, 1024), e_ref[:, lanes])
        grid[:, :, lanes] = moved.astype(BF16).reshape(8, C, 256)


def to_blocks(grid, e_ref, blocks):
    @pl.loop(0, 4)
    def _(n):
        rows = pl.ds(pl.multiple_of(n * 256, 256), 256)
        moved = dot_t(grid[...].reshape(8 * C, 1024), e_ref[rows, :])
        moved = moved.astype(BF16).reshape(8, C, 256)
        for pair in range(4):
            for k in range(4):
                low = moved[2 * pair, :, 64 * k : 64 * k + 64]
                high = moved[2 * pair + 1, :, 64 * k : 64 * k + 64]
                blocks[4 * n + k, :, pair * LANE : (pair + 1) * LANE] = jnp.concatenate(
                    [low, high], axis=1
                )


def pack_edges(grid, depth, t_ref, packed):
    edges = dot(grid.reshape(depth * C, grid.shape[2]), t_ref[...]).reshape(depth, C, LANE)
    total = edges[0]
    for z in range(1, depth):
        total = total + pltpu.roll(edges[z], 16 * z, 1)
    packed[...] = total.astype(BF16)


def unpack_edges(received, row, left_ok, right_ok, depth):
    lane = iota((C, LANE), 1) % 16
    left = jnp.where(left_ok, received[2 * row].astype(F32), 0.0)
    right = jnp.where(right_ok, received[2 * row + 1].astype(F32), 0.0)
    both = jnp.where(lane < 8, left, right)
    parts = [both] + [pltpu.roll(both, LANE - 16 * z, 1) for z in range(1, depth)]
    return jnp.stack(parts, axis=0).astype(BF16).reshape(depth * C, LANE)


def widen(grid, sides, received, s_ref, wide, count, depth, place):
    gx, gy = place
    low_ok, high_ok = gx > 0, gx < NX - 1
    left_ok, right_ok = gy > 0, gy < NY - 1

    def put(rows, halo, x, lanes):
        moved = dot(jnp.concatenate([rows, halo], axis=1), s_ref[x]).astype(BF16)
        wide[:, 0:C, lanes] = moved[:, :LANE].reshape(depth, C, LANE)
        wide[:, C : 2 * C, lanes] = rows.reshape(depth, C, LANE)
        wide[:, 2 * C : 3 * C, lanes] = moved[:, LANE:].reshape(depth, C, LANE)

    zero = jnp.zeros((depth * C, LANE), BF16)
    halo = unpack_edges(received, 0, left_ok & low_ok, right_ok & low_ok, depth)
    rows = jnp.where(low_ok, sides[0].reshape(depth * C, LANE), zero)
    put(rows, halo, count - 1, pl.ds(0, LANE))
    halo = unpack_edges(received, 2, left_ok & high_ok, right_ok & high_ok, depth)
    rows = jnp.where(high_ok, sides[1].reshape(depth * C, LANE), zero)
    put(rows, halo, 0, pl.ds((count + 1) * LANE, LANE))
    halo = unpack_edges(received, 1, left_ok, right_ok, depth)

    @pl.loop(0, count)
    def _(x):
        rows = grid[:, :, pl.ds(pl.multiple_of(x * LANE, LANE), LANE)].reshape(depth * C, LANE)
        put(rows, halo, x, pl.ds(pl.multiple_of((x + 1) * LANE, LANE), LANE))


def window(wide, z, first):
    return jnp.concatenate(
        [wide[z, :, pl.ds(pl.multiple_of(first + dx * LANE, LANE), 256)] for dx in range(3)], axis=0
    )


def convolve(wide, weight, total, depth, width):
    total[...] = jnp.zeros_like(total)

    @pl.loop(0, depth)
    def _(z):
        @pl.loop(0, width // 256)
        def _(n):
            first = pl.multiple_of(n * 256, 256)
            piece = dot(weight[...], window(wide, z, first)).reshape(3, C, 256)
            lanes = pl.ds(first, 256)
            total[pl.ds(z, 3), :, lanes] = total[pl.ds(z, 3), :, lanes] + piece


def kernel_terms(grad, wide, total, depth, width):
    total[...] = jnp.zeros_like(total)

    @pl.loop(0, depth)
    def _(z):
        @pl.loop(0, width // 256)
        def _(n):
            first = pl.multiple_of(n * 256, 256)
            lanes = pl.ds(first, 256)
            ahead = grad[pl.ds(z, 3), :, lanes].reshape(3 * C, 256)
            total[...] = total[...] + dot_t(ahead, window(wide, z, first))


def quarters(grid, wz):
    columns = []
    for a in range(2):
        for b in range(2):
            columns.append(
                jnp.concatenate(
                    [
                        grid[2 * wz + a, :, (2 * wx + b) * LANE : (2 * wx + b + 1) * LANE]
                        for wx in range(4)
                    ],
                    axis=1,
                )
            )
    return jnp.concatenate(columns, axis=0)


def tile_lanes(mask, rows, width):
    return jnp.broadcast_to(jnp.concatenate([mask] * (width // LANE), axis=1)[0:1], (rows, width))


def roll_half(value):
    parts = [
        pltpu.roll(value[:, k * LANE : (k + 1) * LANE], 64, 1) for k in range(value.shape[1] // LANE)
    ]
    return jnp.concatenate(parts, axis=1)


def slope(value):
    sigma = jax.nn.sigmoid(value)
    return sigma * (1.0 + value * (1.0 - sigma))


def section(
    slots_ref,
    count_ref,
    feat_hbm,
    cot_hbm,
    wf,
    wfb,
    wc,
    wcb,
    ddn,
    dga,
    uup,
    ugr,
    out_hbm,
    ig_hbm,
    gf_out,
    gc_out,
    gu_out,
    gd_out,
    feat,
    cot_in,
    work,
    places,
    shift_f,
    shift_c,
    edge_f,
    edge_c,
    fine,
    cot,
    fine3,
    hidden,
    act,
    low,
    low3,
    coarse,
    grect,
    rect2,
    gcoarse,
    gcoarse3,
    gdown2,
    ghid,
    ghid3,
    result,
    blocks_out,
    blocks_ig,
    term_f,
    term_c,
    term_u,
    term_d,
    packed,
    sides_f,
    sides_c,
    edges_in,
    grads,
    first_in,
    chunk,
    second_in,
    done,
    local_sem,
    send_sem,
    recv_sem,
    sum_send,
    sum_recv,
):
    gx = lax.axis_index("gx")
    gy = lax.axis_index("gy")
    here = (gx, gy)

    load_feat = pltpu.make_async_copy(feat_hbm, feat, local_sem.at[0])
    load_cot = pltpu.make_async_copy(cot_hbm, cot_in, local_sem.at[1])
    load_feat.start()
    load_cot.start()

    barrier = pltpu.get_barrier_semaphore()

    @pl.loop(1, NX)
    def _(d):
        pl.semaphore_signal(
            barrier, inc=1, device_id=(lax.rem(gx + d, NX), gy), device_id_type=MESH
        )
        pl.semaphore_signal(
            barrier, inc=1, device_id=(gx, lax.rem(gy + d, NY)), device_id_type=MESH
        )

    for dx in (1, NX - 1):
        for dy in (1, NY - 1):
            pl.semaphore_signal(
                barrier,
                inc=1,
                device_id=(lax.rem(gx + dx, NX), lax.rem(gy + dy, NY)),
                device_id_type=MESH,
            )

    live_count = count_ref[0, 0]
    build_places(places, slots_ref, live_count)
    build_shift(shift_f, 8, 127)
    build_shift(shift_c, 4, 63)
    build_edge(edge_f, 1024, 127)
    build_edge(edge_c, 512, 63)
    live = live_lanes(slots_ref, live_count)
    half_live = jnp.where(iota((8, LANE), 1) < 64, live, 0.0)
    lower = jnp.where(iota((8, LANE), 1) < 64, 1.0, 0.0)

    def exchange(step, source, depth, count, sides):
        copies = []
        for side in range(2):
            x = count - 1 if side == 0 else 0
            shift = 1 if side == 0 else NX - 1
            copies.append(
                pltpu.make_async_remote_copy(
                    src_ref=source.at[:, :, pl.ds(x * LANE, LANE)],
                    dst_ref=sides.at[side],
                    send_sem=send_sem.at[step, side],
                    recv_sem=recv_sem.at[step, side],
                    device_id=(lax.rem(gx + shift, NX), gy),
                    device_id_type=MESH,
                )
            )
        for row in range(3):
            for side in range(2):
                copies.append(
                    pltpu.make_async_remote_copy(
                        src_ref=packed.at[step],
                        dst_ref=edges_in.at[step, 2 * row + side],
                        send_sem=send_sem.at[step, 2 + 2 * row + side],
                        recv_sem=recv_sem.at[step, 2 + 2 * row + side],
                        device_id=(
                            lax.rem(gx + NX + 1 - row, NX),
                            lax.rem(gy + (1 if side == 0 else NY - 1), NY),
                        ),
                        device_id_type=MESH,
                    )
                )
        for copy in copies:
            copy.start()
        return copies

    load_feat.wait()
    to_grid(feat, work, places, fine)
    pack_edges(fine[...], 8, edge_f, packed.at[0])
    pl.semaphore_wait(barrier, 2 * (NX - 1) + 4)
    copies = exchange(0, fine, 8, 8, sides_f.at[0])

    load_cot.wait()
    to_grid(cot_in, work, places, cot)
    for wz in range(4):
        both = dot(ugr[...], quarters(cot, wz))
        grect[wz] = both[:C] + roll_half(both[C:])

    for copy in copies:
        copy.wait()
    widen(fine, sides_f.at[0], edges_in.at[0], shift_f, fine3, 8, 8, here)
    convolve(fine3, wf, hidden, 8, 1024)

    live_fine = tile_lanes(live, C, 1024)

    @pl.loop(0, 8)
    def _(z):
        value = hidden[z + 1] * live_fine
        hidden[z + 1] = value
        act[z] = (value * jax.nn.sigmoid(value)).astype(BF16)

    lower_mask = tile_lanes(lower, C, 512)
    for wz in range(4):
        both = dot(ddn[...], quarters(act, wz))
        low[wz] = ((both[:C] + roll_half(both[C:])) * lower_mask).astype(BF16)

    pack_edges(low[...], 4, edge_c, packed.at[1])
    copies = exchange(1, low, 4, 4, sides_c.at[0])
    for copy in copies:
        copy.wait()
    widen(low, sides_c.at[0], edges_in.at[1], shift_c, low3, 4, 4, here)
    convolve(low3, wc, coarse, 4, 512)

    gcoarse[...] = jnp.zeros_like(gcoarse)
    for wz in range(4):
        value = coarse[wz + 1]
        rect = value * jax.nn.sigmoid(value) * lower_mask
        rect2[wz, 0:C] = rect.astype(BF16)
        rect2[wz, C : 2 * C] = roll_half(rect).astype(BF16)
        gcoarse[wz + 1] = (grect[wz] * slope(value) * lower_mask).astype(BF16)

    pack_edges(gcoarse[1:5], 4, edge_c, packed.at[2])
    copies = exchange(2, gcoarse.at[pl.ds(1, 4)], 4, 4, sides_c.at[1])

    for wz in range(4):
        upward = dot(uup[...], rect2[wz])
        for a in range(2):
            for b in range(2):
                k = 2 * a + b
                for wx in range(4):
                    lanes = pl.ds((2 * wx + b) * LANE, LANE)
                    piece = upward[k * C : (k + 1) * C, wx * LANE : (wx + 1) * LANE]
                    result[2 * wz + a, :, lanes] = (
                        hidden[2 * wz + a + 1, :, lanes] + piece
                    ).astype(BF16)
    to_blocks(result, places, blocks_out)
    store_out = pltpu.make_async_copy(blocks_out, out_hbm, local_sem.at[2])
    store_out.start()
    kernel_terms(gcoarse, low3, term_c, 4, 512)
    total = jnp.zeros((4 * C, 2 * C), F32)
    for wz in range(4):
        total = total + dot_t(quarters(cot, wz), rect2[wz])
    term_u[...] = total

    for copy in copies:
        copy.wait()
    widen(gcoarse.at[pl.ds(1, 4)], sides_c.at[1], edges_in.at[2], shift_c, gcoarse3, 4, 4, here)
    convolve(gcoarse3, wcb, coarse, 4, 512)

    live_coarse = tile_lanes(half_live, C, 512)
    ghid[0] = jnp.zeros((C, 1024), BF16)
    ghid[9] = jnp.zeros((C, 1024), BF16)
    for wz in range(4):
        value = coarse[wz + 1] * live_coarse
        gdown2[wz, 0:C] = value.astype(BF16)
        gdown2[wz, C : 2 * C] = roll_half(value).astype(BF16)
        back = dot(dga[...], gdown2[wz])
        for a in range(2):
            for b in range(2):
                k = 2 * a + b
                for wx in range(4):
                    lanes = pl.ds((2 * wx + b) * LANE, LANE)
                    piece = back[k * C : (k + 1) * C, wx * LANE : (wx + 1) * LANE]
                    ghid[2 * wz + a + 1, :, lanes] = (
                        cot[2 * wz + a, :, lanes].astype(F32)
                        + piece * slope(hidden[2 * wz + a + 1, :, lanes])
                    ).astype(BF16)

    pack_edges(ghid[1:9], 8, edge_f, packed.at[3])
    copies = exchange(3, ghid.at[pl.ds(1, 8)], 8, 8, sides_f.at[1])

    total = jnp.zeros((2 * C, 4 * C), F32)
    for wz in range(4):
        total = total + dot_t(gdown2[wz], quarters(act, wz))
    term_d[...] = total
    kernel_terms(ghid, fine3, term_f, 8, 1024)

    grads[...] = jnp.zeros_like(grads)
    for k in range(4):
        wide = min(LANE, 432 - k * LANE)
        lanes = slice(k * LANE, k * LANE + wide)
        grads[144 * k : 144 * k + 144, 0:wide] = term_f[:, lanes].astype(BF16)
        grads[576 + 144 * k : 720 + 144 * k, 0:wide] = term_c[:, lanes].astype(BF16)
    grads[1152:1344, 0:96] = term_u[...].astype(BF16)
    grads[1344:1440, :] = term_d[:, 0:LANE].astype(BF16)
    grads[1440:1536, 0:64] = term_d[:, LANE:192].astype(BF16)

    def chunk_rows(index):
        return pl.ds(pl.multiple_of(index * CHUNK, CHUNK), CHUNK)

    def first_copy(d):
        peer = lax.rem(gx + d, NX)
        return pltpu.make_async_remote_copy(
            src_ref=grads.at[chunk_rows(peer)],
            dst_ref=first_in.at[d],
            send_sem=sum_send.at[0, d],
            recv_sem=sum_recv.at[0, d],
            device_id=(peer, gy),
            device_id_type=MESH,
        )

    def second_copy(d):
        return pltpu.make_async_remote_copy(
            src_ref=chunk.at[0],
            dst_ref=second_in.at[d],
            send_sem=sum_send.at[1, d],
            recv_sem=sum_recv.at[1, d],
            device_id=(gx, lax.rem(gy + d, NY)),
            device_id_type=MESH,
        )

    def third_copy(d):
        return pltpu.make_async_remote_copy(
            src_ref=chunk.at[1],
            dst_ref=done.at[chunk_rows(gx)],
            send_sem=sum_send.at[2, d],
            recv_sem=sum_recv.at[2, d],
            device_id=(lax.rem(gx + d, NX), gy),
            device_id_type=MESH,
        )

    @pl.loop(1, NX)
    def _(d):
        first_copy(d).start()

    for copy in copies:
        copy.wait()
    widen(ghid.at[pl.ds(1, 8)], sides_f.at[1], edges_in.at[3], shift_f, ghid3, 8, 8, here)
    convolve(ghid3, wfb, hidden, 8, 1024)

    @pl.loop(1, NX)
    def _(d):
        first_copy(d).wait()

    own = grads[chunk_rows(gx), :].astype(F32)
    own = lax.fori_loop(1, NX, lambda d, acc: acc + first_in[d].astype(F32), own)
    chunk[0] = own.astype(BF16)

    @pl.loop(1, NY)
    def _(d):
        second_copy(d).start()

    @pl.loop(0, 8)
    def _(z):
        result[z] = hidden[z + 1].astype(BF16)

    to_blocks(result, places, blocks_ig)
    store_ig = pltpu.make_async_copy(blocks_ig, ig_hbm, local_sem.at[3])
    store_ig.start()

    @pl.loop(1, NY)
    def _(d):
        second_copy(d).wait()

    own = lax.fori_loop(1, NY, lambda d, acc: acc + second_in[d].astype(F32), own)
    chunk[1] = own.astype(BF16)

    @pl.loop(1, NX)
    def _(d):
        third_copy(d).start()

    done[chunk_rows(gx), :] = chunk[1]

    @pl.loop(1, NX)
    def _(d):
        third_copy(d).wait()

    scale = 1.0 / math.sqrt(SLOTS * 512 * NX * NY)
    for k in range(4):
        wide = min(LANE, 432 - k * LANE)
        lanes = slice(k * LANE, k * LANE + wide)
        gf_out[:, lanes] = done[144 * k : 144 * k + 144, 0:wide].astype(F32) * scale
        gc_out[:, lanes] = done[576 + 144 * k : 720 + 144 * k, 0:wide].astype(F32) * scale
    gu_out[...] = done[1152:1344, 0:96].astype(F32) * scale
    gd_out[:, 0:LANE] = done[1344:1440, :].astype(F32) * scale
    gd_out[:, LANE:192] = done[1440:1536, 0:64].astype(F32) * scale
    store_out.wait()
    store_ig.wait()


def on_device(
    features, block_slots, block_count, cotangent, fine_weight, down_weight, coarse_weight, up_weight
):
    def forward_rows(weight):
        return (
            weight.reshape(C, 3, 9, C)[:, ::-1].transpose(1, 0, 2, 3).reshape(3 * C, 9 * C)
        )

    def backward_rows(weight):
        return weight.reshape(C, 3, 9, C)[:, :, ::-1].transpose(1, 3, 2, 0).reshape(3 * C, 9 * C)

    down = down_weight.reshape(C, 4, 2, C)
    ddn = down.transpose(2, 0, 1, 3).reshape(2 * C, 4 * C)
    dga = down.transpose(1, 3, 2, 0).reshape(4 * C, 2 * C)
    up = up_weight.reshape(4, 2, C, C)
    uup = up.transpose(0, 2, 1, 3).reshape(4 * C, 2 * C)
    ugr = up.transpose(1, 3, 0, 2).reshape(2 * C, 4 * C)

    vmem = pl.BlockSpec(memory_space=pltpu.VMEM)
    smem = pl.BlockSpec(memory_space=pltpu.SMEM)
    anywhere = pl.BlockSpec(memory_space=pl.ANY)
    blocks = (SLOTS, C, 512)
    out, ig, gf, gc, gu, gd = pl.pallas_call(
        section,
        out_shape=(
            jax.ShapeDtypeStruct(blocks, BF16),
            jax.ShapeDtypeStruct(blocks, BF16),
            jax.ShapeDtypeStruct((3 * C, 9 * C), F32),
            jax.ShapeDtypeStruct((3 * C, 9 * C), F32),
            jax.ShapeDtypeStruct((4 * C, 2 * C), F32),
            jax.ShapeDtypeStruct((2 * C, 4 * C), F32),
        ),
        in_specs=[smem, smem, anywhere, anywhere] + [vmem] * 8,
        out_specs=(anywhere, anywhere, vmem, vmem, vmem, vmem),
        scratch_shapes=[
            pltpu.VMEM(blocks, BF16),
            pltpu.VMEM(blocks, BF16),
            pltpu.VMEM((8, C, 1024), BF16),
            pltpu.VMEM((1024, 1024), BF16),
            pltpu.VMEM((8, 256, 256), BF16),
            pltpu.VMEM((4, 256, 256), BF16),
            pltpu.VMEM((1024, LANE), BF16),
            pltpu.VMEM((512, LANE), BF16),
            pltpu.VMEM((8, C, 1024), BF16),
            pltpu.VMEM((8, C, 1024), BF16),
            pltpu.VMEM((8, 3 * C, 1280), BF16),
            pltpu.VMEM((10, C, 1024), F32),
            pltpu.VMEM((8, C, 1024), BF16),
            pltpu.VMEM((4, C, 512), BF16),
            pltpu.VMEM((4, 3 * C, 768), BF16),
            pltpu.VMEM((6, C, 512), F32),
            pltpu.VMEM((4, C, 512), F32),
            pltpu.VMEM((4, 2 * C, 512), BF16),
            pltpu.VMEM((6, C, 512), BF16),
            pltpu.VMEM((4, 3 * C, 768), BF16),
            pltpu.VMEM((4, 2 * C, 512), BF16),
            pltpu.VMEM((10, C, 1024), BF16),
            pltpu.VMEM((8, 3 * C, 1280), BF16),
            pltpu.VMEM((8, C, 1024), BF16),
            pltpu.VMEM(blocks, BF16),
            pltpu.VMEM(blocks, BF16),
            pltpu.VMEM((3 * C, 9 * C), F32),
            pltpu.VMEM((3 * C, 9 * C), F32),
            pltpu.VMEM((4 * C, 2 * C), F32),
            pltpu.VMEM((2 * C, 4 * C), F32),
            pltpu.VMEM((4, C, LANE), BF16),
            pltpu.VMEM((2, 2, 8, C, LANE), BF16),
            pltpu.VMEM((2, 2, 4, C, LANE), BF16),
            pltpu.VMEM((4, 6, C, LANE), BF16),
            pltpu.VMEM((ROWS, LANE), BF16),
            pltpu.VMEM((NX, CHUNK, LANE), BF16),
            pltpu.VMEM((2, CHUNK, LANE), BF16),
            pltpu.VMEM((NY, CHUNK, LANE), BF16),
            pltpu.VMEM((ROWS, LANE), BF16),
            pltpu.SemaphoreType.DMA((4,)),
            pltpu.SemaphoreType.DMA((4, 8)),
            pltpu.SemaphoreType.DMA((4, 8)),
            pltpu.SemaphoreType.DMA((3, NX)),
            pltpu.SemaphoreType.DMA((3, NX)),
        ],
        compiler_params=pltpu.CompilerParams(
            collective_id=0, has_side_effects=True, vmem_limit_bytes=50 * 1024 * 1024
        ),
        name="section",
    )(
        block_slots.reshape(1, SLOTS),
        block_count.reshape(1, 1),
        features.reshape(blocks),
        cotangent.reshape(blocks),
        forward_rows(fine_weight),
        backward_rows(fine_weight),
        forward_rows(coarse_weight),
        backward_rows(coarse_weight),
        ddn,
        dga,
        uup,
        ugr,
    )

    def kernel_grad(rows):
        return rows.reshape(3, C, 9, C)[::-1].transpose(1, 0, 2, 3).reshape(C, 27, C)

    shape_out = (1, 1) + blocks
    return (
        out.reshape(shape_out),
        ig.reshape(shape_out),
        kernel_grad(gf),
        gd.reshape(2, C, 4, C).transpose(1, 2, 0, 3).reshape(C, 8, C),
        kernel_grad(gc),
        gu.reshape(4, C, 2, C).transpose(0, 2, 1, 3).reshape(8, C, C),
    )


def solution(mesh):
    split = P("gx", "gy", None, None, None)
    return jax.shard_map(
        on_device,
        mesh=mesh,
        in_specs=(split, P("gx", "gy", None), P("gx", "gy"), split, P(), P(), P(), P()),
        out_specs=(split, split, P(), P(), P(), P()),
        check_vma=False,
    )
```

```python
import math

import jax
import jax.numpy as jnp
from jax import lax
from jax.experimental import pallas as pl
from jax.experimental.pallas import tpu as pltpu
from jax.sharding import PartitionSpec as P

C = 48
SLOTS = 16
LANE = 128
NX = 16
NY = 16
ROWS = 1536
CHUNK = ROWS // NX
F32 = jnp.float32
BF16 = jnp.bfloat16
MESH = pl.DeviceIdType.MESH


def dot(a, b):
    return jnp.dot(a, b, preferred_element_type=F32)


def dot_t(a, b):
    return lax.dot_general(a, b, (((1,), (1,)), ((), ())), preferred_element_type=F32)


def iota(shape, dim):
    return lax.broadcasted_iota(jnp.int32, shape, dim)


def one_hot(cond):
    return jnp.where(cond, 1.0, 0.0).astype(BF16)


def build_shift(s_ref, count, last):
    row = iota((256, 256), 0)
    col = iota((256, 256), 1)
    lane = col % LANE
    right = col >= LANE
    if last == 127:
        before = jnp.where(lane < 64, lane + 63, lane - 64)
        after = jnp.where(lane < 64, lane + 64, lane - 63)
        before = jnp.where(lane == 0, -1, before)
        after = jnp.where(lane == 127, -1, after)
    else:
        before = jnp.where((lane == 0) | (lane > last), -1, lane - 1)
        after = jnp.where(lane >= last, -1, lane + 1)
    source = jnp.where(right, after, before)
    place = jnp.where(lane == jnp.where(right, last, 0), jnp.where(right, LANE + 8, LANE), -512)

    @pl.loop(0, count)
    def _(x):
        s_ref[x] = one_hot((row == source) | (row == place + x))


def build_edge(t_ref, length, last):
    row = iota((length, LANE), 0)
    col = iota((length, LANE), 1)
    lane = row % LANE
    x = row // LANE
    t_ref[...] = one_hot(((lane == last) & (col == x)) | ((lane == 0) & (col == x + 8)))


def build_places(e_ref, slots_ref, live_count):
    e_ref[...] = jnp.zeros_like(e_ref)
    row = iota((16, 256), 0)
    col = iota((16, 256), 1)
    y = row % 8
    own = (row // 8) == (col // LANE)
    spot = col % LANE - 64 * (y % 2) - y // 2

    @pl.loop(0, SLOTS)
    def _(s):
        place = jnp.where(s < live_count, slots_ref[0, s], 4096)
        tile = one_hot(own & (spot == 4 * place))
        for j in range(4):
            e_ref[pl.ds(pl.multiple_of(64 * s + 16 * j, 16), 16), 256 * j : 256 * j + 256] = tile


def live_lanes(slots_ref, live_count):
    spot = (iota((8, LANE), 1) % 64) // 4

    def step(s, total):
        place = jnp.where(s < live_count, slots_ref[0, s], 4096)
        return total + jnp.where(spot == place, 1.0, 0.0)

    return lax.fori_loop(0, SLOTS, step, jnp.zeros((8, LANE), F32))


def to_grid(blocks, work, e_ref, grid):
    for t in range(8):
        lanes = slice(t * LANE, (t + 1) * LANE)
        for pair in range(4):
            one = blocks[2 * t, :, pair * LANE : (pair + 1) * LANE]
            two = blocks[2 * t + 1, :, pair * LANE : (pair + 1) * LANE]
            work[2 * pair, :, lanes] = jnp.concatenate([one[:, :64], two[:, :64]], axis=1)
            work[2 * pair + 1, :, lanes] = jnp.concatenate([one[:, 64:], two[:, 64:]], axis=1)

    for n in range(4):
        lanes = slice(n * 256, (n + 1) * 256)
        moved = dot(work[...].reshape(8 * C, 1024), e_ref[:, lanes])
        grid[:, :, lanes] = moved.astype(BF16).reshape(8, C, 256)


def to_blocks(grid, e_ref, blocks):
    for n in range(4):
        rows = slice(n * 256, (n + 1) * 256)
        moved = dot_t(grid[...].reshape(8 * C, 1024), e_ref[rows, :])
        moved = moved.astype(BF16).reshape(8, C, 256)
        for pair in range(4):
            for k in range(4):
                low = moved[2 * pair, :, 64 * k : 64 * k + 64]
                high = moved[2 * pair + 1, :, 64 * k : 64 * k + 64]
                blocks[4 * n + k, :, pair * LANE : (pair + 1) * LANE] = jnp.concatenate(
                    [low, high], axis=1
                )


def pack_edges(grid, depth, t_ref, packed):
    edges = dot(grid.reshape(depth * C, grid.shape[2]), t_ref[...]).reshape(depth, C, LANE)
    total = edges[0]
    for z in range(1, depth):
        total = total + pltpu.roll(edges[z], 16 * z, 1)
    packed[...] = total.astype(BF16)


def unpack_edges(received, row, left_ok, right_ok, depth):
    lane = iota((C, LANE), 1) % 16
    left = jnp.where(left_ok, received[2 * row].astype(F32), 0.0)
    right = jnp.where(right_ok, received[2 * row + 1].astype(F32), 0.0)
    both = jnp.where(lane < 8, left, right)
    parts = [both] + [pltpu.roll(both, LANE - 16 * z, 1) for z in range(1, depth)]
    return jnp.stack(parts, axis=0).astype(BF16).reshape(depth * C, LANE)


def widen(grid, sides, received, s_ref, wide, count, depth, place):
    gx, gy = place
    low_ok, high_ok = gx > 0, gx < NX - 1
    left_ok, right_ok = gy > 0, gy < NY - 1

    def put(rows, halo, x, lanes):
        moved = dot(jnp.concatenate([rows, halo], axis=1), s_ref[x]).astype(BF16)
        wide[:, 0:C, lanes] = moved[:, :LANE].reshape(depth, C, LANE)
        wide[:, C : 2 * C, lanes] = rows.reshape(depth, C, LANE)
        wide[:, 2 * C : 3 * C, lanes] = moved[:, LANE:].reshape(depth, C, LANE)

    zero = jnp.zeros((depth * C, LANE), BF16)
    halo = unpack_edges(received, 0, left_ok & low_ok, right_ok & low_ok, depth)
    rows = jnp.where(low_ok, sides[0].reshape(depth * C, LANE), zero)
    put(rows, halo, count - 1, pl.ds(0, LANE))
    halo = unpack_edges(received, 2, left_ok & high_ok, right_ok & high_ok, depth)
    rows = jnp.where(high_ok, sides[1].reshape(depth * C, LANE), zero)
    put(rows, halo, 0, pl.ds((count + 1) * LANE, LANE))
    halo = unpack_edges(received, 1, left_ok, right_ok, depth)

    for x in range(count):
        rows = grid[:, :, x * LANE : (x + 1) * LANE].reshape(depth * C, LANE)
        put(rows, halo, x, pl.ds((x + 1) * LANE, LANE))


def window(wide, z, first, width):
    return jnp.concatenate(
        [wide[z, :, first + dx * LANE : first + dx * LANE + width] for dx in range(3)], axis=0
    )


def convolve(wide, weight, total, depth, width):
    total[...] = jnp.zeros_like(total)
    for z in range(depth):
        for first in range(0, width, 256):
            piece = dot(weight[...], window(wide, z, first, 256)).reshape(3, C, 256)
            lanes = slice(first, first + 256)
            total[z : z + 3, :, lanes] = total[z : z + 3, :, lanes] + piece


def kernel_terms(grad, wide, total, depth, width):
    ahead = [grad[z : z + 3].reshape(3 * C, width) for z in range(depth)]
    pieces = [window(wide, z, 0, width) for z in range(depth)]
    total[...] = dot_t(jnp.concatenate(ahead, axis=1), jnp.concatenate(pieces, axis=1))


def quarters(grid, wz):
    columns = []
    for a in range(2):
        for b in range(2):
            columns.append(
                jnp.concatenate(
                    [
                        grid[2 * wz + a, :, (2 * wx + b) * LANE : (2 * wx + b + 1) * LANE]
                        for wx in range(4)
                    ],
                    axis=1,
                )
            )
    return jnp.concatenate(columns, axis=0)


def tile_lanes(mask, rows, width):
    return jnp.broadcast_to(jnp.concatenate([mask] * (width // LANE), axis=1)[0:1], (rows, width))


def roll_half(value):
    parts = [
        pltpu.roll(value[:, k * LANE : (k + 1) * LANE], 64, 1) for k in range(value.shape[1] // LANE)
    ]
    return jnp.concatenate(parts, axis=1)


def slope(value):
    sigma = jax.nn.sigmoid(value)
    return sigma * (1.0 + value * (1.0 - sigma))


def section(
    slots_ref,
    count_ref,
    feat_hbm,
    cot_hbm,
    wf,
    wfb,
    wc,
    wcb,
    ddn,
    dga,
    uup,
    ugr,
    out_hbm,
    ig_hbm,
    gf_out,
    gc_out,
    gu_out,
    gd_out,
    feat,
    cot_in,
    work,
    places,
    shift_f,
    shift_c,
    edge_f,
    edge_c,
    fine,
    cot,
    fine3,
    hidden,
    act,
    low,
    low3,
    coarse,
    grect,
    rect2,
    gcoarse,
    gcoarse3,
    gdown2,
    ghid,
    ghid3,
    result,
    blocks_out,
    blocks_ig,
    term_f,
    term_c,
    term_u,
    term_d,
    packed,
    sides_f,
    sides_c,
    edges_in,
    grads,
    first_in,
    chunk,
    second_in,
    done,
    local_sem,
    send_sem,
    recv_sem,
    sum_send,
    sum_recv,
):
    gx = lax.axis_index("gx")
    gy = lax.axis_index("gy")
    here = (gx, gy)

    load_feat = pltpu.make_async_copy(feat_hbm, feat, local_sem.at[0])
    load_cot = pltpu.make_async_copy(cot_hbm, cot_in, local_sem.at[1])
    load_feat.start()
    load_cot.start()

    barrier = pltpu.get_barrier_semaphore()

    @pl.loop(1, NX)
    def _(d):
        pl.semaphore_signal(
            barrier, inc=1, device_id=(lax.rem(gx + d, NX), gy), device_id_type=MESH
        )
        pl.semaphore_signal(
            barrier, inc=1, device_id=(gx, lax.rem(gy + d, NY)), device_id_type=MESH
        )

    for dx in (1, NX - 1):
        for dy in (1, NY - 1):
            pl.semaphore_signal(
                barrier,
                inc=1,
                device_id=(lax.rem(gx + dx, NX), lax.rem(gy + dy, NY)),
                device_id_type=MESH,
            )

    live_count = count_ref[0, 0]
    build_places(places, slots_ref, live_count)
    build_shift(shift_f, 8, 127)
    build_shift(shift_c, 4, 63)
    build_edge(edge_f, 1024, 127)
    build_edge(edge_c, 512, 63)
    live = live_lanes(slots_ref, live_count)
    half_live = jnp.where(iota((8, LANE), 1) < 64, live, 0.0)
    lower = jnp.where(iota((8, LANE), 1) < 64, 1.0, 0.0)

    def exchange(step, source, depth, count, sides):
        copies = []
        for side in range(2):
            x = count - 1 if side == 0 else 0
            shift = 1 if side == 0 else NX - 1
            copies.append(
                pltpu.make_async_remote_copy(
                    src_ref=source.at[:, :, pl.ds(x * LANE, LANE)],
                    dst_ref=sides.at[side],
                    send_sem=send_sem.at[step, side],
                    recv_sem=recv_sem.at[step, side],
                    device_id=(lax.rem(gx + shift, NX), gy),
                    device_id_type=MESH,
                )
            )
        for row in range(3):
            for side in range(2):
                copies.append(
                    pltpu.make_async_remote_copy(
                        src_ref=packed.at[step],
                        dst_ref=edges_in.at[step, 2 * row + side],
                        send_sem=send_sem.at[step, 2 + 2 * row + side],
                        recv_sem=recv_sem.at[step, 2 + 2 * row + side],
                        device_id=(
                            lax.rem(gx + NX + 1 - row, NX),
                            lax.rem(gy + (1 if side == 0 else NY - 1), NY),
                        ),
                        device_id_type=MESH,
                    )
                )
        for copy in copies:
            copy.start()
        return copies

    load_feat.wait()
    to_grid(feat, work, places, fine)
    pack_edges(fine[...], 8, edge_f, packed.at[0])
    pl.semaphore_wait(barrier, 2 * (NX - 1) + 4)
    copies = exchange(0, fine, 8, 8, sides_f.at[0])

    load_cot.wait()
    to_grid(cot_in, work, places, cot)
    for wz in range(4):
        both = dot(ugr[...], quarters(cot, wz))
        grect[wz] = both[:C] + roll_half(both[C:])

    for copy in copies:
        copy.wait()
    widen(fine, sides_f.at[0], edges_in.at[0], shift_f, fine3, 8, 8, here)
    convolve(fine3, wf, hidden, 8, 1024)

    live_fine = tile_lanes(live, C, 1024)

    @pl.loop(0, 8)
    def _(z):
        value = hidden[z + 1] * live_fine
        hidden[z + 1] = value
        act[z] = (value * jax.nn.sigmoid(value)).astype(BF16)

    lower_mask = tile_lanes(lower, C, 512)
    for wz in range(4):
        both = dot(ddn[...], quarters(act, wz))
        low[wz] = ((both[:C] + roll_half(both[C:])) * lower_mask).astype(BF16)

    pack_edges(low[...], 4, edge_c, packed.at[1])
    copies = exchange(1, low, 4, 4, sides_c.at[0])
    for copy in copies:
        copy.wait()
    widen(low, sides_c.at[0], edges_in.at[1], shift_c, low3, 4, 4, here)
    convolve(low3, wc, coarse, 4, 512)

    gcoarse[...] = jnp.zeros_like(gcoarse)
    for wz in range(4):
        value = coarse[wz + 1]
        rect = value * jax.nn.sigmoid(value) * lower_mask
        rect2[wz, 0:C] = rect.astype(BF16)
        rect2[wz, C : 2 * C] = roll_half(rect).astype(BF16)
        gcoarse[wz + 1] = (grect[wz] * slope(value) * lower_mask).astype(BF16)

    pack_edges(gcoarse[1:5], 4, edge_c, packed.at[2])
    copies = exchange(2, gcoarse.at[pl.ds(1, 4)], 4, 4, sides_c.at[1])

    for wz in range(4):
        upward = dot(uup[...], rect2[wz])
        for a in range(2):
            for b in range(2):
                k = 2 * a + b
                for wx in range(4):
                    lanes = pl.ds((2 * wx + b) * LANE, LANE)
                    piece = upward[k * C : (k + 1) * C, wx * LANE : (wx + 1) * LANE]
                    result[2 * wz + a, :, lanes] = (
                        hidden[2 * wz + a + 1, :, lanes] + piece
                    ).astype(BF16)
    to_blocks(result, places, blocks_out)
    store_out = pltpu.make_async_copy(blocks_out, out_hbm, local_sem.at[2])
    store_out.start()
    kernel_terms(gcoarse, low3, term_c, 4, 512)
    total = jnp.zeros((4 * C, 2 * C), F32)
    for wz in range(4):
        total = total + dot_t(quarters(cot, wz), rect2[wz])
    term_u[...] = total

    for copy in copies:
        copy.wait()
    widen(gcoarse.at[pl.ds(1, 4)], sides_c.at[1], edges_in.at[2], shift_c, gcoarse3, 4, 4, here)
    convolve(gcoarse3, wcb, coarse, 4, 512)

    live_coarse = tile_lanes(half_live, C, 512)
    ghid[0] = jnp.zeros((C, 1024), BF16)
    ghid[9] = jnp.zeros((C, 1024), BF16)
    for wz in range(4):
        value = coarse[wz + 1] * live_coarse
        gdown2[wz, 0:C] = value.astype(BF16)
        gdown2[wz, C : 2 * C] = roll_half(value).astype(BF16)
        back = dot(dga[...], gdown2[wz])
        for a in range(2):
            for b in range(2):
                k = 2 * a + b
                for wx in range(4):
                    lanes = pl.ds((2 * wx + b) * LANE, LANE)
                    piece = back[k * C : (k + 1) * C, wx * LANE : (wx + 1) * LANE]
                    ghid[2 * wz + a + 1, :, lanes] = (
                        cot[2 * wz + a, :, lanes].astype(F32)
                        + piece * slope(hidden[2 * wz + a + 1, :, lanes])
                    ).astype(BF16)

    pack_edges(ghid[1:9], 8, edge_f, packed.at[3])
    copies = exchange(3, ghid.at[pl.ds(1, 8)], 8, 8, sides_f.at[1])

    total = jnp.zeros((2 * C, 4 * C), F32)
    for wz in range(4):
        total = total + dot_t(gdown2[wz], quarters(act, wz))
    term_d[...] = total
    kernel_terms(ghid, fine3, term_f, 8, 1024)

    grads[...] = jnp.zeros_like(grads)
    for k in range(4):
        wide = min(LANE, 432 - k * LANE)
        lanes = slice(k * LANE, k * LANE + wide)
        grads[144 * k : 144 * k + 144, 0:wide] = term_f[:, lanes].astype(BF16)
        grads[576 + 144 * k : 720 + 144 * k, 0:wide] = term_c[:, lanes].astype(BF16)
    grads[1152:1344, 0:96] = term_u[...].astype(BF16)
    grads[1344:1440, :] = term_d[:, 0:LANE].astype(BF16)
    grads[1440:1536, 0:64] = term_d[:, LANE:192].astype(BF16)

    def chunk_rows(index):
        return pl.ds(pl.multiple_of(index * CHUNK, CHUNK), CHUNK)

    def first_copy(d):
        peer = lax.rem(gx + d, NX)
        return pltpu.make_async_remote_copy(
            src_ref=grads.at[chunk_rows(peer)],
            dst_ref=first_in.at[d],
            send_sem=sum_send.at[0, d],
            recv_sem=sum_recv.at[0, d],
            device_id=(peer, gy),
            device_id_type=MESH,
        )

    def second_copy(d):
        return pltpu.make_async_remote_copy(
            src_ref=chunk.at[0],
            dst_ref=second_in.at[d],
            send_sem=sum_send.at[1, d],
            recv_sem=sum_recv.at[1, d],
            device_id=(gx, lax.rem(gy + d, NY)),
            device_id_type=MESH,
        )

    def third_copy(d):
        return pltpu.make_async_remote_copy(
            src_ref=chunk.at[1],
            dst_ref=done.at[chunk_rows(gx)],
            send_sem=sum_send.at[2, d],
            recv_sem=sum_recv.at[2, d],
            device_id=(lax.rem(gx + d, NX), gy),
            device_id_type=MESH,
        )

    @pl.loop(1, NX)
    def _(d):
        first_copy(d).start()

    for copy in copies:
        copy.wait()
    widen(ghid.at[pl.ds(1, 8)], sides_f.at[1], edges_in.at[3], shift_f, ghid3, 8, 8, here)
    convolve(ghid3, wfb, hidden, 8, 1024)

    @pl.loop(1, NX)
    def _(d):
        first_copy(d).wait()

    own = grads[chunk_rows(gx), :].astype(F32)
    own = lax.fori_loop(1, NX, lambda d, acc: acc + first_in[d].astype(F32), own)
    chunk[0] = own.astype(BF16)

    @pl.loop(1, NY)
    def _(d):
        second_copy(d).start()

    @pl.loop(0, 8)
    def _(z):
        result[z] = hidden[z + 1].astype(BF16)

    to_blocks(result, places, blocks_ig)
    store_ig = pltpu.make_async_copy(blocks_ig, ig_hbm, local_sem.at[3])
    store_ig.start()

    @pl.loop(1, NY)
    def _(d):
        second_copy(d).wait()

    own = lax.fori_loop(1, NY, lambda d, acc: acc + second_in[d].astype(F32), own)
    chunk[1] = own.astype(BF16)

    @pl.loop(1, NX)
    def _(d):
        third_copy(d).start()

    done[chunk_rows(gx), :] = chunk[1]

    @pl.loop(1, NX)
    def _(d):
        third_copy(d).wait()

    scale = 1.0 / math.sqrt(SLOTS * 512 * NX * NY)
    for k in range(4):
        wide = min(LANE, 432 - k * LANE)
        lanes = slice(k * LANE, k * LANE + wide)
        gf_out[:, lanes] = done[144 * k : 144 * k + 144, 0:wide].astype(F32) * scale
        gc_out[:, lanes] = done[576 + 144 * k : 720 + 144 * k, 0:wide].astype(F32) * scale
    gu_out[...] = done[1152:1344, 0:96].astype(F32) * scale
    gd_out[:, 0:LANE] = done[1344:1440, :].astype(F32) * scale
    gd_out[:, LANE:192] = done[1440:1536, 0:64].astype(F32) * scale
    store_out.wait()
    store_ig.wait()


def on_device(
    features, block_slots, block_count, cotangent, fine_weight, down_weight, coarse_weight, up_weight
):
    def forward_rows(weight):
        return (
            weight.reshape(C, 3, 9, C)[:, ::-1].transpose(1, 0, 2, 3).reshape(3 * C, 9 * C)
        )

    def backward_rows(weight):
        return weight.reshape(C, 3, 9, C)[:, :, ::-1].transpose(1, 3, 2, 0).reshape(3 * C, 9 * C)

    down = down_weight.reshape(C, 4, 2, C)
    ddn = down.transpose(2, 0, 1, 3).reshape(2 * C, 4 * C)
    dga = down.transpose(1, 3, 2, 0).reshape(4 * C, 2 * C)
    up = up_weight.reshape(4, 2, C, C)
    uup = up.transpose(0, 2, 1, 3).reshape(4 * C, 2 * C)
    ugr = up.transpose(1, 3, 0, 2).reshape(2 * C, 4 * C)

    vmem = pl.BlockSpec(memory_space=pltpu.VMEM)
    smem = pl.BlockSpec(memory_space=pltpu.SMEM)
    anywhere = pl.BlockSpec(memory_space=pl.ANY)
    blocks = (SLOTS, C, 512)
    out, ig, gf, gc, gu, gd = pl.pallas_call(
        section,
        out_shape=(
            jax.ShapeDtypeStruct(blocks, BF16),
            jax.ShapeDtypeStruct(blocks, BF16),
            jax.ShapeDtypeStruct((3 * C, 9 * C), F32),
            jax.ShapeDtypeStruct((3 * C, 9 * C), F32),
            jax.ShapeDtypeStruct((4 * C, 2 * C), F32),
            jax.ShapeDtypeStruct((2 * C, 4 * C), F32),
        ),
        in_specs=[smem, smem, anywhere, anywhere] + [vmem] * 8,
        out_specs=(anywhere, anywhere, vmem, vmem, vmem, vmem),
        scratch_shapes=[
            pltpu.VMEM(blocks, BF16),
            pltpu.VMEM(blocks, BF16),
            pltpu.VMEM((8, C, 1024), BF16),
            pltpu.VMEM((1024, 1024), BF16),
            pltpu.VMEM((8, 256, 256), BF16),
            pltpu.VMEM((4, 256, 256), BF16),
            pltpu.VMEM((1024, LANE), BF16),
            pltpu.VMEM((512, LANE), BF16),
            pltpu.VMEM((8, C, 1024), BF16),
            pltpu.VMEM((8, C, 1024), BF16),
            pltpu.VMEM((8, 3 * C, 1280), BF16),
            pltpu.VMEM((10, C, 1024), F32),
            pltpu.VMEM((8, C, 1024), BF16),
            pltpu.VMEM((4, C, 512), BF16),
            pltpu.VMEM((4, 3 * C, 768), BF16),
            pltpu.VMEM((6, C, 512), F32),
            pltpu.VMEM((4, C, 512), F32),
            pltpu.VMEM((4, 2 * C, 512), BF16),
            pltpu.VMEM((6, C, 512), BF16),
            pltpu.VMEM((4, 3 * C, 768), BF16),
            pltpu.VMEM((4, 2 * C, 512), BF16),
            pltpu.VMEM((10, C, 1024), BF16),
            pltpu.VMEM((8, 3 * C, 1280), BF16),
            pltpu.VMEM((8, C, 1024), BF16),
            pltpu.VMEM(blocks, BF16),
            pltpu.VMEM(blocks, BF16),
            pltpu.VMEM((3 * C, 9 * C), F32),
            pltpu.VMEM((3 * C, 9 * C), F32),
            pltpu.VMEM((4 * C, 2 * C), F32),
            pltpu.VMEM((2 * C, 4 * C), F32),
            pltpu.VMEM((4, C, LANE), BF16),
            pltpu.VMEM((2, 2, 8, C, LANE), BF16),
            pltpu.VMEM((2, 2, 4, C, LANE), BF16),
            pltpu.VMEM((4, 6, C, LANE), BF16),
            pltpu.VMEM((ROWS, LANE), BF16),
            pltpu.VMEM((NX, CHUNK, LANE), BF16),
            pltpu.VMEM((2, CHUNK, LANE), BF16),
            pltpu.VMEM((NY, CHUNK, LANE), BF16),
            pltpu.VMEM((ROWS, LANE), BF16),
            pltpu.SemaphoreType.DMA((4,)),
            pltpu.SemaphoreType.DMA((4, 8)),
            pltpu.SemaphoreType.DMA((4, 8)),
            pltpu.SemaphoreType.DMA((3, NX)),
            pltpu.SemaphoreType.DMA((3, NX)),
        ],
        compiler_params=pltpu.CompilerParams(
            collective_id=0, has_side_effects=True, vmem_limit_bytes=50 * 1024 * 1024
        ),
        name="section",
    )(
        block_slots.reshape(1, SLOTS),
        block_count.reshape(1, 1),
        features.reshape(blocks),
        cotangent.reshape(blocks),
        forward_rows(fine_weight),
        backward_rows(fine_weight),
        forward_rows(coarse_weight),
        backward_rows(coarse_weight),
        ddn,
        dga,
        uup,
        ugr,
    )

    def kernel_grad(rows):
        return rows.reshape(3, C, 9, C)[::-1].transpose(1, 0, 2, 3).reshape(C, 27, C)

    shape_out = (1, 1) + blocks
    return (
        out.reshape(shape_out),
        ig.reshape(shape_out),
        kernel_grad(gf),
        gd.reshape(2, C, 4, C).transpose(1, 2, 0, 3).reshape(C, 8, C),
        kernel_grad(gc),
        gu.reshape(4, C, 2, C).transpose(0, 2, 1, 3).reshape(8, C, C),
    )


def solution(mesh):
    split = P("gx", "gy", None, None, None)
    return jax.shard_map(
        on_device,
        mesh=mesh,
        in_specs=(split, P("gx", "gy", None), P("gx", "gy"), split, P(), P(), P(), P()),
        out_specs=(split, split, P(), P(), P(), P()),
        check_vma=False,
    )
```

```python
import math

import jax
import jax.numpy as jnp
from jax import lax
from jax.experimental import pallas as pl
from jax.experimental.pallas import tpu as pltpu
from jax.sharding import PartitionSpec as P

C = 48
SLOTS = 16
LANE = 128
NX = 16
NY = 16
ROWS = 768
CHUNK = ROWS // NY
F32 = jnp.float32
BF16 = jnp.bfloat16
MESH = pl.DeviceIdType.MESH


def dot(a, b):
    return jnp.dot(a, b, preferred_element_type=F32)


def dot_t(a, b):
    return lax.dot_general(a, b, (((1,), (1,)), ((), ())), preferred_element_type=F32)


def iota(shape, dim):
    return lax.broadcasted_iota(jnp.int32, shape, dim)


def one_hot(cond):
    return jnp.where(cond, 1.0, 0.0).astype(BF16)


def build_shift(s_ref, count, last):
    row = iota((256, 256), 0)
    col = iota((256, 256), 1)
    lane = col % LANE
    right = col >= LANE
    if last == 127:
        before = jnp.where(lane < 64, lane + 63, lane - 64)
        after = jnp.where(lane < 64, lane + 64, lane - 63)
        before = jnp.where(lane == 0, -1, before)
        after = jnp.where(lane == 127, -1, after)
    else:
        before = jnp.where((lane == 0) | (lane > last), -1, lane - 1)
        after = jnp.where(lane >= last, -1, lane + 1)
    source = jnp.where(right, after, before)
    place = jnp.where(lane == jnp.where(right, last, 0), jnp.where(right, LANE + 8, LANE), -512)

    @pl.loop(0, count)
    def _(x):
        s_ref[x] = one_hot((row == source) | (row == place + x))


def build_edge(t_ref, length, last):
    row = iota((length, LANE), 0)
    col = iota((length, LANE), 1)
    lane = row % LANE
    x = row // LANE
    t_ref[...] = one_hot(((lane == last) & (col == x)) | ((lane == 0) & (col == x + 8)))


def build_places(e_ref, slots_ref, live_count):
    e_ref[...] = jnp.zeros_like(e_ref)
    row = iota((16, 256), 0)
    col = iota((16, 256), 1)
    y = row % 8
    own = (row // 8) == (col // LANE)
    spot = col % LANE - 64 * (y % 2) - y // 2

    @pl.loop(0, SLOTS)
    def _(s):
        place = jnp.where(s < live_count, slots_ref[0, s], 4096)
        tile = one_hot(own & (spot == 4 * place))
        for j in range(4):
            e_ref[pl.ds(pl.multiple_of(64 * s + 16 * j, 16), 16), 256 * j : 256 * j + 256] = tile


def live_lanes(slots_ref, live_count):
    spot = (iota((8, LANE), 1) % 64) // 4

    def step(s, total):
        place = jnp.where(s < live_count, slots_ref[0, s], 4096)
        return total + jnp.where(spot == place, 1.0, 0.0)

    return lax.fori_loop(0, SLOTS, step, jnp.zeros((8, LANE), F32))


def to_grid(blocks, work, e_ref, grid):
    for t in range(8):
        lanes = slice(t * LANE, (t + 1) * LANE)
        for pair in range(4):
            one = blocks[2 * t, :, pair * LANE : (pair + 1) * LANE]
            two = blocks[2 * t + 1, :, pair * LANE : (pair + 1) * LANE]
            work[2 * pair, :, lanes] = jnp.concatenate([one[:, :64], two[:, :64]], axis=1)
            work[2 * pair + 1, :, lanes] = jnp.concatenate([one[:, 64:], two[:, 64:]], axis=1)

    for n in range(4):
        lanes = slice(n * 256, (n + 1) * 256)
        moved = dot(work[...].reshape(8 * C, 1024), e_ref[:, lanes])
        grid[:, :, lanes] = moved.astype(BF16).reshape(8, C, 256)


def to_blocks(grid, e_ref, blocks):
    for n in range(4):
        rows = slice(n * 256, (n + 1) * 256)
        moved = dot_t(grid[...].reshape(8 * C, 1024), e_ref[rows, :])
        moved = moved.astype(BF16).reshape(8, C, 256)
        for pair in range(4):
            for k in range(4):
                low = moved[2 * pair, :, 64 * k : 64 * k + 64]
                high = moved[2 * pair + 1, :, 64 * k : 64 * k + 64]
                blocks[4 * n + k, :, pair * LANE : (pair + 1) * LANE] = jnp.concatenate(
                    [low, high], axis=1
                )


def pack_edges(grid, depth, t_ref, packed):
    edges = dot(grid.reshape(depth * C, grid.shape[2]), t_ref[...]).reshape(depth, C, LANE)
    total = edges[0]
    for z in range(1, depth):
        total = total + pltpu.roll(edges[z], 16 * z, 1)
    packed[...] = total.astype(BF16)


def unpack_edges(received, row, left_ok, right_ok, depth):
    lane = iota((C, LANE), 1) % 16
    left = jnp.where(left_ok, received[2 * row].astype(F32), 0.0)
    right = jnp.where(right_ok, received[2 * row + 1].astype(F32), 0.0)
    both = jnp.where(lane < 8, left, right)
    parts = [both] + [pltpu.roll(both, LANE - 16 * z, 1) for z in range(1, depth)]
    return jnp.stack(parts, axis=0).astype(BF16).reshape(depth * C, LANE)


def widen(grid, sides, received, s_ref, wide, count, depth, place):
    gx, gy = place
    low_ok, high_ok = gx > 0, gx < NX - 1
    left_ok, right_ok = gy > 0, gy < NY - 1

    def put(rows, halo, x, lanes):
        moved = dot(jnp.concatenate([rows, halo], axis=1), s_ref[x]).astype(BF16)
        wide[:, 0:C, lanes] = moved[:, :LANE].reshape(depth, C, LANE)
        wide[:, C : 2 * C, lanes] = rows.reshape(depth, C, LANE)
        wide[:, 2 * C : 3 * C, lanes] = moved[:, LANE:].reshape(depth, C, LANE)

    zero = jnp.zeros((depth * C, LANE), BF16)
    halo = unpack_edges(received, 0, left_ok & low_ok, right_ok & low_ok, depth)
    rows = jnp.where(low_ok, sides[0].reshape(depth * C, LANE), zero)
    put(rows, halo, count - 1, pl.ds(0, LANE))
    halo = unpack_edges(received, 2, left_ok & high_ok, right_ok & high_ok, depth)
    rows = jnp.where(high_ok, sides[1].reshape(depth * C, LANE), zero)
    put(rows, halo, 0, pl.ds((count + 1) * LANE, LANE))
    halo = unpack_edges(received, 1, left_ok, right_ok, depth)

    for x in range(count):
        rows = grid[:, :, x * LANE : (x + 1) * LANE].reshape(depth * C, LANE)
        put(rows, halo, x, pl.ds((x + 1) * LANE, LANE))


def window(wide, z, first, width):
    return jnp.concatenate(
        [wide[z, :, first + dx * LANE : first + dx * LANE + width] for dx in range(3)], axis=0
    )


def convolve(wide, weight, total, depth, width):
    total[...] = jnp.zeros_like(total)
    for z in range(depth):
        for first in range(0, width, 256):
            piece = dot(weight[...], window(wide, z, first, 256)).reshape(3, C, 256)
            lanes = slice(first, first + 256)
            total[z : z + 3, :, lanes] = total[z : z + 3, :, lanes] + piece


def kernel_terms(grad, wide, total, depth, width):
    ahead = [grad[z : z + 3].reshape(3 * C, width) for z in range(depth)]
    pieces = [window(wide, z, 0, width) for z in range(depth)]
    total[...] = dot_t(jnp.concatenate(ahead, axis=1), jnp.concatenate(pieces, axis=1))


def quarters(grid, wz):
    columns = []
    for a in range(2):
        for b in range(2):
            columns.append(
                jnp.concatenate(
                    [
                        grid[2 * wz + a, :, (2 * wx + b) * LANE : (2 * wx + b + 1) * LANE]
                        for wx in range(4)
                    ],
                    axis=1,
                )
            )
    return jnp.concatenate(columns, axis=0)


def tile_lanes(mask, rows, width):
    return jnp.broadcast_to(jnp.concatenate([mask] * (width // LANE), axis=1)[0:1], (rows, width))


def roll_half(value):
    parts = [
        pltpu.roll(value[:, k * LANE : (k + 1) * LANE], 64, 1) for k in range(value.shape[1] // LANE)
    ]
    return jnp.concatenate(parts, axis=1)


def kernel_rows(weight, stack, eye, forward, backward):
    for dz in range(3):
        for k in range(9):
            block = weight[9 * dz + k]
            forward[(2 - dz) * C : (3 - dz) * C, k * C : (k + 1) * C] = block
            stack[(8 - k) * C : (9 - k) * C, :] = block
        backward[dz * C : (dz + 1) * C, :] = dot_t(eye[0:C, 0:C], stack[...]).astype(BF16)


def step_rows(down, up, stage, eye, ddn, dga, uup, ugr):
    for o in range(C):
        stage[8 * o : 8 * o + 8, 0:C] = down[o].astype(F32)
    for k in range(4):
        for e in range(2):
            q = 2 * k + e
            block = stage[pl.ds(q, C, stride=8), :].astype(BF16)[:, 0:C]
            ddn[e * C : (e + 1) * C, k * C : (k + 1) * C] = block
            uup[k * C : (k + 1) * C, e * C : (e + 1) * C] = up[q]
    dga[...] = dot_t(eye[...], ddn[...]).astype(BF16)
    ugr[...] = dot_t(eye[0 : 2 * C, 0 : 2 * C], uup[...]).astype(BF16)


def slope(value):
    sigma = jax.nn.sigmoid(value)
    return sigma * (1.0 + value * (1.0 - sigma))


def section(
    slots_ref,
    count_ref,
    feat,
    cot_hbm,
    fine_hbm,
    down_hbm,
    coarse_hbm,
    up_hbm,
    blocks_out,
    blocks_ig,
    sums,
    cot_in,
    fine_w,
    down_w,
    coarse_w,
    up_w,
    stage,
    stack,
    eye,
    wf,
    wfb,
    wc,
    wcb,
    ddn,
    dga,
    uup,
    ugr,
    work,
    places,
    shift_f,
    shift_c,
    edge_f,
    edge_c,
    fine,
    cot,
    fine3,
    hidden,
    act,
    low,
    low3,
    coarse,
    grect,
    rect2,
    gcoarse,
    gcoarse3,
    gdown2,
    ghid,
    ghid3,
    result,
    term_f,
    term_c,
    packed,
    sides_f,
    sides_c,
    edges_in,
    grads,
    first_in,
    chunk,
    second_in,
    local_sem,
    send_sem,
    recv_sem,
    sum_send,
    sum_recv,
):
    gx = lax.axis_index("gx")
    gy = lax.axis_index("gy")
    here = (gx, gy)

    loads = [
        pltpu.make_async_copy(source, target, local_sem.at[k])
        for k, (source, target) in enumerate(
            (
                (fine_hbm, fine_w),
                (down_hbm, down_w),
                (coarse_hbm, coarse_w),
                (up_hbm, up_w),
                (cot_hbm, cot_in),
            )
        )
    ]
    for load in loads:
        load.start()

    barrier = pltpu.get_barrier_semaphore()

    @pl.loop(1, NX)
    def _(d):
        pl.semaphore_signal(
            barrier, inc=1, device_id=(lax.rem(gx + d, NX), gy), device_id_type=MESH
        )
        pl.semaphore_signal(
            barrier, inc=1, device_id=(gx, lax.rem(gy + d, NY)), device_id_type=MESH
        )

    for dx in (1, NX - 1):
        for dy in (1, NY - 1):
            pl.semaphore_signal(
                barrier,
                inc=1,
                device_id=(lax.rem(gx + dx, NX), lax.rem(gy + dy, NY)),
                device_id_type=MESH,
            )

    live_count = count_ref[0, 0]
    build_places(places, slots_ref, live_count)
    build_edge(edge_f, 1024, 127)
    live = live_lanes(slots_ref, live_count)
    half_live = jnp.where(iota((8, LANE), 1) < 64, live, 0.0)
    lower = jnp.where(iota((8, LANE), 1) < 64, 1.0, 0.0)

    def exchange(step, source, depth, count, sides):
        copies = []
        for side in range(2):
            x = count - 1 if side == 0 else 0
            shift = 1 if side == 0 else NX - 1
            copies.append(
                pltpu.make_async_remote_copy(
                    src_ref=source.at[:, :, pl.ds(x * LANE, LANE)],
                    dst_ref=sides.at[side],
                    send_sem=send_sem.at[step, side],
                    recv_sem=recv_sem.at[step, side],
                    device_id=(lax.rem(gx + shift, NX), gy),
                    device_id_type=MESH,
                )
            )
        for row in range(3):
            for side in range(2):
                copies.append(
                    pltpu.make_async_remote_copy(
                        src_ref=packed.at[step],
                        dst_ref=edges_in.at[step, 2 * row + side],
                        send_sem=send_sem.at[step, 2 + 2 * row + side],
                        recv_sem=recv_sem.at[step, 2 + 2 * row + side],
                        device_id=(
                            lax.rem(gx + NX + 1 - row, NX),
                            lax.rem(gy + (1 if side == 0 else NY - 1), NY),
                        ),
                        device_id_type=MESH,
                    )
                )
        for copy in copies:
            copy.start()
        return copies

    to_grid(feat, work, places, fine)
    pack_edges(fine[...], 8, edge_f, packed.at[0])
    pl.semaphore_wait(barrier, 2 * (NX - 1) + 4)
    copies = exchange(0, fine, 8, 8, sides_f.at[0])

    build_shift(shift_f, 8, 127)
    build_shift(shift_c, 4, 63)
    build_edge(edge_c, 512, 63)
    for load in loads:
        load.wait()
    eye[...] = one_hot(iota((4 * C, 4 * C), 0) == iota((4 * C, 4 * C), 1))
    stage[...] = jnp.zeros_like(stage)
    kernel_rows(fine_w, stack, eye, wf, wfb)
    kernel_rows(coarse_w, stack, eye, wc, wcb)
    step_rows(down_w, up_w, stage, eye, ddn, dga, uup, ugr)
    to_grid(cot_in, work, places, cot)
    for wz in range(4):
        both = dot(ugr[...], quarters(cot, wz))
        grect[wz] = both[:C] + roll_half(both[C:])

    for copy in copies:
        copy.wait()
    widen(fine, sides_f.at[0], edges_in.at[0], shift_f, fine3, 8, 8, here)
    convolve(fine3, wf, hidden, 8, 1024)

    live_fine = tile_lanes(live, C, 1024)

    @pl.loop(0, 8)
    def _(z):
        value = hidden[z + 1] * live_fine
        hidden[z + 1] = value
        act[z] = (value * jax.nn.sigmoid(value)).astype(BF16)

    lower_mask = tile_lanes(lower, C, 512)
    for wz in range(4):
        both = dot(ddn[...], quarters(act, wz))
        low[wz] = ((both[:C] + roll_half(both[C:])) * lower_mask).astype(BF16)

    pack_edges(low[...], 4, edge_c, packed.at[1])
    copies = exchange(1, low, 4, 4, sides_c.at[0])
    for copy in copies:
        copy.wait()
    widen(low, sides_c.at[0], edges_in.at[1], shift_c, low3, 4, 4, here)
    convolve(low3, wc, coarse, 4, 512)

    gcoarse[...] = jnp.zeros_like(gcoarse)
    for wz in range(4):
        value = coarse[wz + 1]
        rect = value * jax.nn.sigmoid(value) * lower_mask
        rect2[wz, 0:C] = rect.astype(BF16)
        rect2[wz, C : 2 * C] = roll_half(rect).astype(BF16)
        gcoarse[wz + 1] = (grect[wz] * slope(value) * lower_mask).astype(BF16)

    pack_edges(gcoarse[1:5], 4, edge_c, packed.at[2])
    copies = exchange(2, gcoarse.at[pl.ds(1, 4)], 4, 4, sides_c.at[1])

    def chunk_rows(index):
        return pl.ds(pl.multiple_of(index * CHUNK, CHUNK), CHUNK)

    def reduction(part):
        def first(d):
            peer = lax.rem(gy + d, NY)
            return pltpu.make_async_remote_copy(
                src_ref=grads.at[part, chunk_rows(peer)],
                dst_ref=first_in.at[part, d],
                send_sem=sum_send.at[part, 0, d],
                recv_sem=sum_recv.at[part, 0, d],
                device_id=(gx, peer),
                device_id_type=MESH,
            )

        def second(d):
            return pltpu.make_async_remote_copy(
                src_ref=chunk.at[part, 0],
                dst_ref=second_in.at[part, d],
                send_sem=sum_send.at[part, 1, d],
                recv_sem=sum_recv.at[part, 1, d],
                device_id=(lax.rem(gx + d, NX), gy),
                device_id_type=MESH,
            )

        def third(d):
            return pltpu.make_async_remote_copy(
                src_ref=chunk.at[part, 1],
                dst_ref=sums.at[part, chunk_rows(gy)],
                send_sem=sum_send.at[part, 2, d],
                recv_sem=sum_recv.at[part, 2, d],
                device_id=(gx, lax.rem(gy + d, NY)),
                device_id_type=MESH,
            )

        return first, second, third

    def start_all(copy):
        @pl.loop(1, NX)
        def _(d):
            copy(d).start()

    def wait_all(copy):
        @pl.loop(1, NX)
        def _(d):
            copy(d).wait()

    def start_second(part):
        own = grads[part, chunk_rows(gy), :].astype(F32)
        for d in range(1, NY):
            own = own + first_in[part, d].astype(F32)
        chunk[part, 0] = own.astype(BF16)
        start_all(reductions[part][1])
        return own

    def start_third(part, own):
        for d in range(1, NX):
            own = own + second_in[part, d].astype(F32)
        chunk[part, 1] = own.astype(BF16)
        start_all(reductions[part][2])
        sums[part, chunk_rows(gy), :] = chunk[part, 1]

    def put_rows(part, term):
        for k in range(4):
            wide = min(LANE, 9 * C - k * LANE)
            grads[part, 3 * C * k : 3 * C * (k + 1), 0:wide] = term[
                :, k * LANE : k * LANE + wide
            ].astype(BF16)

    reductions = [reduction(0), reduction(1)]
    grads[...] = jnp.zeros_like(grads)

    for wz in range(4):
        upward = dot(uup[...], rect2[wz])
        for a in range(2):
            for b in range(2):
                k = 2 * a + b
                for wx in range(4):
                    lanes = pl.ds((2 * wx + b) * LANE, LANE)
                    piece = upward[k * C : (k + 1) * C, wx * LANE : (wx + 1) * LANE]
                    result[2 * wz + a, :, lanes] = (
                        hidden[2 * wz + a + 1, :, lanes] + piece
                    ).astype(BF16)
    kernel_terms(gcoarse, low3, term_c, 4, 512)
    total = jnp.zeros((4 * C, 2 * C), F32)
    for wz in range(4):
        total = total + dot_t(quarters(cot, wz), rect2[wz])
    put_rows(0, term_c)
    grads[0, 12 * C : 16 * C, 0 : 2 * C] = total.astype(BF16)
    start_all(reductions[0][0])
    to_blocks(result, places, blocks_out)

    for copy in copies:
        copy.wait()
    widen(gcoarse.at[pl.ds(1, 4)], sides_c.at[1], edges_in.at[2], shift_c, gcoarse3, 4, 4, here)
    convolve(gcoarse3, wcb, coarse, 4, 512)

    live_coarse = tile_lanes(half_live, C, 512)
    ghid[0] = jnp.zeros((C, 1024), BF16)
    ghid[9] = jnp.zeros((C, 1024), BF16)
    for wz in range(4):
        value = coarse[wz + 1] * live_coarse
        gdown2[wz, 0:C] = value.astype(BF16)
        gdown2[wz, C : 2 * C] = roll_half(value).astype(BF16)
        back = dot(dga[...], gdown2[wz])
        for a in range(2):
            for b in range(2):
                k = 2 * a + b
                for wx in range(4):
                    lanes = pl.ds((2 * wx + b) * LANE, LANE)
                    piece = back[k * C : (k + 1) * C, wx * LANE : (wx + 1) * LANE]
                    ghid[2 * wz + a + 1, :, lanes] = (
                        cot[2 * wz + a, :, lanes].astype(F32)
                        + piece * slope(hidden[2 * wz + a + 1, :, lanes])
                    ).astype(BF16)

    pack_edges(ghid[1:9], 8, edge_f, packed.at[3])
    copies = exchange(3, ghid.at[pl.ds(1, 8)], 8, 8, sides_f.at[1])

    wait_all(reductions[0][0])
    early = start_second(0)
    total = jnp.zeros((2 * C, 4 * C), F32)
    for wz in range(4):
        total = total + dot_t(gdown2[wz], quarters(act, wz))
    grads[1, 12 * C : 14 * C, :] = total[:, 0:LANE].astype(BF16)
    grads[1, 14 * C : 16 * C, 0:64] = total[:, LANE:192].astype(BF16)
    kernel_terms(ghid, fine3, term_f, 8, 1024)
    put_rows(1, term_f)
    start_all(reductions[1][0])

    for copy in copies:
        copy.wait()
    widen(ghid.at[pl.ds(1, 8)], sides_f.at[1], edges_in.at[3], shift_f, ghid3, 8, 8, here)
    convolve(ghid3, wfb, hidden, 8, 1024)

    wait_all(reductions[1][0])
    late = start_second(1)
    wait_all(reductions[0][1])
    start_third(0, early)

    for z in range(8):
        result[z] = hidden[z + 1].astype(BF16)
    to_blocks(result, places, blocks_ig)

    wait_all(reductions[1][1])
    start_third(1, late)
    wait_all(reductions[0][2])
    wait_all(reductions[1][2])


def unpack(sums, out_in, ig_in, out_hbm, ig_hbm, gf, gd, gc, gu, stage, sem):
    copies = [
        pltpu.make_async_copy(out_in, out_hbm, sem.at[0]),
        pltpu.make_async_copy(ig_in, ig_hbm, sem.at[1]),
    ]
    for copy in copies:
        copy.start()
    scale = 1.0 / math.sqrt(SLOTS * 512 * NX * NY)

    for part, target in ((1, gf), (0, gc)):
        rows = jnp.concatenate(
            [sums[part, 3 * C * k : 3 * C * (k + 1), :] for k in range(4)], axis=1
        )
        rows = rows.astype(F32) * scale
        for dz in range(3):
            for k in range(9):
                block = rows[(2 - dz) * C : (3 - dz) * C, k * C : (k + 1) * C]
                target[9 * dz + k] = block
    tail = sums[1, 14 * C : 16 * C, :]
    rows = jnp.concatenate([sums[1, 12 * C : 14 * C, :], tail, tail], axis=1)
    rows = rows.astype(F32) * scale
    for k in range(4):
        for e in range(2):
            gu[2 * k + e] = (
                sums[0, (12 + k) * C : (13 + k) * C, e * C : (e + 1) * C].astype(F32) * scale
            )
            block = rows[e * C : (e + 1) * C, k * C : k * C + LANE]
            stage[pl.ds(2 * k + e, C, stride=8), :] = block
    for o in range(C):
        gd[o] = stage[8 * o : 8 * o + 8, 0:C]
    for copy in copies:
        copy.wait()


def on_device(
    features, block_slots, block_count, cotangent, fine_weight, down_weight, coarse_weight, up_weight
):
    vmem = pl.BlockSpec(memory_space=pltpu.VMEM)
    smem = pl.BlockSpec(memory_space=pltpu.SMEM)
    hbm = pl.BlockSpec(memory_space=pltpu.HBM)
    blocks = (SLOTS, C, 512)
    kernel_shape = (27, C, C)
    block_shape = jax.ShapeDtypeStruct(blocks, BF16)
    out, ig, sums = pl.pallas_call(
        section,
        out_shape=(block_shape, block_shape, jax.ShapeDtypeStruct((2, ROWS, LANE), BF16)),
        in_specs=[smem, smem, vmem] + [hbm] * 5,
        out_specs=(vmem, vmem, vmem),
        scratch_shapes=[
            pltpu.VMEM(blocks, BF16),
            pltpu.VMEM(kernel_shape, BF16),
            pltpu.VMEM((C, 8, C), BF16),
            pltpu.VMEM(kernel_shape, BF16),
            pltpu.VMEM((8, C, C), BF16),
            pltpu.VMEM((8 * C, LANE), F32),
            pltpu.VMEM((9 * C, C), BF16),
            pltpu.VMEM((4 * C, 4 * C), BF16),
            pltpu.VMEM((3 * C, 9 * C), BF16),
            pltpu.VMEM((3 * C, 9 * C), BF16),
            pltpu.VMEM((3 * C, 9 * C), BF16),
            pltpu.VMEM((3 * C, 9 * C), BF16),
            pltpu.VMEM((2 * C, 4 * C), BF16),
            pltpu.VMEM((4 * C, 2 * C), BF16),
            pltpu.VMEM((4 * C, 2 * C), BF16),
            pltpu.VMEM((2 * C, 4 * C), BF16),
            pltpu.VMEM((8, C, 1024), BF16),
            pltpu.VMEM((1024, 1024), BF16),
            pltpu.VMEM((8, 256, 256), BF16),
            pltpu.VMEM((4, 256, 256), BF16),
            pltpu.VMEM((1024, LANE), BF16),
            pltpu.VMEM((512, LANE), BF16),
            pltpu.VMEM((8, C, 1024), BF16),
            pltpu.VMEM((8, C, 1024), BF16),
            pltpu.VMEM((8, 3 * C, 1280), BF16),
            pltpu.VMEM((10, C, 1024), F32),
            pltpu.VMEM((8, C, 1024), BF16),
            pltpu.VMEM((4, C, 512), BF16),
            pltpu.VMEM((4, 3 * C, 768), BF16),
            pltpu.VMEM((6, C, 512), F32),
            pltpu.VMEM((4, C, 512), F32),
            pltpu.VMEM((4, 2 * C, 512), BF16),
            pltpu.VMEM((6, C, 512), BF16),
            pltpu.VMEM((4, 3 * C, 768), BF16),
            pltpu.VMEM((4, 2 * C, 512), BF16),
            pltpu.VMEM((10, C, 1024), BF16),
            pltpu.VMEM((8, 3 * C, 1280), BF16),
            pltpu.VMEM((8, C, 1024), BF16),
            pltpu.VMEM((3 * C, 9 * C), F32),
            pltpu.VMEM((3 * C, 9 * C), F32),
            pltpu.VMEM((4, C, LANE), BF16),
            pltpu.VMEM((2, 2, 8, C, LANE), BF16),
            pltpu.VMEM((2, 2, 4, C, LANE), BF16),
            pltpu.VMEM((4, 6, C, LANE), BF16),
            pltpu.VMEM((2, ROWS, LANE), BF16),
            pltpu.VMEM((2, NY, CHUNK, LANE), BF16),
            pltpu.VMEM((2, 2, CHUNK, LANE), BF16),
            pltpu.VMEM((2, NX, CHUNK, LANE), BF16),
            pltpu.SemaphoreType.DMA((5,)),
            pltpu.SemaphoreType.DMA((4, 8)),
            pltpu.SemaphoreType.DMA((4, 8)),
            pltpu.SemaphoreType.DMA((2, 3, NX)),
            pltpu.SemaphoreType.DMA((2, 3, NX)),
        ],
        compiler_params=pltpu.CompilerParams(
            collective_id=0, has_side_effects=True, vmem_limit_bytes=50 * 1024 * 1024
        ),
        name="section",
    )(
        block_slots.reshape(1, SLOTS),
        block_count.reshape(1, 1),
        features.reshape(blocks),
        cotangent.reshape(blocks),
        fine_weight.transpose(1, 0, 2),
        down_weight,
        coarse_weight.transpose(1, 0, 2),
        up_weight,
    )
    out, ig, gf, gd, gc, gu = pl.pallas_call(
        unpack,
        out_shape=(
            block_shape,
            block_shape,
            jax.ShapeDtypeStruct(kernel_shape, F32),
            jax.ShapeDtypeStruct((C, 8, C), F32),
            jax.ShapeDtypeStruct(kernel_shape, F32),
            jax.ShapeDtypeStruct((8, C, C), F32),
        ),
        in_specs=[vmem, vmem, vmem],
        out_specs=(hbm, hbm, vmem, vmem, vmem, vmem),
        scratch_shapes=[pltpu.VMEM((8 * C, LANE), F32), pltpu.SemaphoreType.DMA((2,))],
        compiler_params=pltpu.CompilerParams(vmem_limit_bytes=8 * 1024 * 1024),
        name="unpack",
    )(sums, out, ig)
    shape_out = (1, 1) + blocks
    gf, gc = gf.transpose(1, 0, 2), gc.transpose(1, 0, 2)
    return out.reshape(shape_out), ig.reshape(shape_out), gf, gd, gc, gu


def solution(mesh):
    split = P("gx", "gy", None, None, None)
    return jax.shard_map(
        on_device,
        mesh=mesh,
        in_specs=(split, P("gx", "gy", None), P("gx", "gy"), split, P(), P(), P(), P()),
        out_specs=(split, split, P(), P(), P(), P()),
        check_vma=False,
    )
```

```python
import math

import jax
import jax.numpy as jnp
from jax import lax
from jax.experimental import pallas as pl
from jax.experimental.pallas import tpu as pltpu
from jax.sharding import PartitionSpec as P

C = 48
SLOTS = 16
LANE = 128
NX = 16
NY = 16
ROWS_A = 512
ROWS_B = 1024
F32 = jnp.float32
BF16 = jnp.bfloat16
MESH = pl.DeviceIdType.MESH


def dot(a, b):
    return jnp.dot(a, b, preferred_element_type=F32)


def dot_t(a, b):
    return lax.dot_general(a, b, (((1,), (1,)), ((), ())), preferred_element_type=F32)


def iota(shape, dim):
    return lax.broadcasted_iota(jnp.int32, shape, dim)


def one_hot(cond):
    return jnp.where(cond, 1.0, 0.0).astype(BF16)


def build_shift_fine(s_ref):
    row = iota((256, 256), 0)
    col = iota((256, 256), 1)
    lane = col % LANE
    right = col >= LANE
    before = jnp.where(lane < 64, lane + 63, lane - 64)
    after = jnp.where(lane < 64, lane + 64, lane - 63)
    before = jnp.where(lane == 0, -1, before)
    after = jnp.where(lane == 127, -1, after)
    source = jnp.where(right, after, before)
    place = jnp.where(lane == jnp.where(right, 127, 0), jnp.where(right, LANE + 8, LANE), -512)

    @pl.loop(0, 8)
    def _(x):
        s_ref[x] = one_hot((row == source) | (row == place + x))


def coarse_edge(group):
    return jnp.where(
        group == 0, 63, jnp.where(group == 1, 62, jnp.where(group == 2, 0, jnp.where(group == 3, 1, -1)))
    )


def build_shift_coarse(s_ref):
    row = iota((256, 384), 0)
    col = iota((256, 384), 1)
    source = (col % LANE + col // LANE + LANE - 1) % LANE
    halo = row - LANE
    spot = jnp.where(
        halo < 4, 127, jnp.where(halo < 8, 126, jnp.where(halo < 12, 64, jnp.where(halo < 16, 65, -1)))
    )
    own = (row < 64) & (row == source)
    other = (halo >= 0) & (spot == source)

    @pl.loop(0, 4)
    def _(x):
        s_ref[x] = one_hot(own | (other & (halo % 4 == x)))


def build_roll(r_ref):
    row = iota((LANE, 256), 0)
    col = iota((LANE, 256), 1)
    r_ref[...] = one_hot(row == (col % LANE + 2 * (col // LANE) + LANE - 1) % LANE)


def build_edges(fine_ref, coarse_ref):
    row = iota((1024, LANE), 0)
    col = iota((1024, LANE), 1)
    lane = row % LANE
    x = row // LANE
    fine_ref[...] = one_hot(((lane == 127) & (col == x)) | ((lane == 0) & (col == x + 8)))
    row = iota((512, LANE), 0)
    col = iota((512, LANE), 1)
    coarse_ref[...] = one_hot((row % LANE == coarse_edge(col // 4)) & (row // LANE == col % 4))


def build_places(e_ref, slots_ref, live_count):
    e_ref[...] = jnp.zeros_like(e_ref)
    row = iota((16, 256), 0)
    col = iota((16, 256), 1)
    y = row % 8
    own = (row // 8) == (col // LANE)
    spot = col % LANE - 64 * (y % 2) - y // 2

    @pl.loop(0, SLOTS)
    def _(s):
        place = jnp.where(s < live_count, slots_ref[0, s], 4096)
        tile = one_hot(own & (spot == 4 * place))
        for j in range(4):
            e_ref[pl.ds(pl.multiple_of(64 * s + 16 * j, 16), 16), 256 * j : 256 * j + 256] = tile


def live_lanes(slots_ref, live_count):
    spot = (iota((8, LANE), 1) % 64) // 4

    def step(s, total):
        place = jnp.where(s < live_count, slots_ref[0, s], 4096)
        return total + jnp.where(spot == place, 1.0, 0.0)

    return lax.fori_loop(0, SLOTS, step, jnp.zeros((8, LANE), F32))


def to_grid(blocks, work, e_ref, grid):
    for t in range(8):
        lanes = slice(t * LANE, (t + 1) * LANE)
        for pair in range(4):
            one = blocks[2 * t, :, pair * LANE : (pair + 1) * LANE]
            two = blocks[2 * t + 1, :, pair * LANE : (pair + 1) * LANE]
            work[2 * pair, :, lanes] = jnp.concatenate([one[:, :64], two[:, :64]], axis=1)
            work[2 * pair + 1, :, lanes] = jnp.concatenate([one[:, 64:], two[:, 64:]], axis=1)

    for n in range(4):
        lanes = slice(n * 256, (n + 1) * 256)
        moved = dot(work[...].reshape(8 * C, 1024), e_ref[:, lanes])
        grid[:, :, lanes] = moved.astype(BF16).reshape(8, C, 256)


def to_blocks(grid, e_ref, blocks):
    for n in range(4):
        rows = slice(n * 256, (n + 1) * 256)
        moved = dot_t(grid[...].reshape(8 * C, 1024), e_ref[rows, :])
        moved = moved.astype(BF16).reshape(8, C, 256)
        for pair in range(4):
            for k in range(4):
                low = moved[2 * pair, :, 64 * k : 64 * k + 64]
                high = moved[2 * pair + 1, :, 64 * k : 64 * k + 64]
                blocks[4 * n + k, :, pair * LANE : (pair + 1) * LANE] = jnp.concatenate(
                    [low, high], axis=1
                )


def pack_edges(grid, depth, t_ref, packed):
    edges = dot(grid.reshape(depth * C, grid.shape[2]), t_ref[...]).reshape(depth, C, LANE)
    total = edges[0]
    for z in range(1, depth):
        total = total + pltpu.roll(edges[z], 16 * z, 1)
    packed[...] = total.astype(BF16)


def unpack_edges(received, row, left_ok, right_ok, depth):
    lane = iota((C, LANE), 1) % 16
    left = jnp.where(left_ok, received[2 * row].astype(F32), 0.0)
    right = jnp.where(right_ok, received[2 * row + 1].astype(F32), 0.0)
    both = jnp.where(lane < 8, left, right)
    parts = [both] + [pltpu.roll(both, LANE - 16 * z, 1) for z in range(1, depth)]
    return jnp.stack(parts, axis=0).astype(BF16).reshape(depth * C, LANE)


def widen(grid, sides, received, s_ref, wide, count, depth, place):
    gx, gy = place
    low_ok, high_ok = gx > 0, gx < NX - 1
    left_ok, right_ok = gy > 0, gy < NY - 1

    def put(rows, halo, x, lanes):
        moved = dot(jnp.concatenate([rows, halo], axis=1), s_ref[x]).astype(BF16)
        wide[:, 0:C, lanes] = moved[:, :LANE].reshape(depth, C, LANE)
        wide[:, C : 2 * C, lanes] = rows.reshape(depth, C, LANE)
        wide[:, 2 * C : 3 * C, lanes] = moved[:, LANE:].reshape(depth, C, LANE)

    zero = jnp.zeros((depth * C, LANE), BF16)
    halo = unpack_edges(received, 0, left_ok & low_ok, right_ok & low_ok, depth)
    rows = jnp.where(low_ok, sides[0].reshape(depth * C, LANE), zero)
    put(rows, halo, count - 1, pl.ds(0, LANE))
    halo = unpack_edges(received, 2, left_ok & high_ok, right_ok & high_ok, depth)
    rows = jnp.where(high_ok, sides[1].reshape(depth * C, LANE), zero)
    put(rows, halo, 0, pl.ds((count + 1) * LANE, LANE))
    halo = unpack_edges(received, 1, left_ok, right_ok, depth)

    for x in range(count):
        rows = grid[:, :, x * LANE : (x + 1) * LANE].reshape(depth * C, LANE)
        put(rows, halo, x, pl.ds((x + 1) * LANE, LANE))


def coarse_halos(received, place):
    gx, gy = place
    left_ok, right_ok = gy > 0, gy < NY - 1
    low_ok, high_ok = gx > 0, gx < NX - 1
    return (
        unpack_edges(received, 0, left_ok & low_ok, right_ok & low_ok, 4),
        unpack_edges(received, 1, left_ok, right_ok, 4),
        unpack_edges(received, 2, left_ok & high_ok, right_ok & high_ok, 4),
    )


def widen_coarse(grid, sides, received, s_ref, wide, place):
    gx = place[0]
    halos = coarse_halos(received, place)
    zero = jnp.zeros((4 * C, LANE), BF16)
    for column in range(8):
        if column < 2:
            lanes = slice(column * LANE, (column + 1) * LANE)
            rows = jnp.where(gx > 0, sides[0, :, :, lanes].reshape(4 * C, LANE), zero)
            halo, x = halos[0], column + 2
        elif column < 6:
            x = column - 2
            rows = grid[:, :, x * LANE : (x + 1) * LANE].reshape(4 * C, LANE)
            halo = halos[1]
        else:
            x = column - 6
            lanes = slice(x * LANE, (x + 1) * LANE)
            rows = jnp.where(gx < NX - 1, sides[1, :, :, lanes].reshape(4 * C, LANE), zero)
            halo = halos[2]
        moved = dot(jnp.concatenate([rows, halo], axis=1), s_ref[x]).astype(BF16)
        for t in range(3):
            part = moved[:, t * LANE : (t + 1) * LANE].reshape(4, C, LANE)
            wide[:, t * C : (t + 1) * C, column * LANE : (column + 1) * LANE] = part


def extend_grect(grect, sides, received, s_ref, wide, place):
    gx = place[0]
    halos = coarse_halos(received, place)
    zero = jnp.zeros((4 * C, LANE), F32)
    for column in range(6):
        if column == 0:
            rows = jnp.where(gx > 0, sides[0].reshape(4 * C, LANE).astype(F32), zero)
            halo, x = halos[0], 3
        elif column < 5:
            x = column - 1
            rows = grect[:, :, x * LANE : (x + 1) * LANE].reshape(4 * C, LANE)
            halo = halos[1]
        else:
            rows = jnp.where(gx < NX - 1, sides[1].reshape(4 * C, LANE).astype(F32), zero)
            halo, x = halos[2], 0
        total = rows + dot(halo, s_ref[x, LANE:, LANE : 2 * LANE])
        wide[:, :, column * LANE : (column + 1) * LANE] = total.reshape(4, C, LANE)


def roll_columns(grid, r_ref, wide):
    for column in range(6):
        lanes = slice(column * LANE, (column + 1) * LANE)
        rows = grid[:, :, lanes]
        moved = dot(rows.reshape(4 * C, LANE), r_ref[...]).astype(BF16)
        wide[:, 0:C, lanes] = moved[:, :LANE].reshape(4, C, LANE)
        wide[:, C : 2 * C, lanes] = rows
        wide[:, 2 * C : 3 * C, lanes] = moved[:, LANE:].reshape(4, C, LANE)


def window(wide, z, first, width):
    return jnp.concatenate(
        [wide[z, :, first + dx * LANE : first + dx * LANE + width] for dx in range(3)], axis=0
    )


def convolve(wide, weight, total, depth, width):
    total[...] = jnp.zeros_like(total)
    for z in range(depth):
        for first in range(0, width, 256):
            piece = dot(weight[...], window(wide, z, first, 256)).reshape(3, C, 256)
            lanes = slice(first, first + 256)
            total[z : z + 3, :, lanes] = total[z : z + 3, :, lanes] + piece


def kernel_terms(grad, wide, total, depth, width, start):
    ahead = [grad[z : z + 3].reshape(3 * C, width) for z in range(depth)]
    pieces = [window(wide, z, start, width) for z in range(depth)]
    total[...] = dot_t(jnp.concatenate(ahead, axis=1), jnp.concatenate(pieces, axis=1))


def quarters(grid, wz):
    columns = []
    for a in range(2):
        for b in range(2):
            columns.append(
                jnp.concatenate(
                    [
                        grid[2 * wz + a, :, (2 * wx + b) * LANE : (2 * wx + b + 1) * LANE]
                        for wx in range(4)
                    ],
                    axis=1,
                )
            )
    return jnp.concatenate(columns, axis=0)


def tile_lanes(mask, rows, width):
    return jnp.broadcast_to(jnp.concatenate([mask] * (width // LANE), axis=1)[0:1], (rows, width))


def roll_half(value):
    parts = [
        pltpu.roll(value[:, k * LANE : (k + 1) * LANE], 64, 1) for k in range(value.shape[1] // LANE)
    ]
    return jnp.concatenate(parts, axis=1)


def kernel_rows(weight, stack, eye, forward, backward):
    for dz in range(3):
        for k in range(9):
            block = weight[9 * dz + k]
            forward[(2 - dz) * C : (3 - dz) * C, k * C : (k + 1) * C] = block
            stack[(8 - k) * C : (9 - k) * C, :] = block
        backward[dz * C : (dz + 1) * C, :] = dot_t(eye[0:C, 0:C], stack[...]).astype(BF16)


def step_rows(down, up, stage, eye, ddn, dga, uup, ugr):
    for o in range(C):
        stage[8 * o : 8 * o + 8, 0:C] = down[o].astype(F32)
    for k in range(4):
        for e in range(2):
            q = 2 * k + e
            block = stage[pl.ds(q, C, stride=8), :].astype(BF16)[:, 0:C]
            ddn[e * C : (e + 1) * C, k * C : (k + 1) * C] = block
            uup[k * C : (k + 1) * C, e * C : (e + 1) * C] = up[q]
    dga[...] = dot_t(eye[...], ddn[...]).astype(BF16)
    ugr[...] = dot_t(eye[0 : 2 * C, 0 : 2 * C], uup[...]).astype(BF16)


def slope(value):
    sigma = jax.nn.sigmoid(value)
    return sigma * (1.0 + value * (1.0 - sigma))


def section(
    slots_ref,
    count_ref,
    feat_hbm,
    cot_hbm,
    fine_hbm,
    down_hbm,
    coarse_hbm,
    up_hbm,
    blocks_out,
    blocks_ig,
    sums_a,
    sums_b,
    feat,
    cot_in,
    fine_w,
    down_w,
    coarse_w,
    up_w,
    stage,
    stack,
    eye,
    wf,
    wfb,
    wc,
    wcb,
    ddn,
    dga,
    uup,
    ugr,
    work,
    places,
    shift_f,
    shift_c,
    roll_c,
    edge_f,
    edge_c,
    fine,
    cot,
    fine3,
    hidden,
    act,
    low,
    low3,
    coarse,
    coarse2,
    grect,
    grect_low,
    grect_wide,
    rect2,
    gcoarse,
    gcoarse_own,
    gcoarse3,
    gdown2,
    ghid,
    ghid3,
    result,
    term_f,
    term_c,
    packed,
    sides_f,
    sides_c,
    sides_g,
    edges_in,
    grads_a,
    first_in_a,
    chunk_a,
    second_in_a,
    grads_b,
    first_in_b,
    chunk_b,
    second_in_b,
    local_sem,
    send_sem,
    recv_sem,
    sum_send,
    sum_recv,
):
    gx = lax.axis_index("gx")
    gy = lax.axis_index("gy")
    here = (gx, gy)

    load_feat = pltpu.make_async_copy(feat_hbm, feat, local_sem.at[5])
    load_feat.start()
    loads = [
        pltpu.make_async_copy(source, target, local_sem.at[k])
        for k, (source, target) in enumerate(
            (
                (fine_hbm, fine_w),
                (down_hbm, down_w),
                (coarse_hbm, coarse_w),
                (up_hbm, up_w),
                (cot_hbm, cot_in),
            )
        )
    ]
    for load in loads:
        load.start()

    barrier = pltpu.get_barrier_semaphore()

    @pl.loop(1, NX)
    def _(d):
        pl.semaphore_signal(
            barrier, inc=1, device_id=(lax.rem(gx + d, NX), gy), device_id_type=MESH
        )
        pl.semaphore_signal(
            barrier, inc=1, device_id=(gx, lax.rem(gy + d, NY)), device_id_type=MESH
        )

    for dx in (1, NX - 1):
        for dy in (1, NY - 1):
            pl.semaphore_signal(
                barrier,
                inc=1,
                device_id=(lax.rem(gx + dx, NX), lax.rem(gy + dy, NY)),
                device_id_type=MESH,
            )

    live_count = count_ref[0, 0]
    build_places(places, slots_ref, live_count)
    build_edges(edge_f, edge_c)
    live = live_lanes(slots_ref, live_count)
    half_live = jnp.where(iota((8, LANE), 1) < 64, live, 0.0)
    lower = jnp.where(iota((8, LANE), 1) < 64, 1.0, 0.0)

    def exchange(step, source, length, width, sides):
        copies = []
        for side in range(2):
            first = length - width if side == 0 else 0
            shift = 1 if side == 0 else NX - 1
            copies.append(
                pltpu.make_async_remote_copy(
                    src_ref=source.at[:, :, pl.ds(first, width)],
                    dst_ref=sides.at[side],
                    send_sem=send_sem.at[step, side],
                    recv_sem=recv_sem.at[step, side],
                    device_id=(lax.rem(gx + shift, NX), gy),
                    device_id_type=MESH,
                )
            )
        for row in range(3):
            for side in range(2):
                copies.append(
                    pltpu.make_async_remote_copy(
                        src_ref=packed.at[step],
                        dst_ref=edges_in.at[step, 2 * row + side],
                        send_sem=send_sem.at[step, 2 + 2 * row + side],
                        recv_sem=recv_sem.at[step, 2 + 2 * row + side],
                        device_id=(
                            lax.rem(gx + NX + 1 - row, NX),
                            lax.rem(gy + (1 if side == 0 else NY - 1), NY),
                        ),
                        device_id_type=MESH,
                    )
                )
        for copy in copies:
            copy.start()
        return copies

    def reduction(grads, first_in, chunk, second_in, sums, part):
        rows = chunk.shape[1]

        def chunk_rows(index):
            return pl.ds(pl.multiple_of(index * rows, rows), rows)

        def first(d):
            peer = lax.rem(gy + d, NY)
            return pltpu.make_async_remote_copy(
                src_ref=grads.at[chunk_rows(peer)],
                dst_ref=first_in.at[d],
                send_sem=sum_send.at[part, 0, d],
                recv_sem=sum_recv.at[part, 0, d],
                device_id=(gx, peer),
                device_id_type=MESH,
            )

        def second(d):
            return pltpu.make_async_remote_copy(
                src_ref=chunk.at[0],
                dst_ref=second_in.at[d],
                send_sem=sum_send.at[part, 1, d],
                recv_sem=sum_recv.at[part, 1, d],
                device_id=(lax.rem(gx + d, NX), gy),
                device_id_type=MESH,
            )

        def third(d):
            return pltpu.make_async_remote_copy(
                src_ref=chunk.at[1],
                dst_ref=sums.at[chunk_rows(gy)],
                send_sem=sum_send.at[part, 2, d],
                recv_sem=sum_recv.at[part, 2, d],
                device_id=(gx, lax.rem(gy + d, NY)),
                device_id_type=MESH,
            )

        def start_first():
            start_all(first)

        def start_second():
            wait_all(first)
            own = grads[chunk_rows(gy), :].astype(F32)
            for d in range(1, NY):
                own = own + first_in[d].astype(F32)
            chunk[0] = own.astype(BF16)
            start_all(second)
            return own

        def start_third(own):
            wait_all(second)
            for d in range(1, NX):
                own = own + second_in[d].astype(F32)
            chunk[1] = own.astype(BF16)
            start_all(third)
            sums[chunk_rows(gy), :] = chunk[1]

        def finish():
            wait_all(third)

        return start_first, start_second, start_third, finish

    def start_all(copy):
        @pl.loop(1, NX)
        def _(d):
            copy(d).start()

    def wait_all(copy):
        @pl.loop(1, NX)
        def _(d):
            copy(d).wait()

    def put_rows(grads, term):
        for k in range(3):
            grads[3 * C * k : 3 * C * (k + 1), :] = term[:, k * LANE : (k + 1) * LANE].astype(BF16)
        grads[9 * C : 9 * C + 80, 0:C] = term[0:80, 3 * LANE :].astype(BF16)
        grads[9 * C : 9 * C + 64, 64 : 64 + C] = term[80:144, 3 * LANE :].astype(BF16)

    load_feat.wait()
    to_grid(feat, work, places, fine)
    pack_edges(fine[...], 8, edge_f, packed.at[0])
    pl.semaphore_wait(barrier, 2 * (NX - 1) + 4)
    copies = exchange(0, fine, 1024, LANE, sides_f.at[0])

    for load in loads:
        load.wait()
    build_shift_coarse(shift_c)
    to_grid(cot_in, work, places, cot)
    eye[...] = one_hot(iota((4 * C, 4 * C), 0) == iota((4 * C, 4 * C), 1))
    stage[...] = jnp.zeros_like(stage)
    step_rows(down_w, up_w, stage, eye, ddn, dga, uup, ugr)
    lower_mask = tile_lanes(lower, C, 512)
    for wz in range(4):
        both = dot(ugr[...], quarters(cot, wz))
        value = (both[:C] + roll_half(both[C:])) * lower_mask
        grect[wz] = value
        grect_low[wz] = value.astype(BF16)
    pack_edges(grect_low[...], 4, edge_c, packed.at[2])
    grect_copies = exchange(2, grect_low, 512, LANE, sides_g)
    build_shift_fine(shift_f)
    build_roll(roll_c)
    kernel_rows(fine_w, stack, eye, wf, wfb)
    kernel_rows(coarse_w, stack, eye, wc, wcb)
    grads_a[...] = jnp.zeros_like(grads_a)
    grads_b[...] = jnp.zeros_like(grads_b)
    gcoarse_own[...] = jnp.zeros_like(gcoarse_own)

    for copy in copies:
        copy.wait()
    widen(fine, sides_f.at[0], edges_in.at[0], shift_f, fine3, 8, 8, here)
    convolve(fine3, wf, hidden, 8, 1024)

    live_fine = tile_lanes(live, C, 1024)
    for z in range(8):
        value = hidden[z + 1] * live_fine
        hidden[z + 1] = value
        act[z] = (value * jax.nn.sigmoid(value)).astype(BF16)

    for wz in range(4):
        both = dot(ddn[...], quarters(act, wz))
        low[wz] = ((both[:C] + roll_half(both[C:])) * lower_mask).astype(BF16)

    pack_edges(low[...], 4, edge_c, packed.at[1])
    copies = exchange(1, low, 512, 2 * LANE, sides_c)
    for copy in grect_copies:
        copy.wait()
    extend_grect(grect, sides_g, edges_in.at[2], shift_c, grect_wide, here)
    for copy in copies:
        copy.wait()
    widen_coarse(low, sides_c, edges_in.at[1], shift_c, low3, here)
    convolve(low3, wc, coarse, 4, 768)

    for wz in range(4):
        value = coarse[wz + 1]
        grad = grect_wide[wz] * slope(value)
        gcoarse[wz] = grad.astype(BF16)
        gcoarse_own[wz + 1] = (grad[:, LANE : 5 * LANE] * lower_mask).astype(BF16)
        value = value[:, LANE : 5 * LANE]
        rect = value * jax.nn.sigmoid(value) * lower_mask
        rect2[wz, 0:C] = rect.astype(BF16)
        rect2[wz, C : 2 * C] = roll_half(rect).astype(BF16)

    roll_columns(gcoarse, roll_c, gcoarse3)
    convolve(gcoarse3, wcb, coarse2, 4, 512)

    live_coarse = tile_lanes(half_live, C, 512)
    ghid[0] = jnp.zeros((C, 1024), BF16)
    ghid[9] = jnp.zeros((C, 1024), BF16)
    for wz in range(4):
        value = coarse2[wz + 1] * live_coarse
        gdown2[wz, 0:C] = value.astype(BF16)
        gdown2[wz, C : 2 * C] = roll_half(value).astype(BF16)
        back = dot(dga[...], gdown2[wz])
        for a in range(2):
            for b in range(2):
                k = 2 * a + b
                for wx in range(4):
                    lanes = pl.ds((2 * wx + b) * LANE, LANE)
                    piece = back[k * C : (k + 1) * C, wx * LANE : (wx + 1) * LANE]
                    ghid[2 * wz + a + 1, :, lanes] = (
                        cot[2 * wz + a, :, lanes].astype(F32)
                        + piece * slope(hidden[2 * wz + a + 1, :, lanes])
                    ).astype(BF16)

    pack_edges(ghid[1:9], 8, edge_f, packed.at[3])
    copies = exchange(3, ghid.at[pl.ds(1, 8)], 1024, LANE, sides_f.at[1])

    first_a, second_a, third_a, finish_a = reduction(
        grads_a, first_in_a, chunk_a, second_in_a, sums_a, 0
    )
    first_b, second_b, third_b, finish_b = reduction(
        grads_b, first_in_b, chunk_b, second_in_b, sums_b, 1
    )
    kernel_terms(gcoarse_own, low3, term_c, 4, 512, LANE)
    total_u = jnp.zeros((4 * C, 2 * C), F32)
    total_d = jnp.zeros((2 * C, 4 * C), F32)
    for wz in range(4):
        total_u = total_u + dot_t(quarters(cot, wz), rect2[wz])
        total_d = total_d + dot_t(gdown2[wz], quarters(act, wz))
    put_rows(grads_b, term_c)
    grads_b[512:704, 0 : 2 * C] = total_u.astype(BF16)
    grads_b[704:800, :] = total_d[:, 0:LANE].astype(BF16)
    grads_b[800:896, 0:64] = total_d[:, LANE:192].astype(BF16)
    first_b()
    kernel_terms(ghid, fine3, term_f, 8, 1024, 0)
    put_rows(grads_a, term_f)
    first_a()

    for wz in range(4):
        upward = dot(uup[...], rect2[wz])
        for a in range(2):
            for b in range(2):
                k = 2 * a + b
                for wx in range(4):
                    lanes = pl.ds((2 * wx + b) * LANE, LANE)
                    piece = upward[k * C : (k + 1) * C, wx * LANE : (wx + 1) * LANE]
                    result[2 * wz + a, :, lanes] = (
                        hidden[2 * wz + a + 1, :, lanes] + piece
                    ).astype(BF16)
    to_blocks(result, places, blocks_out)
    own_b = second_b()
    own_a = second_a()

    for copy in copies:
        copy.wait()
    widen(ghid.at[pl.ds(1, 8)], sides_f.at[1], edges_in.at[3], shift_f, ghid3, 8, 8, here)
    convolve(ghid3, wfb, hidden, 8, 1024)
    for z in range(8):
        result[z] = hidden[z + 1].astype(BF16)
    to_blocks(result, places, blocks_ig)

    third_b(own_b)
    third_a(own_a)
    finish_b()
    finish_a()


def unpack(sums_a, sums_b, out_in, ig_in, out_hbm, ig_hbm, gf, gd, gc, gu, stage, sem):
    copies = [
        pltpu.make_async_copy(out_in, out_hbm, sem.at[0]),
        pltpu.make_async_copy(ig_in, ig_hbm, sem.at[1]),
    ]
    for copy in copies:
        copy.start()
    scale = 1.0 / math.sqrt(SLOTS * 512 * NX * NY)

    for sums, target in ((sums_a, gf), (sums_b, gc)):
        tail = sums[9 * C : 9 * C + 80, :]
        tail = jnp.concatenate([tail[:, 0:64], tail[0:64, 64:LANE]], axis=0)
        rows = jnp.concatenate(
            [sums[3 * C * k : 3 * C * (k + 1), :] for k in range(3)] + [tail], axis=1
        )
        rows = rows.astype(F32) * scale
        for dz in range(3):
            for k in range(9):
                block = rows[(2 - dz) * C : (3 - dz) * C, k * C : (k + 1) * C]
                target[9 * dz + k] = block
    tail = sums_b[800:896, :]
    rows = jnp.concatenate([sums_b[704:800, :], tail, tail], axis=1)
    rows = rows.astype(F32) * scale
    for k in range(4):
        for e in range(2):
            gu[2 * k + e] = (
                sums_b[512 + k * C : 512 + (k + 1) * C, e * C : (e + 1) * C].astype(F32) * scale
            )
            block = rows[e * C : (e + 1) * C, k * C : k * C + LANE]
            stage[pl.ds(2 * k + e, C, stride=8), :] = block
    for o in range(C):
        gd[o] = stage[8 * o : 8 * o + 8, 0:C]
    for copy in copies:
        copy.wait()


def on_device(
    features, block_slots, block_count, cotangent, fine_weight, down_weight, coarse_weight, up_weight
):
    vmem = pl.BlockSpec(memory_space=pltpu.VMEM)
    smem = pl.BlockSpec(memory_space=pltpu.SMEM)
    hbm = pl.BlockSpec(memory_space=pltpu.HBM)
    blocks = (SLOTS, C, 512)
    kernel_shape = (27, C, C)
    block_shape = jax.ShapeDtypeStruct(blocks, BF16)
    out, ig, sums_a, sums_b = pl.pallas_call(
        section,
        out_shape=(
            block_shape,
            block_shape,
            jax.ShapeDtypeStruct((ROWS_A, LANE), BF16),
            jax.ShapeDtypeStruct((ROWS_B, LANE), BF16),
        ),
        in_specs=[smem, smem] + [hbm] * 6,
        out_specs=(vmem, vmem, vmem, vmem),
        scratch_shapes=[
            pltpu.VMEM(blocks, BF16),
            pltpu.VMEM(blocks, BF16),
            pltpu.VMEM(kernel_shape, BF16),
            pltpu.VMEM((C, 8, C), BF16),
            pltpu.VMEM(kernel_shape, BF16),
            pltpu.VMEM((8, C, C), BF16),
            pltpu.VMEM((8 * C, LANE), F32),
            pltpu.VMEM((9 * C, C), BF16),
            pltpu.VMEM((4 * C, 4 * C), BF16),
            pltpu.VMEM((3 * C, 9 * C), BF16),
            pltpu.VMEM((3 * C, 9 * C), BF16),
            pltpu.VMEM((3 * C, 9 * C), BF16),
            pltpu.VMEM((3 * C, 9 * C), BF16),
            pltpu.VMEM((2 * C, 4 * C), BF16),
            pltpu.VMEM((4 * C, 2 * C), BF16),
            pltpu.VMEM((4 * C, 2 * C), BF16),
            pltpu.VMEM((2 * C, 4 * C), BF16),
            pltpu.VMEM((8, C, 1024), BF16),
            pltpu.VMEM((1024, 1024), BF16),
            pltpu.VMEM((8, 256, 256), BF16),
            pltpu.VMEM((4, 256, 384), BF16),
            pltpu.VMEM((LANE, 256), BF16),
            pltpu.VMEM((1024, LANE), BF16),
            pltpu.VMEM((512, LANE), BF16),
            pltpu.VMEM((8, C, 1024), BF16),
            pltpu.VMEM((8, C, 1024), BF16),
            pltpu.VMEM((8, 3 * C, 1280), BF16),
            pltpu.VMEM((10, C, 1024), F32),
            pltpu.VMEM((8, C, 1024), BF16),
            pltpu.VMEM((4, C, 512), BF16),
            pltpu.VMEM((4, 3 * C, 1024), BF16),
            pltpu.VMEM((6, C, 768), F32),
            pltpu.VMEM((6, C, 512), F32),
            pltpu.VMEM((4, C, 512), F32),
            pltpu.VMEM((4, C, 512), BF16),
            pltpu.VMEM((4, C, 768), F32),
            pltpu.VMEM((4, 2 * C, 512), BF16),
            pltpu.VMEM((4, C, 768), BF16),
            pltpu.VMEM((6, C, 512), BF16),
            pltpu.VMEM((4, 3 * C, 768), BF16),
            pltpu.VMEM((4, 2 * C, 512), BF16),
            pltpu.VMEM((10, C, 1024), BF16),
            pltpu.VMEM((8, 3 * C, 1280), BF16),
            pltpu.VMEM((8, C, 1024), BF16),
            pltpu.VMEM((3 * C, 9 * C), F32),
            pltpu.VMEM((3 * C, 9 * C), F32),
            pltpu.VMEM((4, C, LANE), BF16),
            pltpu.VMEM((2, 2, 8, C, LANE), BF16),
            pltpu.VMEM((2, 4, C, 2 * LANE), BF16),
            pltpu.VMEM((2, 4, C, LANE), BF16),
            pltpu.VMEM((4, 6, C, LANE), BF16),
            pltpu.VMEM((ROWS_A, LANE), BF16),
            pltpu.VMEM((NY, ROWS_A // NY, LANE), BF16),
            pltpu.VMEM((2, ROWS_A // NY, LANE), BF16),
            pltpu.VMEM((NX, ROWS_A // NY, LANE), BF16),
            pltpu.VMEM((ROWS_B, LANE), BF16),
            pltpu.VMEM((NY, ROWS_B // NY, LANE), BF16),
            pltpu.VMEM((2, ROWS_B // NY, LANE), BF16),
            pltpu.VMEM((NX, ROWS_B // NY, LANE), BF16),
            pltpu.SemaphoreType.DMA((6,)),
            pltpu.SemaphoreType.DMA((4, 8)),
            pltpu.SemaphoreType.DMA((4, 8)),
            pltpu.SemaphoreType.DMA((2, 3, NX)),
            pltpu.SemaphoreType.DMA((2, 3, NX)),
        ],
        compiler_params=pltpu.CompilerParams(
            collective_id=0, has_side_effects=True, vmem_limit_bytes=50 * 1024 * 1024
        ),
        name="section",
    )(
        block_slots.reshape(1, SLOTS),
        block_count.reshape(1, 1),
        *(
            pltpu.with_memory_space_constraint(value, pltpu.HBM)
            for value in (
                features.reshape(blocks),
                cotangent.reshape(blocks),
                fine_weight.transpose(1, 0, 2),
                down_weight,
                coarse_weight.transpose(1, 0, 2),
                up_weight,
            )
        ),
    )
    out, ig, gf, gd, gc, gu = pl.pallas_call(
        unpack,
        out_shape=(
            block_shape,
            block_shape,
            jax.ShapeDtypeStruct(kernel_shape, F32),
            jax.ShapeDtypeStruct((C, 8, C), F32),
            jax.ShapeDtypeStruct(kernel_shape, F32),
            jax.ShapeDtypeStruct((8, C, C), F32),
        ),
        in_specs=[vmem, vmem, vmem, vmem],
        out_specs=(hbm, hbm, vmem, vmem, vmem, vmem),
        scratch_shapes=[pltpu.VMEM((8 * C, LANE), F32), pltpu.SemaphoreType.DMA((2,))],
        compiler_params=pltpu.CompilerParams(vmem_limit_bytes=8 * 1024 * 1024),
        name="unpack",
    )(sums_a, sums_b, out, ig)
    shape_out = (1, 1) + blocks
    gf, gc = gf.transpose(1, 0, 2), gc.transpose(1, 0, 2)
    return out.reshape(shape_out), ig.reshape(shape_out), gf, gd, gc, gu


def solution(mesh):
    split = P("gx", "gy", None, None, None)
    return jax.shard_map(
        on_device,
        mesh=mesh,
        in_specs=(split, P("gx", "gy", None), P("gx", "gy"), split, P(), P(), P(), P()),
        out_specs=(split, split, P(), P(), P(), P()),
        check_vma=False,
    )
```

```python
import math

import jax
import jax.numpy as jnp
from jax import lax
from jax.experimental import pallas as pl
from jax.experimental.pallas import tpu as pltpu
from jax.sharding import PartitionSpec as P

C = 48
SLOTS = 16
LANE = 128
NX = 16
NY = 16
ROWS_A = 512
ROWS_B = 768
F32 = jnp.float32
BF16 = jnp.bfloat16
MESH = pl.DeviceIdType.MESH


def dot(a, b):
    return jnp.dot(a, b, preferred_element_type=F32)


def dot_t(a, b):
    return lax.dot_general(a, b, (((1,), (1,)), ((), ())), preferred_element_type=F32)


def iota(shape, dim):
    return lax.broadcasted_iota(jnp.int32, shape, dim)


def one_hot(cond):
    return jnp.where(cond, 1.0, 0.0).astype(BF16)


def build_shift_fine(s_ref):
    row = iota((256, 256), 0)
    col = iota((256, 256), 1)
    lane = col % LANE
    right = col >= LANE
    before = jnp.where(lane < 64, lane + 63, lane - 64)
    after = jnp.where(lane < 64, lane + 64, lane - 63)
    before = jnp.where(lane == 0, -1, before)
    after = jnp.where(lane == 127, -1, after)
    source = jnp.where(right, after, before)
    place = jnp.where(lane == jnp.where(right, 127, 0), jnp.where(right, LANE + 8, LANE), -512)

    @pl.loop(0, 8)
    def _(x):
        s_ref[x] = one_hot((row == source) | (row == place + x))


def coarse_edge(group):
    return jnp.where(
        group == 0, 63, jnp.where(group == 1, 62, jnp.where(group == 2, 0, jnp.where(group == 3, 1, -1)))
    )


def build_shift_coarse(s_ref):
    row = iota((256, 384), 0)
    col = iota((256, 384), 1)
    source = (col % LANE + col // LANE + LANE - 1) % LANE
    halo = row - LANE
    spot = jnp.where(
        halo < 4, 127, jnp.where(halo < 8, 126, jnp.where(halo < 12, 64, jnp.where(halo < 16, 65, -1)))
    )
    own = (row < 64) & (row == source)
    other = (halo >= 0) & (spot == source)

    @pl.loop(0, 4)
    def _(x):
        s_ref[x] = one_hot(own | (other & (halo % 4 == x)))


def build_roll(r_ref):
    row = iota((LANE, 256), 0)
    col = iota((LANE, 256), 1)
    r_ref[...] = one_hot(row == (col % LANE + 2 * (col // LANE) + LANE - 1) % LANE)


def build_edges(fine_ref, coarse_ref):
    row = iota((1024, LANE), 0)
    col = iota((1024, LANE), 1)
    lane = row % LANE
    x = row // LANE
    fine_ref[...] = one_hot(((lane == 127) & (col == x)) | ((lane == 0) & (col == x + 8)))
    row = iota((512, LANE), 0)
    col = iota((512, LANE), 1)
    coarse_ref[...] = one_hot((row % LANE == coarse_edge(col // 4)) & (row // LANE == col % 4))


def build_places(e_ref, slots_ref, live_count):
    e_ref[...] = jnp.zeros_like(e_ref)
    row = iota((16, 256), 0)
    col = iota((16, 256), 1)
    y = row % 8
    own = (row // 8) == (col // LANE)
    spot = col % LANE - 64 * (y % 2) - y // 2

    @pl.loop(0, SLOTS)
    def _(s):
        place = jnp.where(s < live_count, slots_ref[0, s], 4096)
        tile = one_hot(own & (spot == 4 * place))
        for j in range(4):
            e_ref[pl.ds(pl.multiple_of(64 * s + 16 * j, 16), 16), 256 * j : 256 * j + 256] = tile


def live_lanes(slots_ref, live_count):
    spot = (iota((8, LANE), 1) % 64) // 4

    def step(s, total):
        place = jnp.where(s < live_count, slots_ref[0, s], 4096)
        return total + jnp.where(spot == place, 1.0, 0.0)

    return lax.fori_loop(0, SLOTS, step, jnp.zeros((8, LANE), F32))


def to_grid(blocks, work, e_ref, grid):
    for t in range(8):
        lanes = slice(t * LANE, (t + 1) * LANE)
        for pair in range(4):
            one = blocks[2 * t, :, pair * LANE : (pair + 1) * LANE]
            two = blocks[2 * t + 1, :, pair * LANE : (pair + 1) * LANE]
            work[2 * pair, :, lanes] = jnp.concatenate([one[:, :64], two[:, :64]], axis=1)
            work[2 * pair + 1, :, lanes] = jnp.concatenate([one[:, 64:], two[:, 64:]], axis=1)

    for n in range(4):
        lanes = slice(n * 256, (n + 1) * 256)
        moved = dot(work[...].reshape(8 * C, 1024), e_ref[:, lanes])
        grid[:, :, lanes] = moved.astype(BF16).reshape(8, C, 256)


def to_blocks(grid, e_ref, blocks):
    for n in range(4):
        rows = slice(n * 256, (n + 1) * 256)
        moved = dot_t(grid[...].reshape(8 * C, 1024), e_ref[rows, :])
        moved = moved.astype(BF16).reshape(8, C, 256)
        for pair in range(4):
            for k in range(4):
                low = moved[2 * pair, :, 64 * k : 64 * k + 64]
                high = moved[2 * pair + 1, :, 64 * k : 64 * k + 64]
                blocks[4 * n + k, :, pair * LANE : (pair + 1) * LANE] = jnp.concatenate(
                    [low, high], axis=1
                )


def pack_edges(grid, depth, t_ref, packed):
    edges = dot(grid.reshape(depth * C, grid.shape[2]), t_ref[...]).reshape(depth, C, LANE)
    total = edges[0]
    for z in range(1, depth):
        total = total + pltpu.roll(edges[z], 16 * z, 1)
    packed[...] = total.astype(BF16)


def unpack_edges(received, row, left_ok, right_ok, depth):
    lane = iota((C, LANE), 1) % 16
    left = jnp.where(left_ok, received[2 * row].astype(F32), 0.0)
    right = jnp.where(right_ok, received[2 * row + 1].astype(F32), 0.0)
    both = jnp.where(lane < 8, left, right)
    parts = [both] + [pltpu.roll(both, LANE - 16 * z, 1) for z in range(1, depth)]
    return jnp.stack(parts, axis=0).astype(BF16).reshape(depth * C, LANE)


def widen(grid, sides, received, s_ref, wide, count, depth, place):
    gx, gy = place
    low_ok, high_ok = gx > 0, gx < NX - 1
    left_ok, right_ok = gy > 0, gy < NY - 1

    def put(rows, halo, x, lanes):
        moved = dot(jnp.concatenate([rows, halo], axis=1), s_ref[x]).astype(BF16)
        wide[:, 0:C, lanes] = moved[:, :LANE].reshape(depth, C, LANE)
        wide[:, C : 2 * C, lanes] = rows.reshape(depth, C, LANE)
        wide[:, 2 * C : 3 * C, lanes] = moved[:, LANE:].reshape(depth, C, LANE)

    zero = jnp.zeros((depth * C, LANE), BF16)
    halo = unpack_edges(received, 0, left_ok & low_ok, right_ok & low_ok, depth)
    rows = jnp.where(low_ok, sides[0].reshape(depth * C, LANE), zero)
    put(rows, halo, count - 1, pl.ds(0, LANE))
    halo = unpack_edges(received, 2, left_ok & high_ok, right_ok & high_ok, depth)
    rows = jnp.where(high_ok, sides[1].reshape(depth * C, LANE), zero)
    put(rows, halo, 0, pl.ds((count + 1) * LANE, LANE))
    halo = unpack_edges(received, 1, left_ok, right_ok, depth)

    for x in range(count):
        rows = grid[:, :, x * LANE : (x + 1) * LANE].reshape(depth * C, LANE)
        put(rows, halo, x, pl.ds((x + 1) * LANE, LANE))


def coarse_halos(received, place):
    gx, gy = place
    left_ok, right_ok = gy > 0, gy < NY - 1
    low_ok, high_ok = gx > 0, gx < NX - 1
    return (
        unpack_edges(received, 0, left_ok & low_ok, right_ok & low_ok, 4),
        unpack_edges(received, 1, left_ok, right_ok, 4),
        unpack_edges(received, 2, left_ok & high_ok, right_ok & high_ok, 4),
    )


def widen_coarse(grid, sides, received, s_ref, wide, place):
    gx = place[0]
    halos = coarse_halos(received, place)
    zero = jnp.zeros((4 * C, LANE), BF16)
    for column in range(8):
        if column < 2:
            lanes = slice(column * LANE, (column + 1) * LANE)
            rows = jnp.where(gx > 0, sides[0, :, :, lanes].reshape(4 * C, LANE), zero)
            halo, x = halos[0], column + 2
        elif column < 6:
            x = column - 2
            rows = grid[:, :, x * LANE : (x + 1) * LANE].reshape(4 * C, LANE)
            halo = halos[1]
        else:
            x = column - 6
            lanes = slice(x * LANE, (x + 1) * LANE)
            rows = jnp.where(gx < NX - 1, sides[1, :, :, lanes].reshape(4 * C, LANE), zero)
            halo = halos[2]
        moved = dot(jnp.concatenate([rows, halo], axis=1), s_ref[x]).astype(BF16)
        for t in range(3):
            part = moved[:, t * LANE : (t + 1) * LANE].reshape(4, C, LANE)
            wide[:, t * C : (t + 1) * C, column * LANE : (column + 1) * LANE] = part


def extend_grect(grect, sides, received, s_ref, wide, place):
    gx = place[0]
    halos = coarse_halos(received, place)
    zero = jnp.zeros((4 * C, LANE), F32)
    for column in range(6):
        if column == 0:
            rows = jnp.where(gx > 0, sides[0].reshape(4 * C, LANE).astype(F32), zero)
            halo, x = halos[0], 3
        elif column < 5:
            x = column - 1
            rows = grect[:, :, x * LANE : (x + 1) * LANE].reshape(4 * C, LANE)
            halo = halos[1]
        else:
            rows = jnp.where(gx < NX - 1, sides[1].reshape(4 * C, LANE).astype(F32), zero)
            halo, x = halos[2], 0
        total = rows + dot(halo, s_ref[x, LANE:, LANE : 2 * LANE])
        wide[:, :, column * LANE : (column + 1) * LANE] = total.reshape(4, C, LANE)


def roll_columns(grid, r_ref, wide):
    for column in range(6):
        lanes = slice(column * LANE, (column + 1) * LANE)
        rows = grid[:, :, lanes]
        moved = dot(rows.reshape(4 * C, LANE), r_ref[...]).astype(BF16)
        wide[:, 0:C, lanes] = moved[:, :LANE].reshape(4, C, LANE)
        wide[:, C : 2 * C, lanes] = rows
        wide[:, 2 * C : 3 * C, lanes] = moved[:, LANE:].reshape(4, C, LANE)


def window(wide, z, first, width):
    return jnp.concatenate(
        [wide[z, :, first + dx * LANE : first + dx * LANE + width] for dx in range(3)], axis=0
    )


def convolve(wide, weight, total, depth, width):
    total[...] = jnp.zeros_like(total)
    for z in range(depth):
        for first in range(0, width, 256):
            piece = dot(weight[...], window(wide, z, first, 256)).reshape(3, C, 256)
            lanes = slice(first, first + 256)
            total[z : z + 3, :, lanes] = total[z : z + 3, :, lanes] + piece


def kernel_terms(grad, wide, total, depth, width, start):
    ahead = [grad[z : z + 3].reshape(3 * C, width) for z in range(depth)]
    pieces = [window(wide, z, start, width) for z in range(depth)]
    total[...] = dot_t(jnp.concatenate(ahead, axis=1), jnp.concatenate(pieces, axis=1))


def quarters(grid, wz):
    columns = []
    for a in range(2):
        for b in range(2):
            columns.append(
                jnp.concatenate(
                    [
                        grid[2 * wz + a, :, (2 * wx + b) * LANE : (2 * wx + b + 1) * LANE]
                        for wx in range(4)
                    ],
                    axis=1,
                )
            )
    return jnp.concatenate(columns, axis=0)


def tile_lanes(mask, rows, width):
    return jnp.broadcast_to(jnp.concatenate([mask] * (width // LANE), axis=1)[0:1], (rows, width))


def roll_half(value):
    parts = [
        pltpu.roll(value[:, k * LANE : (k + 1) * LANE], 64, 1) for k in range(value.shape[1] // LANE)
    ]
    return jnp.concatenate(parts, axis=1)


def kernel_rows(weight, stack, eye, forward, backward):
    for dz in range(3):
        for k in range(9):
            block = weight[9 * dz + k]
            forward[(2 - dz) * C : (3 - dz) * C, k * C : (k + 1) * C] = block
            stack[(8 - k) * C : (9 - k) * C, :] = block
        backward[dz * C : (dz + 1) * C, :] = dot_t(eye[0:C, 0:C], stack[...]).astype(BF16)


def step_rows(down, up, stage, eye, ddn, dga, uup, ugr):
    for o in range(C):
        stage[8 * o : 8 * o + 8, 0:C] = down[o].astype(F32)
    for k in range(4):
        for e in range(2):
            q = 2 * k + e
            block = stage[pl.ds(q, C, stride=8), :].astype(BF16)[:, 0:C]
            ddn[e * C : (e + 1) * C, k * C : (k + 1) * C] = block
            uup[k * C : (k + 1) * C, e * C : (e + 1) * C] = up[q]
    dga[...] = dot_t(eye[...], ddn[...]).astype(BF16)
    ugr[...] = dot_t(eye[0 : 2 * C, 0 : 2 * C], uup[...]).astype(BF16)


def slope(value):
    sigma = jax.nn.sigmoid(value)
    return sigma * (1.0 + value * (1.0 - sigma))


def section(
    slots_ref,
    count_ref,
    feat_hbm,
    cot_hbm,
    fine_hbm,
    down_hbm,
    coarse_hbm,
    up_hbm,
    blocks_out,
    blocks_ig,
    sums_a,
    sums_b,
    feat,
    cot_in,
    fine_w,
    down_w,
    coarse_w,
    up_w,
    stage,
    stack,
    eye,
    wf,
    wfb,
    wc,
    wcb,
    ddn,
    dga,
    uup,
    ugr,
    work,
    places,
    shift_f,
    shift_c,
    roll_c,
    edge_f,
    edge_c,
    fine,
    cot,
    fine3,
    hidden,
    act,
    low,
    low3,
    coarse,
    coarse2,
    grect,
    grect_low,
    grect_wide,
    rect2,
    gcoarse,
    gcoarse_own,
    gcoarse3,
    gdown2,
    ghid,
    ghid3,
    result,
    term_f,
    term_c,
    packed,
    sides_f,
    sides_c,
    sides_g,
    edges_in,
    grads_a,
    first_in_a,
    chunk_a,
    second_in_a,
    grads_b,
    first_in_b,
    chunk_b,
    second_in_b,
    local_sem,
    send_sem,
    recv_sem,
    sum_send,
    sum_recv,
):
    gx = lax.axis_index("gx")
    gy = lax.axis_index("gy")
    here = (gx, gy)

    load_feat = pltpu.make_async_copy(feat_hbm, feat, local_sem.at[5])
    load_feat.start()
    loads = [
        pltpu.make_async_copy(source, target, local_sem.at[k])
        for k, (source, target) in enumerate(
            (
                (fine_hbm, fine_w),
                (down_hbm, down_w),
                (coarse_hbm, coarse_w),
                (up_hbm, up_w),
                (cot_hbm, cot_in),
            )
        )
    ]
    for load in loads:
        load.start()

    barrier = pltpu.get_barrier_semaphore()

    @pl.loop(1, NX)
    def _(d):
        pl.semaphore_signal(
            barrier, inc=1, device_id=(lax.rem(gx + d, NX), gy), device_id_type=MESH
        )
        pl.semaphore_signal(
            barrier, inc=1, device_id=(gx, lax.rem(gy + d, NY)), device_id_type=MESH
        )

    for dx in (1, NX - 1):
        for dy in (1, NY - 1):
            pl.semaphore_signal(
                barrier,
                inc=1,
                device_id=(lax.rem(gx + dx, NX), lax.rem(gy + dy, NY)),
                device_id_type=MESH,
            )

    live_count = count_ref[0, 0]
    build_places(places, slots_ref, live_count)
    build_edges(edge_f, edge_c)
    live = live_lanes(slots_ref, live_count)
    half_live = jnp.where(iota((8, LANE), 1) < 64, live, 0.0)
    lower = jnp.where(iota((8, LANE), 1) < 64, 1.0, 0.0)

    def exchange(step, source, length, width, sides):
        copies = []
        for side in range(2):
            first = length - width if side == 0 else 0
            shift = 1 if side == 0 else NX - 1
            copies.append(
                pltpu.make_async_remote_copy(
                    src_ref=source.at[:, :, pl.ds(first, width)],
                    dst_ref=sides.at[side],
                    send_sem=send_sem.at[step, side],
                    recv_sem=recv_sem.at[step, side],
                    device_id=(lax.rem(gx + shift, NX), gy),
                    device_id_type=MESH,
                )
            )
        for row in range(3):
            for side in range(2):
                copies.append(
                    pltpu.make_async_remote_copy(
                        src_ref=packed.at[step],
                        dst_ref=edges_in.at[step, 2 * row + side],
                        send_sem=send_sem.at[step, 2 + 2 * row + side],
                        recv_sem=recv_sem.at[step, 2 + 2 * row + side],
                        device_id=(
                            lax.rem(gx + NX + 1 - row, NX),
                            lax.rem(gy + (1 if side == 0 else NY - 1), NY),
                        ),
                        device_id_type=MESH,
                    )
                )
        for copy in copies:
            copy.start()
        return copies

    def reduction(grads, first_in, chunk, second_in, sums, part):
        rows = chunk.shape[1]

        def chunk_rows(index):
            return pl.ds(pl.multiple_of(index * rows, rows), rows)

        def first(d):
            peer = lax.rem(gy + d, NY)
            return pltpu.make_async_remote_copy(
                src_ref=grads.at[chunk_rows(peer)],
                dst_ref=first_in.at[d],
                send_sem=sum_send.at[part, 0, d],
                recv_sem=sum_recv.at[part, 0, d],
                device_id=(gx, peer),
                device_id_type=MESH,
            )

        def second(d):
            return pltpu.make_async_remote_copy(
                src_ref=chunk.at[0],
                dst_ref=second_in.at[d],
                send_sem=sum_send.at[part, 1, d],
                recv_sem=sum_recv.at[part, 1, d],
                device_id=(lax.rem(gx + d, NX), gy),
                device_id_type=MESH,
            )

        def third(d):
            return pltpu.make_async_remote_copy(
                src_ref=chunk.at[1],
                dst_ref=sums.at[chunk_rows(gy)],
                send_sem=sum_send.at[part, 2, d],
                recv_sem=sum_recv.at[part, 2, d],
                device_id=(gx, lax.rem(gy + d, NY)),
                device_id_type=MESH,
            )

        def start_first():
            start_all(first)

        def start_second():
            wait_all(first)
            own = grads[chunk_rows(gy), :].astype(F32)
            for d in range(1, NY):
                own = own + first_in[d].astype(F32)
            chunk[0] = own.astype(BF16)
            start_all(second)
            return own

        def start_third(own):
            wait_all(second)
            for d in range(1, NX):
                own = own + second_in[d].astype(F32)
            chunk[1] = own.astype(BF16)
            start_all(third)
            sums[chunk_rows(gy), :] = chunk[1]

        def finish():
            wait_all(third)

        return start_first, start_second, start_third, finish

    def start_all(copy):
        @pl.loop(1, NX)
        def _(d):
            copy(d).start()

    def wait_all(copy):
        @pl.loop(1, NX)
        def _(d):
            copy(d).wait()

    def put_rows(grads, term):
        for k in range(3):
            grads[3 * C * k : 3 * C * (k + 1), :] = term[:, k * LANE : (k + 1) * LANE].astype(BF16)
        tail = term[:, 3 * LANE :]
        grads[9 * C : 9 * C + 72, 0:C] = tail[0:72].astype(BF16)
        grads[9 * C : 9 * C + 72, C : 2 * C] = tail[72:144].astype(BF16)

    load_feat.wait()
    to_grid(feat, work, places, fine)
    pack_edges(fine[...], 8, edge_f, packed.at[0])
    pl.semaphore_wait(barrier, 2 * (NX - 1) + 4)
    copies = exchange(0, fine, 1024, LANE, sides_f.at[0])

    for load in loads:
        load.wait()
    build_shift_coarse(shift_c)
    to_grid(cot_in, work, places, cot)
    eye[...] = one_hot(iota((4 * C, 4 * C), 0) == iota((4 * C, 4 * C), 1))
    stage[...] = jnp.zeros_like(stage)
    step_rows(down_w, up_w, stage, eye, ddn, dga, uup, ugr)
    lower_mask = tile_lanes(lower, C, 512)
    for wz in range(4):
        both = dot(ugr[...], quarters(cot, wz))
        value = (both[:C] + roll_half(both[C:])) * lower_mask
        grect[wz] = value
        grect_low[wz] = value.astype(BF16)
    pack_edges(grect_low[...], 4, edge_c, packed.at[2])
    grect_copies = exchange(2, grect_low, 512, LANE, sides_g)
    build_shift_fine(shift_f)
    build_roll(roll_c)
    kernel_rows(fine_w, stack, eye, wf, wfb)
    kernel_rows(coarse_w, stack, eye, wc, wcb)
    grads_a[...] = jnp.zeros_like(grads_a)
    grads_b[...] = jnp.zeros_like(grads_b)
    gcoarse_own[...] = jnp.zeros_like(gcoarse_own)

    for copy in copies:
        copy.wait()
    widen(fine, sides_f.at[0], edges_in.at[0], shift_f, fine3, 8, 8, here)
    convolve(fine3, wf, hidden, 8, 1024)

    live_fine = tile_lanes(live, C, 1024)
    for z in range(8):
        value = hidden[z + 1] * live_fine
        hidden[z + 1] = value
        act[z] = (value * jax.nn.sigmoid(value)).astype(BF16)

    for wz in range(4):
        both = dot(ddn[...], quarters(act, wz))
        low[wz] = ((both[:C] + roll_half(both[C:])) * lower_mask).astype(BF16)

    pack_edges(low[...], 4, edge_c, packed.at[1])
    copies = exchange(1, low, 512, 2 * LANE, sides_c)
    for copy in grect_copies:
        copy.wait()
    extend_grect(grect, sides_g, edges_in.at[2], shift_c, grect_wide, here)
    for copy in copies:
        copy.wait()
    widen_coarse(low, sides_c, edges_in.at[1], shift_c, low3, here)
    convolve(low3, wc, coarse, 4, 768)

    for wz in range(4):
        value = coarse[wz + 1]
        grad = grect_wide[wz] * slope(value)
        gcoarse[wz] = grad.astype(BF16)
        gcoarse_own[wz + 1] = (grad[:, LANE : 5 * LANE] * lower_mask).astype(BF16)
        value = value[:, LANE : 5 * LANE]
        rect = value * jax.nn.sigmoid(value) * lower_mask
        rect2[wz, 0:C] = rect.astype(BF16)
        rect2[wz, C : 2 * C] = roll_half(rect).astype(BF16)

    roll_columns(gcoarse, roll_c, gcoarse3)
    convolve(gcoarse3, wcb, coarse2, 4, 512)

    live_coarse = tile_lanes(half_live, C, 512)
    ghid[0] = jnp.zeros((C, 1024), BF16)
    ghid[9] = jnp.zeros((C, 1024), BF16)
    for wz in range(4):
        value = coarse2[wz + 1] * live_coarse
        gdown2[wz, 0:C] = value.astype(BF16)
        gdown2[wz, C : 2 * C] = roll_half(value).astype(BF16)
        back = dot(dga[...], gdown2[wz])
        for a in range(2):
            for b in range(2):
                k = 2 * a + b
                for wx in range(4):
                    lanes = pl.ds((2 * wx + b) * LANE, LANE)
                    piece = back[k * C : (k + 1) * C, wx * LANE : (wx + 1) * LANE]
                    ghid[2 * wz + a + 1, :, lanes] = (
                        cot[2 * wz + a, :, lanes].astype(F32)
                        + piece * slope(hidden[2 * wz + a + 1, :, lanes])
                    ).astype(BF16)

    first_a, second_a, third_a, finish_a = reduction(
        grads_a, first_in_a, chunk_a, second_in_a, sums_a, 0
    )
    first_b, second_b, third_b, finish_b = reduction(
        grads_b, first_in_b, chunk_b, second_in_b, sums_b, 1
    )
    kernel_terms(gcoarse_own, low3, term_c, 4, 512, LANE)
    total_u = jnp.zeros((4 * C, 2 * C), F32)
    total_d = jnp.zeros((2 * C, 4 * C), F32)
    for wz in range(4):
        total_u = total_u + dot_t(quarters(cot, wz), rect2[wz])
        total_d = total_d + dot_t(gdown2[wz], quarters(act, wz))
    put_rows(grads_b, term_c)
    low_d = total_d[:, 0:LANE].astype(BF16)
    high_d = total_d[:, LANE:192].astype(BF16)
    grads_b[512:704, 0 : 2 * C] = total_u.astype(BF16)
    grads_b[512:608, 96:LANE] = high_d[:, 0:32]
    grads_b[608:704, 96:LANE] = high_d[:, 32:64]
    grads_b[704:768, :] = low_d[0:64]
    grads_b[432:464, 96:LANE] = low_d[64:96, 0:32]
    grads_b[464:496, 96:LANE] = low_d[64:96, 32:64]
    grads_a[432:464, 96:LANE] = low_d[64:96, 64:96]
    grads_a[464:496, 96:LANE] = low_d[64:96, 96:LANE]
    first_b()
    kernel_terms(ghid, fine3, term_f, 8, 1024, 0)
    put_rows(grads_a, term_f)
    first_a()
    pack_edges(ghid[1:9], 8, edge_f, packed.at[3])
    copies = exchange(3, ghid.at[pl.ds(1, 8)], 1024, LANE, sides_f.at[1])

    for wz in range(4):
        upward = dot(uup[...], rect2[wz])
        for a in range(2):
            for b in range(2):
                k = 2 * a + b
                for wx in range(4):
                    lanes = pl.ds((2 * wx + b) * LANE, LANE)
                    piece = upward[k * C : (k + 1) * C, wx * LANE : (wx + 1) * LANE]
                    result[2 * wz + a, :, lanes] = (
                        hidden[2 * wz + a + 1, :, lanes] + piece
                    ).astype(BF16)
    to_blocks(result, places, blocks_out)
    own_b = second_b()
    own_a = second_a()

    for copy in copies:
        copy.wait()
    widen(ghid.at[pl.ds(1, 8)], sides_f.at[1], edges_in.at[3], shift_f, ghid3, 8, 8, here)
    convolve(ghid3, wfb, hidden, 8, 1024)
    for z in range(8):
        result[z] = hidden[z + 1].astype(BF16)
    to_blocks(result, places, blocks_ig)

    third_b(own_b)
    third_a(own_a)
    finish_b()
    finish_a()


def unpack(
    sums_a,
    sums_b,
    out_in,
    ig_in,
    out_hbm,
    ig_hbm,
    gf_hbm,
    gd_hbm,
    gc_hbm,
    gu_hbm,
    gf,
    gd,
    gc,
    gu,
    stage,
    sem,
):
    copies = [
        pltpu.make_async_copy(source, target, sem.at[k])
        for k, (source, target) in enumerate(
            (
                (gf, gf_hbm),
                (gc, gc_hbm),
                (gu, gu_hbm),
                (gd, gd_hbm),
                (out_in, out_hbm),
                (ig_in, ig_hbm),
            )
        )
    ]
    copies[4].start()
    copies[5].start()
    scale = 1.0 / math.sqrt(SLOTS * 512 * NX * NY)

    for part, (sums, target) in enumerate(((sums_a, gf), (sums_b, gc))):
        tail = sums[9 * C : 9 * C + 80, :].astype(F32)
        tail = jnp.concatenate([tail[0:72, 0:C], tail[0:72, C : 2 * C]], axis=0)
        rows = jnp.concatenate(
            [sums[3 * C * k : 3 * C * (k + 1), :].astype(F32) for k in range(3)] + [tail], axis=1
        )
        rows = rows * scale
        for dz in range(3):
            for k in range(9):
                block = rows[(2 - dz) * C : (3 - dz) * C, k * C : (k + 1) * C]
                target[9 * dz + k] = block
        copies[part].start()
    for k in range(4):
        for e in range(2):
            block = sums_b[512 + k * C : 512 + (k + 1) * C, e * C : (e + 1) * C]
            gu[2 * k + e] = block.astype(F32) * scale
    copies[2].start()
    last = jnp.concatenate(
        [
            sums[first : first + 32, 96:LANE].astype(F32)
            for sums in (sums_b, sums_a)
            for first in (432, 464)
        ],
        axis=1,
    )
    low = jnp.concatenate([sums_b[704:768, :].astype(F32), last], axis=0)
    high = jnp.concatenate(
        [sums_b[512:608, 96:LANE].astype(F32), sums_b[608:704, 96:LANE].astype(F32)], axis=1
    )
    rows = jnp.concatenate([low, high], axis=1) * scale
    for k in range(4):
        for e in range(2):
            block = rows[e * C : (e + 1) * C, k * C : (k + 1) * C]
            stage[pl.ds(2 * k + e, C, stride=8), :] = jnp.concatenate(
                [block, jnp.zeros((C, LANE - C), F32)], axis=1
            )
    for o in range(C):
        gd[o] = stage[8 * o : 8 * o + 8, 0:C]
    copies[3].start()
    for copy in copies:
        copy.wait()


def on_device(
    features, block_slots, block_count, cotangent, fine_weight, down_weight, coarse_weight, up_weight
):
    vmem = pl.BlockSpec(memory_space=pltpu.VMEM)
    smem = pl.BlockSpec(memory_space=pltpu.SMEM)
    hbm = pl.BlockSpec(memory_space=pltpu.HBM)
    blocks = (SLOTS, C, 512)
    kernel_shape = (27, C, C)
    block_shape = jax.ShapeDtypeStruct(blocks, BF16)
    out, ig, sums_a, sums_b = pl.pallas_call(
        section,
        out_shape=(
            block_shape,
            block_shape,
            jax.ShapeDtypeStruct((ROWS_A, LANE), BF16),
            jax.ShapeDtypeStruct((ROWS_B, LANE), BF16),
        ),
        in_specs=[smem, smem] + [hbm] * 6,
        out_specs=(vmem, vmem, vmem, vmem),
        scratch_shapes=[
            pltpu.VMEM(blocks, BF16),
            pltpu.VMEM(blocks, BF16),
            pltpu.VMEM(kernel_shape, BF16),
            pltpu.VMEM((C, 8, C), BF16),
            pltpu.VMEM(kernel_shape, BF16),
            pltpu.VMEM((8, C, C), BF16),
            pltpu.VMEM((8 * C, LANE), F32),
            pltpu.VMEM((9 * C, C), BF16),
            pltpu.VMEM((4 * C, 4 * C), BF16),
            pltpu.VMEM((3 * C, 9 * C), BF16),
            pltpu.VMEM((3 * C, 9 * C), BF16),
            pltpu.VMEM((3 * C, 9 * C), BF16),
            pltpu.VMEM((3 * C, 9 * C), BF16),
            pltpu.VMEM((2 * C, 4 * C), BF16),
            pltpu.VMEM((4 * C, 2 * C), BF16),
            pltpu.VMEM((4 * C, 2 * C), BF16),
            pltpu.VMEM((2 * C, 4 * C), BF16),
            pltpu.VMEM((8, C, 1024), BF16),
            pltpu.VMEM((1024, 1024), BF16),
            pltpu.VMEM((8, 256, 256), BF16),
            pltpu.VMEM((4, 256, 384), BF16),
            pltpu.VMEM((LANE, 256), BF16),
            pltpu.VMEM((1024, LANE), BF16),
            pltpu.VMEM((512, LANE), BF16),
            pltpu.VMEM((8, C, 1024), BF16),
            pltpu.VMEM((8, C, 1024), BF16),
            pltpu.VMEM((8, 3 * C, 1280), BF16),
            pltpu.VMEM((10, C, 1024), F32),
            pltpu.VMEM((8, C, 1024), BF16),
            pltpu.VMEM((4, C, 512), BF16),
            pltpu.VMEM((4, 3 * C, 1024), BF16),
            pltpu.VMEM((6, C, 768), F32),
            pltpu.VMEM((6, C, 512), F32),
            pltpu.VMEM((4, C, 512), F32),
            pltpu.VMEM((4, C, 512), BF16),
            pltpu.VMEM((4, C, 768), F32),
            pltpu.VMEM((4, 2 * C, 512), BF16),
            pltpu.VMEM((4, C, 768), BF16),
            pltpu.VMEM((6, C, 512), BF16),
            pltpu.VMEM((4, 3 * C, 768), BF16),
            pltpu.VMEM((4, 2 * C, 512), BF16),
            pltpu.VMEM((10, C, 1024), BF16),
            pltpu.VMEM((8, 3 * C, 1280), BF16),
            pltpu.VMEM((8, C, 1024), BF16),
            pltpu.VMEM((3 * C, 9 * C), F32),
            pltpu.VMEM((3 * C, 9 * C), F32),
            pltpu.VMEM((4, C, LANE), BF16),
            pltpu.VMEM((2, 2, 8, C, LANE), BF16),
            pltpu.VMEM((2, 4, C, 2 * LANE), BF16),
            pltpu.VMEM((2, 4, C, LANE), BF16),
            pltpu.VMEM((4, 6, C, LANE), BF16),
            pltpu.VMEM((ROWS_A, LANE), BF16),
            pltpu.VMEM((NY, ROWS_A // NY, LANE), BF16),
            pltpu.VMEM((2, ROWS_A // NY, LANE), BF16),
            pltpu.VMEM((NX, ROWS_A // NY, LANE), BF16),
            pltpu.VMEM((ROWS_B, LANE), BF16),
            pltpu.VMEM((NY, ROWS_B // NY, LANE), BF16),
            pltpu.VMEM((2, ROWS_B // NY, LANE), BF16),
            pltpu.VMEM((NX, ROWS_B // NY, LANE), BF16),
            pltpu.SemaphoreType.DMA((6,)),
            pltpu.SemaphoreType.DMA((4, 8)),
            pltpu.SemaphoreType.DMA((4, 8)),
            pltpu.SemaphoreType.DMA((2, 3, NX)),
            pltpu.SemaphoreType.DMA((2, 3, NX)),
        ],
        compiler_params=pltpu.CompilerParams(
            collective_id=0, has_side_effects=True, vmem_limit_bytes=50 * 1024 * 1024
        ),
        name="section",
    )(
        block_slots.reshape(1, SLOTS),
        block_count.reshape(1, 1),
        *(
            pltpu.with_memory_space_constraint(value, pltpu.HBM)
            for value in (
                features.reshape(blocks),
                cotangent.reshape(blocks),
                fine_weight.transpose(1, 0, 2),
                down_weight,
                coarse_weight.transpose(1, 0, 2),
                up_weight,
            )
        ),
    )
    out, ig, gf, gd, gc, gu = pl.pallas_call(
        unpack,
        out_shape=(
            block_shape,
            block_shape,
            jax.ShapeDtypeStruct(kernel_shape, F32),
            jax.ShapeDtypeStruct((C, 8, C), F32),
            jax.ShapeDtypeStruct(kernel_shape, F32),
            jax.ShapeDtypeStruct((8, C, C), F32),
        ),
        in_specs=[vmem, vmem, vmem, vmem],
        out_specs=(hbm,) * 6,
        scratch_shapes=[
            pltpu.VMEM(kernel_shape, F32),
            pltpu.VMEM((C, 8, C), F32),
            pltpu.VMEM(kernel_shape, F32),
            pltpu.VMEM((8, C, C), F32),
            pltpu.VMEM((8 * C, LANE), F32),
            pltpu.SemaphoreType.DMA((6,)),
        ],
        compiler_params=pltpu.CompilerParams(vmem_limit_bytes=8 * 1024 * 1024),
        name="unpack",
    )(sums_a, sums_b, out, ig)
    shape_out = (1, 1) + blocks
    gf, gc = gf.transpose(1, 0, 2), gc.transpose(1, 0, 2)
    return out.reshape(shape_out), ig.reshape(shape_out), gf, gd, gc, gu


def solution(mesh):
    split = P("gx", "gy", None, None, None)
    return jax.shard_map(
        on_device,
        mesh=mesh,
        in_specs=(split, P("gx", "gy", None), P("gx", "gy"), split, P(), P(), P(), P()),
        out_specs=(split, split, P(), P(), P(), P()),
        check_vma=False,
    )
```

```python
import math

import jax
import jax.numpy as jnp
from jax import lax
from jax.experimental import pallas as pl
from jax.experimental.pallas import tpu as pltpu
from jax.sharding import PartitionSpec as P

C = 48
SLOTS = 16
LANE = 128
NX = 16
NY = 16
ROWS_A = 512
ROWS_B = 768
F32 = jnp.float32
BF16 = jnp.bfloat16
MESH = pl.DeviceIdType.MESH


def dot(a, b):
    return jnp.dot(a, b, preferred_element_type=F32)


def dot_t(a, b):
    return lax.dot_general(a, b, (((1,), (1,)), ((), ())), preferred_element_type=F32)


def iota(shape, dim):
    return lax.broadcasted_iota(jnp.int32, shape, dim)


def one_hot(cond):
    return jnp.where(cond, 1.0, 0.0).astype(BF16)


def build_shift_fine(s_ref):
    row = iota((256, 256), 0)
    col = iota((256, 256), 1)
    lane = col % LANE
    right = col >= LANE
    before = jnp.where(lane < 64, lane + 63, lane - 64)
    after = jnp.where(lane < 64, lane + 64, lane - 63)
    before = jnp.where(lane == 0, -1, before)
    after = jnp.where(lane == 127, -1, after)
    source = jnp.where(right, after, before)
    place = jnp.where(lane == jnp.where(right, 127, 0), jnp.where(right, LANE + 8, LANE), -512)

    @pl.loop(0, 8)
    def _(x):
        s_ref[x] = one_hot((row == source) | (row == place + x))


def coarse_edge(group):
    return jnp.where(
        group == 0, 63, jnp.where(group == 1, 62, jnp.where(group == 2, 0, jnp.where(group == 3, 1, -1)))
    )


def build_shift_coarse(s_ref):
    row = iota((256, 384), 0)
    col = iota((256, 384), 1)
    source = (col % LANE + col // LANE + LANE - 1) % LANE
    halo = row - LANE
    spot = jnp.where(
        halo < 4, 127, jnp.where(halo < 8, 126, jnp.where(halo < 12, 64, jnp.where(halo < 16, 65, -1)))
    )
    own = (row < 64) & (row == source)
    other = (halo >= 0) & (spot == source)

    @pl.loop(0, 4)
    def _(x):
        s_ref[x] = one_hot(own | (other & (halo % 4 == x)))


def build_roll(r_ref):
    row = iota((LANE, 256), 0)
    col = iota((LANE, 256), 1)
    r_ref[...] = one_hot(row == (col % LANE + 2 * (col // LANE) + LANE - 1) % LANE)


def build_edges(fine_ref, coarse_ref):
    row = iota((1024, LANE), 0)
    col = iota((1024, LANE), 1)
    lane = row % LANE
    x = row // LANE
    fine_ref[...] = one_hot(((lane == 127) & (col == x)) | ((lane == 0) & (col == x + 8)))
    row = iota((512, LANE), 0)
    col = iota((512, LANE), 1)
    coarse_ref[...] = one_hot((row % LANE == coarse_edge(col // 4)) & (row // LANE == col % 4))


def build_places(e_ref, slots_ref, live_count):
    e_ref[...] = jnp.zeros_like(e_ref)
    row = iota((16, 256), 0)
    col = iota((16, 256), 1)
    y = row % 8
    own = (row // 8) == (col // LANE)
    spot = col % LANE - 64 * (y % 2) - y // 2

    @pl.loop(0, SLOTS)
    def _(s):
        place = jnp.where(s < live_count, slots_ref[0, s], 4096)
        tile = one_hot(own & (spot == 4 * place))
        for j in range(4):
            e_ref[pl.ds(pl.multiple_of(64 * s + 16 * j, 16), 16), 256 * j : 256 * j + 256] = tile


def live_lanes(slots_ref, live_count):
    spot = (iota((8, LANE), 1) % 64) // 4

    def step(s, total):
        place = jnp.where(s < live_count, slots_ref[0, s], 4096)
        return total + jnp.where(spot == place, 1.0, 0.0)

    return lax.fori_loop(0, SLOTS, step, jnp.zeros((8, LANE), F32))


def to_grid(blocks, work, e_ref, grid):
    for t in range(8):
        lanes = slice(t * LANE, (t + 1) * LANE)
        for pair in range(4):
            one = blocks[2 * t, :, pair * LANE : (pair + 1) * LANE]
            two = blocks[2 * t + 1, :, pair * LANE : (pair + 1) * LANE]
            work[2 * pair, :, lanes] = jnp.concatenate([one[:, :64], two[:, :64]], axis=1)
            work[2 * pair + 1, :, lanes] = jnp.concatenate([one[:, 64:], two[:, 64:]], axis=1)

    for n in range(4):
        lanes = slice(n * 256, (n + 1) * 256)
        moved = dot(work[...].reshape(8 * C, 1024), e_ref[:, lanes])
        grid[:, :, lanes] = moved.astype(BF16).reshape(8, C, 256)


def to_blocks(grid, e_ref, blocks):
    for n in range(4):
        rows = slice(n * 256, (n + 1) * 256)
        moved = dot_t(grid[...].reshape(8 * C, 1024), e_ref[rows, :])
        moved = moved.astype(BF16).reshape(8, C, 256)
        for pair in range(4):
            for k in range(4):
                low = moved[2 * pair, :, 64 * k : 64 * k + 64]
                high = moved[2 * pair + 1, :, 64 * k : 64 * k + 64]
                blocks[4 * n + k, :, pair * LANE : (pair + 1) * LANE] = jnp.concatenate(
                    [low, high], axis=1
                )


def pack_edges(grid, depth, t_ref, packed):
    edges = dot(grid.reshape(depth * C, grid.shape[2]), t_ref[...]).reshape(depth, C, LANE)
    total = edges[0]
    for z in range(1, depth):
        total = total + pltpu.roll(edges[z], 16 * z, 1)
    packed[...] = total.astype(BF16)


def unpack_edges(received, row, left_ok, right_ok, depth):
    lane = iota((C, LANE), 1) % 16
    left = jnp.where(left_ok, received[2 * row].astype(F32), 0.0)
    right = jnp.where(right_ok, received[2 * row + 1].astype(F32), 0.0)
    both = jnp.where(lane < 8, left, right)
    parts = [both] + [pltpu.roll(both, LANE - 16 * z, 1) for z in range(1, depth)]
    return jnp.stack(parts, axis=0).astype(BF16).reshape(depth * C, LANE)


def widen(grid, sides, received, s_ref, wide, count, depth, place):
    gx, gy = place
    low_ok, high_ok = gx > 0, gx < NX - 1
    left_ok, right_ok = gy > 0, gy < NY - 1

    def put(rows, halo, x, lanes):
        moved = dot(jnp.concatenate([rows, halo], axis=1), s_ref[x]).astype(BF16)
        wide[:, 0:C, lanes] = moved[:, :LANE].reshape(depth, C, LANE)
        wide[:, C : 2 * C, lanes] = rows.reshape(depth, C, LANE)
        wide[:, 2 * C : 3 * C, lanes] = moved[:, LANE:].reshape(depth, C, LANE)

    zero = jnp.zeros((depth * C, LANE), BF16)
    halo = unpack_edges(received, 0, left_ok & low_ok, right_ok & low_ok, depth)
    rows = jnp.where(low_ok, sides[0].reshape(depth * C, LANE), zero)
    put(rows, halo, count - 1, pl.ds(0, LANE))
    halo = unpack_edges(received, 2, left_ok & high_ok, right_ok & high_ok, depth)
    rows = jnp.where(high_ok, sides[1].reshape(depth * C, LANE), zero)
    put(rows, halo, 0, pl.ds((count + 1) * LANE, LANE))
    halo = unpack_edges(received, 1, left_ok, right_ok, depth)

    for x in range(count):
        rows = grid[:, :, x * LANE : (x + 1) * LANE].reshape(depth * C, LANE)
        put(rows, halo, x, pl.ds((x + 1) * LANE, LANE))


def coarse_halos(received, place):
    gx, gy = place
    left_ok, right_ok = gy > 0, gy < NY - 1
    low_ok, high_ok = gx > 0, gx < NX - 1
    return (
        unpack_edges(received, 0, left_ok & low_ok, right_ok & low_ok, 4),
        unpack_edges(received, 1, left_ok, right_ok, 4),
        unpack_edges(received, 2, left_ok & high_ok, right_ok & high_ok, 4),
    )


def widen_coarse(grid, sides, received, s_ref, wide, place):
    gx = place[0]
    halos = coarse_halos(received, place)
    zero = jnp.zeros((4 * C, LANE), BF16)
    halves = []
    for side, inside in ((0, gx > 0), (1, gx < NX - 1)):
        rows = jnp.where(inside, sides[side].reshape(4 * C, LANE), zero)
        halves.append([rows, pltpu.roll(rows.astype(F32), 64, 1).astype(BF16)])
    for column in range(8):
        if column < 2:
            rows, halo, x = halves[0][column], halos[0], column + 2
        elif column < 6:
            x = column - 2
            rows = grid[:, :, x * LANE : (x + 1) * LANE].reshape(4 * C, LANE)
            halo = halos[1]
        else:
            x = column - 6
            rows, halo = halves[1][x], halos[2]
        moved = dot(jnp.concatenate([rows, halo], axis=1), s_ref[x]).astype(BF16)
        for t in range(3):
            part = moved[:, t * LANE : (t + 1) * LANE].reshape(4, C, LANE)
            wide[:, t * C : (t + 1) * C, column * LANE : (column + 1) * LANE] = part


def extend_grect(grect, sides, received, s_ref, wide, place):
    gx = place[0]
    halos = coarse_halos(received, place)
    zero = jnp.zeros((4 * C, LANE), F32)
    for column in range(6):
        if column == 0:
            rows = jnp.where(gx > 0, sides[0].reshape(4 * C, LANE).astype(F32), zero)
            halo, x = halos[0], 3
        elif column < 5:
            x = column - 1
            rows = grect[:, :, x * LANE : (x + 1) * LANE].reshape(4 * C, LANE)
            halo = halos[1]
        else:
            rows = jnp.where(gx < NX - 1, sides[1].reshape(4 * C, LANE).astype(F32), zero)
            halo, x = halos[2], 0
        total = rows + dot(halo, s_ref[x, LANE:, LANE : 2 * LANE])
        wide[:, :, column * LANE : (column + 1) * LANE] = total.reshape(4, C, LANE)


def roll_columns(grid, r_ref, wide):
    for column in range(6):
        lanes = slice(column * LANE, (column + 1) * LANE)
        rows = grid[:, :, lanes]
        moved = dot(rows.reshape(4 * C, LANE), r_ref[...]).astype(BF16)
        wide[:, 0:C, lanes] = moved[:, :LANE].reshape(4, C, LANE)
        wide[:, C : 2 * C, lanes] = rows
        wide[:, 2 * C : 3 * C, lanes] = moved[:, LANE:].reshape(4, C, LANE)


def window(wide, z, first, width):
    return jnp.concatenate(
        [wide[z, :, first + dx * LANE : first + dx * LANE + width] for dx in range(3)], axis=0
    )


def convolve(wide, weight, total, depth, width):
    total[...] = jnp.zeros_like(total)
    for z in range(depth):
        for first in range(0, width, 256):
            piece = dot(weight[...], window(wide, z, first, 256)).reshape(3, C, 256)
            lanes = slice(first, first + 256)
            total[z : z + 3, :, lanes] = total[z : z + 3, :, lanes] + piece


def kernel_terms(grad, wide, total, depth, width, start):
    ahead = [grad[z : z + 3].reshape(3 * C, width) for z in range(depth)]
    pieces = [window(wide, z, start, width) for z in range(depth)]
    total[...] = dot_t(jnp.concatenate(ahead, axis=1), jnp.concatenate(pieces, axis=1))


def quarters(grid, wz):
    columns = []
    for a in range(2):
        for b in range(2):
            columns.append(
                jnp.concatenate(
                    [
                        grid[2 * wz + a, :, (2 * wx + b) * LANE : (2 * wx + b + 1) * LANE]
                        for wx in range(4)
                    ],
                    axis=1,
                )
            )
    return jnp.concatenate(columns, axis=0)


def tile_lanes(mask, rows, width):
    return jnp.broadcast_to(jnp.concatenate([mask] * (width // LANE), axis=1)[0:1], (rows, width))


def roll_half(value):
    parts = [
        pltpu.roll(value[:, k * LANE : (k + 1) * LANE], 64, 1) for k in range(value.shape[1] // LANE)
    ]
    return jnp.concatenate(parts, axis=1)


def kernel_rows(weight, stack, eye, forward, backward):
    for dz in range(3):
        for k in range(9):
            block = weight[9 * dz + k]
            forward[(2 - dz) * C : (3 - dz) * C, k * C : (k + 1) * C] = block
            stack[(8 - k) * C : (9 - k) * C, :] = block
        backward[dz * C : (dz + 1) * C, :] = dot_t(eye[0:C, 0:C], stack[...]).astype(BF16)


def step_rows(down, up, stage, eye, ddn, dga, uup, ugr):
    for o in range(C):
        stage[8 * o : 8 * o + 8, 0:C] = down[o].astype(F32)
    for k in range(4):
        for e in range(2):
            q = 2 * k + e
            block = stage[pl.ds(q, C, stride=8), :].astype(BF16)[:, 0:C]
            ddn[e * C : (e + 1) * C, k * C : (k + 1) * C] = block
            uup[k * C : (k + 1) * C, e * C : (e + 1) * C] = up[q]
    dga[...] = dot_t(eye[...], ddn[...]).astype(BF16)
    ugr[...] = dot_t(eye[0 : 2 * C, 0 : 2 * C], uup[...]).astype(BF16)


def slope(value):
    sigma = jax.nn.sigmoid(value)
    return sigma * (1.0 + value * (1.0 - sigma))


def section(
    slots_ref,
    count_ref,
    feat_hbm,
    cot_hbm,
    fine_hbm,
    down_hbm,
    coarse_hbm,
    up_hbm,
    blocks_out,
    blocks_ig,
    sums_a,
    sums_b,
    feat,
    cot_in,
    fine_w,
    down_w,
    coarse_w,
    up_w,
    stage,
    stack,
    eye,
    wf,
    wfb,
    wc,
    wcb,
    ddn,
    dga,
    uup,
    ugr,
    work,
    places,
    shift_f,
    shift_c,
    roll_c,
    edge_f,
    edge_c,
    fine,
    cot,
    fine3,
    hidden,
    act,
    low,
    low3,
    coarse,
    coarse2,
    grect,
    grect_low,
    grect_wide,
    rect2,
    gcoarse,
    gcoarse_own,
    gcoarse3,
    gdown2,
    ghid,
    ghid3,
    result,
    term_f,
    term_c,
    packed,
    sides_f,
    outer,
    sides_c,
    sides_g,
    edges_in,
    grads_a,
    first_in_a,
    chunk_a,
    second_in_a,
    grads_b,
    first_in_b,
    chunk_b,
    second_in_b,
    local_sem,
    send_sem,
    recv_sem,
    sum_send,
    sum_recv,
):
    gx = lax.axis_index("gx")
    gy = lax.axis_index("gy")
    here = (gx, gy)

    load_feat = pltpu.make_async_copy(feat_hbm, feat, local_sem.at[5])
    load_feat.start()
    loads = [
        pltpu.make_async_copy(source, target, local_sem.at[k])
        for k, (source, target) in enumerate(
            (
                (fine_hbm, fine_w),
                (down_hbm, down_w),
                (coarse_hbm, coarse_w),
                (up_hbm, up_w),
                (cot_hbm, cot_in),
            )
        )
    ]
    for load in loads:
        load.start()

    barrier = pltpu.get_barrier_semaphore()

    @pl.loop(1, NX)
    def _(d):
        pl.semaphore_signal(
            barrier, inc=1, device_id=(lax.rem(gx + d, NX), gy), device_id_type=MESH
        )
        pl.semaphore_signal(
            barrier, inc=1, device_id=(gx, lax.rem(gy + d, NY)), device_id_type=MESH
        )

    for dx in (1, NX - 1):
        for dy in (1, NY - 1):
            pl.semaphore_signal(
                barrier,
                inc=1,
                device_id=(lax.rem(gx + dx, NX), lax.rem(gy + dy, NY)),
                device_id_type=MESH,
            )

    live_count = count_ref[0, 0]
    build_places(places, slots_ref, live_count)
    build_edges(edge_f, edge_c)
    live = live_lanes(slots_ref, live_count)
    half_live = jnp.where(iota((8, LANE), 1) < 64, live, 0.0)
    lower = jnp.where(iota((8, LANE), 1) < 64, 1.0, 0.0)

    def exchange(step, sources, sides):
        copies = []
        for row in (0, 2, 1):
            for side in range(2):
                copies.append(
                    pltpu.make_async_remote_copy(
                        src_ref=packed.at[step],
                        dst_ref=edges_in.at[step, 2 * row + side],
                        send_sem=send_sem.at[step, 2 + 2 * row + side],
                        recv_sem=recv_sem.at[step, 2 + 2 * row + side],
                        device_id=(
                            lax.rem(gx + NX + 1 - row, NX),
                            lax.rem(gy + (1 if side == 0 else NY - 1), NY),
                        ),
                        device_id_type=MESH,
                    )
                )
        for side in range(2):
            copies.append(
                pltpu.make_async_remote_copy(
                    src_ref=sources[side],
                    dst_ref=sides.at[side],
                    send_sem=send_sem.at[step, side],
                    recv_sem=recv_sem.at[step, side],
                    device_id=(lax.rem(gx + (1 if side == 0 else NX - 1), NX), gy),
                    device_id_type=MESH,
                )
            )
        for copy in copies:
            copy.start()
        return copies

    def outer_columns(source, length):
        return [source.at[:, :, pl.ds(first, LANE)] for first in (length - LANE, 0)]

    def reduction(grads, first_in, chunk, second_in, sums, part):
        rows = chunk.shape[1]

        def chunk_rows(index):
            return pl.ds(pl.multiple_of(index * rows, rows), rows)

        def first(d):
            peer = lax.rem(gy + d, NY)
            return pltpu.make_async_remote_copy(
                src_ref=grads.at[chunk_rows(peer)],
                dst_ref=first_in.at[d],
                send_sem=sum_send.at[part, 0, d],
                recv_sem=sum_recv.at[part, 0, d],
                device_id=(gx, peer),
                device_id_type=MESH,
            )

        def second(d):
            return pltpu.make_async_remote_copy(
                src_ref=chunk.at[0],
                dst_ref=second_in.at[d],
                send_sem=sum_send.at[part, 1, d],
                recv_sem=sum_recv.at[part, 1, d],
                device_id=(lax.rem(gx + d, NX), gy),
                device_id_type=MESH,
            )

        def third(d):
            return pltpu.make_async_remote_copy(
                src_ref=chunk.at[1],
                dst_ref=sums.at[chunk_rows(gy)],
                send_sem=sum_send.at[part, 2, d],
                recv_sem=sum_recv.at[part, 2, d],
                device_id=(gx, lax.rem(gy + d, NY)),
                device_id_type=MESH,
            )

        def start_first():
            start_all(first)

        def start_second():
            wait_all(first)
            own = grads[chunk_rows(gy), :].astype(F32)
            for d in range(1, NY):
                own = own + first_in[d].astype(F32)
            chunk[0] = own.astype(BF16)
            start_all(second)
            return own

        def start_third(own):
            wait_all(second)
            for d in range(1, NX):
                own = own + second_in[d].astype(F32)
            chunk[1] = own.astype(BF16)
            start_all(third)
            sums[chunk_rows(gy), :] = chunk[1]

        def finish():
            wait_all(third)

        return start_first, start_second, start_third, finish

    def start_all(copy):
        @pl.loop(1, NX)
        def _(d):
            copy(d).start()

    def wait_all(copy):
        @pl.loop(1, NX)
        def _(d):
            copy(d).wait()

    def put_rows(grads, term):
        for k in range(3):
            grads[3 * C * k : 3 * C * (k + 1), :] = term[:, k * LANE : (k + 1) * LANE].astype(BF16)
        tail = term[:, 3 * LANE :]
        grads[9 * C : 9 * C + 72, 0:C] = tail[0:72].astype(BF16)
        grads[9 * C : 9 * C + 72, C : 2 * C] = tail[72:144].astype(BF16)

    load_feat.wait()
    to_grid(feat, work, places, fine)
    pack_edges(fine[...], 8, edge_f, packed.at[0])
    pl.semaphore_wait(barrier, 2 * (NX - 1) + 4)
    copies = exchange(0, outer_columns(fine, 1024), sides_f.at[0])

    for load in loads:
        load.wait()
    build_shift_coarse(shift_c)
    to_grid(cot_in, work, places, cot)
    eye[...] = one_hot(iota((4 * C, 4 * C), 0) == iota((4 * C, 4 * C), 1))
    stage[...] = jnp.zeros_like(stage)
    step_rows(down_w, up_w, stage, eye, ddn, dga, uup, ugr)
    lower_mask = tile_lanes(lower, C, 512)
    for wz in range(4):
        both = dot(ugr[...], quarters(cot, wz))
        value = (both[:C] + roll_half(both[C:])) * lower_mask
        grect[wz] = value
        grect_low[wz] = value.astype(BF16)
    pack_edges(grect_low[...], 4, edge_c, packed.at[2])
    build_shift_fine(shift_f)
    build_roll(roll_c)
    kernel_rows(fine_w, stack, eye, wf, wfb)
    kernel_rows(coarse_w, stack, eye, wc, wcb)
    grads_a[...] = jnp.zeros_like(grads_a)
    grads_b[...] = jnp.zeros_like(grads_b)
    gcoarse_own[...] = jnp.zeros_like(gcoarse_own)

    for copy in copies:
        copy.wait()
    grect_copies = exchange(2, outer_columns(grect_low, 512), sides_g)
    widen(fine, sides_f.at[0], edges_in.at[0], shift_f, fine3, 8, 8, here)
    convolve(fine3, wf, hidden, 8, 1024)

    live_fine = tile_lanes(live, C, 1024)
    for z in range(8):
        value = hidden[z + 1] * live_fine
        hidden[z + 1] = value
        act[z] = (value * jax.nn.sigmoid(value)).astype(BF16)

    for wz in range(4):
        both = dot(ddn[...], quarters(act, wz))
        value = (both[:C] + roll_half(both[C:])) * lower_mask
        low[wz] = value.astype(BF16)
        for side, first in ((0, 2 * LANE), (1, 0)):
            second = pltpu.roll(value[:, first + LANE : first + 2 * LANE], 64, 1)
            outer[side, wz] = (value[:, first : first + LANE] + second).astype(BF16)

    pack_edges(low[...], 4, edge_c, packed.at[1])
    copies = exchange(1, [outer.at[0], outer.at[1]], sides_c)
    for copy in grect_copies:
        copy.wait()
    extend_grect(grect, sides_g, edges_in.at[2], shift_c, grect_wide, here)
    for copy in copies:
        copy.wait()
    widen_coarse(low, sides_c, edges_in.at[1], shift_c, low3, here)
    convolve(low3, wc, coarse, 4, 768)

    for wz in range(4):
        value = coarse[wz + 1]
        grad = grect_wide[wz] * slope(value)
        gcoarse[wz] = grad.astype(BF16)
        gcoarse_own[wz + 1] = (grad[:, LANE : 5 * LANE] * lower_mask).astype(BF16)
        value = value[:, LANE : 5 * LANE]
        rect = value * jax.nn.sigmoid(value) * lower_mask
        rect2[wz, 0:C] = rect.astype(BF16)
        rect2[wz, C : 2 * C] = roll_half(rect).astype(BF16)

    roll_columns(gcoarse, roll_c, gcoarse3)
    convolve(gcoarse3, wcb, coarse2, 4, 512)

    live_coarse = tile_lanes(half_live, C, 512)
    ghid[0] = jnp.zeros((C, 1024), BF16)
    ghid[9] = jnp.zeros((C, 1024), BF16)
    for wz in range(4):
        value = coarse2[wz + 1] * live_coarse
        gdown2[wz, 0:C] = value.astype(BF16)
        gdown2[wz, C : 2 * C] = roll_half(value).astype(BF16)
        back = dot(dga[...], gdown2[wz])
        for a in range(2):
            for b in range(2):
                k = 2 * a + b
                for wx in range(4):
                    lanes = pl.ds((2 * wx + b) * LANE, LANE)
                    piece = back[k * C : (k + 1) * C, wx * LANE : (wx + 1) * LANE]
                    ghid[2 * wz + a + 1, :, lanes] = (
                        cot[2 * wz + a, :, lanes].astype(F32)
                        + piece * slope(hidden[2 * wz + a + 1, :, lanes])
                    ).astype(BF16)

    first_a, second_a, third_a, finish_a = reduction(
        grads_a, first_in_a, chunk_a, second_in_a, sums_a, 0
    )
    first_b, second_b, third_b, finish_b = reduction(
        grads_b, first_in_b, chunk_b, second_in_b, sums_b, 1
    )
    kernel_terms(gcoarse_own, low3, term_c, 4, 512, LANE)
    total_u = jnp.zeros((4 * C, 2 * C), F32)
    total_d = jnp.zeros((2 * C, 4 * C), F32)
    for wz in range(4):
        total_u = total_u + dot_t(quarters(cot, wz), rect2[wz])
        total_d = total_d + dot_t(gdown2[wz], quarters(act, wz))
    put_rows(grads_b, term_c)
    low_d = total_d[:, 0:LANE].astype(BF16)
    high_d = total_d[:, LANE:192].astype(BF16)
    grads_b[512:704, 0 : 2 * C] = total_u.astype(BF16)
    grads_b[512:608, 96:LANE] = high_d[:, 0:32]
    grads_b[608:704, 96:LANE] = high_d[:, 32:64]
    grads_b[704:768, :] = low_d[0:64]
    grads_b[432:464, 96:LANE] = low_d[64:96, 0:32]
    grads_b[464:496, 96:LANE] = low_d[64:96, 32:64]
    grads_a[432:464, 96:LANE] = low_d[64:96, 64:96]
    grads_a[464:496, 96:LANE] = low_d[64:96, 96:LANE]
    first_b()
    kernel_terms(ghid, fine3, term_f, 8, 1024, 0)
    put_rows(grads_a, term_f)
    first_a()
    pack_edges(ghid[1:9], 8, edge_f, packed.at[3])
    copies = exchange(3, outer_columns(ghid.at[pl.ds(1, 8)], 1024), sides_f.at[1])

    for wz in range(4):
        upward = dot(uup[...], rect2[wz])
        for a in range(2):
            for b in range(2):
                k = 2 * a + b
                for wx in range(4):
                    lanes = pl.ds((2 * wx + b) * LANE, LANE)
                    piece = upward[k * C : (k + 1) * C, wx * LANE : (wx + 1) * LANE]
                    result[2 * wz + a, :, lanes] = (
                        hidden[2 * wz + a + 1, :, lanes] + piece
                    ).astype(BF16)
    to_blocks(result, places, blocks_out)
    own_b = second_b()
    own_a = second_a()

    for copy in copies:
        copy.wait()
    widen(ghid.at[pl.ds(1, 8)], sides_f.at[1], edges_in.at[3], shift_f, ghid3, 8, 8, here)
    convolve(ghid3, wfb, hidden, 8, 1024)
    for z in range(8):
        result[z] = hidden[z + 1].astype(BF16)
    to_blocks(result, places, blocks_ig)

    third_b(own_b)
    third_a(own_a)
    finish_b()
    finish_a()


def unpack(
    sums_a,
    sums_b,
    out_in,
    ig_in,
    out_hbm,
    ig_hbm,
    gf_hbm,
    gd_hbm,
    gc_hbm,
    gu_hbm,
    gf,
    gd,
    gc,
    gu,
    stage,
    sem,
):
    copies = [
        pltpu.make_async_copy(source, target, sem.at[k])
        for k, (source, target) in enumerate(
            (
                (gf, gf_hbm),
                (gc, gc_hbm),
                (gu, gu_hbm),
                (gd, gd_hbm),
                (out_in, out_hbm),
                (ig_in, ig_hbm),
            )
        )
    ]
    copies[4].start()
    copies[5].start()
    scale = 1.0 / math.sqrt(SLOTS * 512 * NX * NY)

    for part, (sums, target) in enumerate(((sums_a, gf), (sums_b, gc))):
        tail = sums[9 * C : 9 * C + 80, :].astype(F32)
        tail = jnp.concatenate([tail[0:72, 0:C], tail[0:72, C : 2 * C]], axis=0)
        rows = jnp.concatenate(
            [sums[3 * C * k : 3 * C * (k + 1), :].astype(F32) for k in range(3)] + [tail], axis=1
        )
        rows = rows * scale
        for dz in range(3):
            for k in range(9):
                block = rows[(2 - dz) * C : (3 - dz) * C, k * C : (k + 1) * C]
                target[9 * dz + k] = block
        copies[part].start()
    for k in range(4):
        for e in range(2):
            block = sums_b[512 + k * C : 512 + (k + 1) * C, e * C : (e + 1) * C]
            gu[2 * k + e] = block.astype(F32) * scale
    copies[2].start()
    last = jnp.concatenate(
        [
            sums[first : first + 32, 96:LANE].astype(F32)
            for sums in (sums_b, sums_a)
            for first in (432, 464)
        ],
        axis=1,
    )
    low = jnp.concatenate([sums_b[704:768, :].astype(F32), last], axis=0)
    high = jnp.concatenate(
        [sums_b[512:608, 96:LANE].astype(F32), sums_b[608:704, 96:LANE].astype(F32)], axis=1
    )
    rows = jnp.concatenate([low, high], axis=1) * scale
    for k in range(4):
        for e in range(2):
            block = rows[e * C : (e + 1) * C, k * C : (k + 1) * C]
            stage[pl.ds(2 * k + e, C, stride=8), :] = jnp.concatenate(
                [block, jnp.zeros((C, LANE - C), F32)], axis=1
            )
    for o in range(C):
        gd[o] = stage[8 * o : 8 * o + 8, 0:C]
    copies[3].start()
    for copy in copies:
        copy.wait()


def on_device(
    features, block_slots, block_count, cotangent, fine_weight, down_weight, coarse_weight, up_weight
):
    vmem = pl.BlockSpec(memory_space=pltpu.VMEM)
    smem = pl.BlockSpec(memory_space=pltpu.SMEM)
    hbm = pl.BlockSpec(memory_space=pltpu.HBM)
    blocks = (SLOTS, C, 512)
    kernel_shape = (27, C, C)
    block_shape = jax.ShapeDtypeStruct(blocks, BF16)
    out, ig, sums_a, sums_b = pl.pallas_call(
        section,
        out_shape=(
            block_shape,
            block_shape,
            jax.ShapeDtypeStruct((ROWS_A, LANE), BF16),
            jax.ShapeDtypeStruct((ROWS_B, LANE), BF16),
        ),
        in_specs=[smem, smem] + [hbm] * 6,
        out_specs=(vmem, vmem, vmem, vmem),
        scratch_shapes=[
            pltpu.VMEM(blocks, BF16),
            pltpu.VMEM(blocks, BF16),
            pltpu.VMEM(kernel_shape, BF16),
            pltpu.VMEM((C, 8, C), BF16),
            pltpu.VMEM(kernel_shape, BF16),
            pltpu.VMEM((8, C, C), BF16),
            pltpu.VMEM((8 * C, LANE), F32),
            pltpu.VMEM((9 * C, C), BF16),
            pltpu.VMEM((4 * C, 4 * C), BF16),
            pltpu.VMEM((3 * C, 9 * C), BF16),
            pltpu.VMEM((3 * C, 9 * C), BF16),
            pltpu.VMEM((3 * C, 9 * C), BF16),
            pltpu.VMEM((3 * C, 9 * C), BF16),
            pltpu.VMEM((2 * C, 4 * C), BF16),
            pltpu.VMEM((4 * C, 2 * C), BF16),
            pltpu.VMEM((4 * C, 2 * C), BF16),
            pltpu.VMEM((2 * C, 4 * C), BF16),
            pltpu.VMEM((8, C, 1024), BF16),
            pltpu.VMEM((1024, 1024), BF16),
            pltpu.VMEM((8, 256, 256), BF16),
            pltpu.VMEM((4, 256, 384), BF16),
            pltpu.VMEM((LANE, 256), BF16),
            pltpu.VMEM((1024, LANE), BF16),
            pltpu.VMEM((512, LANE), BF16),
            pltpu.VMEM((8, C, 1024), BF16),
            pltpu.VMEM((8, C, 1024), BF16),
            pltpu.VMEM((8, 3 * C, 1280), BF16),
            pltpu.VMEM((10, C, 1024), F32),
            pltpu.VMEM((8, C, 1024), BF16),
            pltpu.VMEM((4, C, 512), BF16),
            pltpu.VMEM((4, 3 * C, 1024), BF16),
            pltpu.VMEM((6, C, 768), F32),
            pltpu.VMEM((6, C, 512), F32),
            pltpu.VMEM((4, C, 512), F32),
            pltpu.VMEM((4, C, 512), BF16),
            pltpu.VMEM((4, C, 768), F32),
            pltpu.VMEM((4, 2 * C, 512), BF16),
            pltpu.VMEM((4, C, 768), BF16),
            pltpu.VMEM((6, C, 512), BF16),
            pltpu.VMEM((4, 3 * C, 768), BF16),
            pltpu.VMEM((4, 2 * C, 512), BF16),
            pltpu.VMEM((10, C, 1024), BF16),
            pltpu.VMEM((8, 3 * C, 1280), BF16),
            pltpu.VMEM((8, C, 1024), BF16),
            pltpu.VMEM((3 * C, 9 * C), F32),
            pltpu.VMEM((3 * C, 9 * C), F32),
            pltpu.VMEM((4, C, LANE), BF16),
            pltpu.VMEM((2, 2, 8, C, LANE), BF16),
            pltpu.VMEM((2, 4, C, LANE), BF16),
            pltpu.VMEM((2, 4, C, LANE), BF16),
            pltpu.VMEM((2, 4, C, LANE), BF16),
            pltpu.VMEM((4, 6, C, LANE), BF16),
            pltpu.VMEM((ROWS_A, LANE), BF16),
            pltpu.VMEM((NY, ROWS_A // NY, LANE), BF16),
            pltpu.VMEM((2, ROWS_A // NY, LANE), BF16),
            pltpu.VMEM((NX, ROWS_A // NY, LANE), BF16),
            pltpu.VMEM((ROWS_B, LANE), BF16),
            pltpu.VMEM((NY, ROWS_B // NY, LANE), BF16),
            pltpu.VMEM((2, ROWS_B // NY, LANE), BF16),
            pltpu.VMEM((NX, ROWS_B // NY, LANE), BF16),
            pltpu.SemaphoreType.DMA((6,)),
            pltpu.SemaphoreType.DMA((4, 8)),
            pltpu.SemaphoreType.DMA((4, 8)),
            pltpu.SemaphoreType.DMA((2, 3, NX)),
            pltpu.SemaphoreType.DMA((2, 3, NX)),
        ],
        compiler_params=pltpu.CompilerParams(
            collective_id=0, has_side_effects=True, vmem_limit_bytes=50 * 1024 * 1024
        ),
        name="section",
    )(
        pltpu.with_memory_space_constraint(block_slots.reshape(1, SLOTS), pltpu.HBM),
        block_count.reshape(1, 1),
        *(
            pltpu.with_memory_space_constraint(value, pltpu.HBM)
            for value in (
                features.reshape(blocks),
                cotangent.reshape(blocks),
                fine_weight.transpose(1, 0, 2),
                down_weight,
                coarse_weight.transpose(1, 0, 2),
                up_weight,
            )
        ),
    )
    out, ig, gf, gd, gc, gu = pl.pallas_call(
        unpack,
        out_shape=(
            block_shape,
            block_shape,
            jax.ShapeDtypeStruct(kernel_shape, F32),
            jax.ShapeDtypeStruct((C, 8, C), F32),
            jax.ShapeDtypeStruct(kernel_shape, F32),
            jax.ShapeDtypeStruct((8, C, C), F32),
        ),
        in_specs=[vmem, vmem, vmem, vmem],
        out_specs=(hbm,) * 6,
        scratch_shapes=[
            pltpu.VMEM(kernel_shape, F32),
            pltpu.VMEM((C, 8, C), F32),
            pltpu.VMEM(kernel_shape, F32),
            pltpu.VMEM((8, C, C), F32),
            pltpu.VMEM((8 * C, LANE), F32),
            pltpu.SemaphoreType.DMA((6,)),
        ],
        compiler_params=pltpu.CompilerParams(vmem_limit_bytes=8 * 1024 * 1024),
        name="unpack",
    )(sums_a, sums_b, out, ig)
    shape_out = (1, 1) + blocks
    gf, gc = gf.transpose(1, 0, 2), gc.transpose(1, 0, 2)
    return out.reshape(shape_out), ig.reshape(shape_out), gf, gd, gc, gu


def solution(mesh):
    split = P("gx", "gy", None, None, None)
    return jax.shard_map(
        on_device,
        mesh=mesh,
        in_specs=(split, P("gx", "gy", None), P("gx", "gy"), split, P(), P(), P(), P()),
        out_specs=(split, split, P(), P(), P(), P()),
        check_vma=False,
    )
```

```python
import math

import jax
import jax.numpy as jnp
from jax import lax
from jax.experimental import pallas as pl
from jax.experimental.pallas import tpu as pltpu
from jax.sharding import PartitionSpec as P

C = 48
SLOTS = 16
LANE = 128
NX = 16
NY = 16
ROWS_A = 512
ROWS_B = 768
F32 = jnp.float32
BF16 = jnp.bfloat16
MESH = pl.DeviceIdType.MESH


def dot(a, b):
    return jnp.dot(a, b, preferred_element_type=F32)


def dot_t(a, b):
    return lax.dot_general(a, b, (((1,), (1,)), ((), ())), preferred_element_type=F32)


def iota(shape, dim):
    return lax.broadcasted_iota(jnp.int32, shape, dim)


def one_hot(cond):
    return jnp.where(cond, 1.0, 0.0).astype(BF16)


def build_shift_fine(s_ref):
    row = iota((256, 256), 0)
    col = iota((256, 256), 1)
    lane = col % LANE
    right = col >= LANE
    before = jnp.where(lane < 64, lane + 63, lane - 64)
    after = jnp.where(lane < 64, lane + 64, lane - 63)
    before = jnp.where(lane == 0, -1, before)
    after = jnp.where(lane == 127, -1, after)
    source = jnp.where(right, after, before)
    place = jnp.where(lane == jnp.where(right, 127, 0), jnp.where(right, LANE + 8, LANE), -512)

    @pl.loop(0, 8)
    def _(x):
        s_ref[x] = one_hot((row == source) | (row == place + x))


def coarse_edge(group):
    return jnp.where(
        group == 0, 63, jnp.where(group == 1, 62, jnp.where(group == 2, 0, jnp.where(group == 3, 1, -1)))
    )


def build_shift_coarse(s_ref):
    row = iota((256, 384), 0)
    col = iota((256, 384), 1)
    source = (col % LANE + col // LANE + LANE - 1) % LANE
    halo = row - LANE
    spot = jnp.where(
        halo < 4, 127, jnp.where(halo < 8, 126, jnp.where(halo < 12, 64, jnp.where(halo < 16, 65, -1)))
    )
    own = (row < 64) & (row == source)
    other = (halo >= 0) & (spot == source)

    @pl.loop(0, 4)
    def _(x):
        s_ref[x] = one_hot(own | (other & (halo % 4 == x)))


def build_roll(r_ref):
    row = iota((LANE, 256), 0)
    col = iota((LANE, 256), 1)
    r_ref[...] = one_hot(row == (col % LANE + 2 * (col // LANE) + LANE - 1) % LANE)


def build_edges(fine_ref, coarse_ref):
    row = iota((1024, LANE), 0)
    col = iota((1024, LANE), 1)
    lane = row % LANE
    x = row // LANE
    fine_ref[...] = one_hot(((lane == 127) & (col == x)) | ((lane == 0) & (col == x + 8)))
    row = iota((512, LANE), 0)
    col = iota((512, LANE), 1)
    coarse_ref[...] = one_hot((row % LANE == coarse_edge(col // 4)) & (row // LANE == col % 4))


def build_places(e_ref, slots_ref, live_count):
    e_ref[...] = jnp.zeros_like(e_ref)
    row = iota((16, 256), 0)
    col = iota((16, 256), 1)
    y = row % 8
    own = (row // 8) == (col // LANE)
    spot = col % LANE - 64 * (y % 2) - y // 2

    @pl.loop(0, SLOTS)
    def _(s):
        place = jnp.where(s < live_count, slots_ref[0, s], 4096)
        tile = one_hot(own & (spot == 4 * place))
        for j in range(4):
            e_ref[pl.ds(pl.multiple_of(64 * s + 16 * j, 16), 16), 256 * j : 256 * j + 256] = tile


def live_lanes(slots_ref, live_count):
    spot = (iota((8, LANE), 1) % 64) // 4

    def step(s, total):
        place = jnp.where(s < live_count, slots_ref[0, s], 4096)
        return total + jnp.where(spot == place, 1.0, 0.0)

    return lax.fori_loop(0, SLOTS, step, jnp.zeros((8, LANE), F32))


def to_grid(blocks, work, e_ref, grid, after_outer=None):
    for t in range(8):
        lanes = slice(t * LANE, (t + 1) * LANE)
        for pair in range(4):
            one = blocks[2 * t, :, pair * LANE : (pair + 1) * LANE]
            two = blocks[2 * t + 1, :, pair * LANE : (pair + 1) * LANE]
            work[2 * pair, :, lanes] = jnp.concatenate([one[:, :64], two[:, :64]], axis=1)
            work[2 * pair + 1, :, lanes] = jnp.concatenate([one[:, 64:], two[:, 64:]], axis=1)

    for n in (0, 3, 1, 2):
        if n == 1 and after_outer is not None:
            after_outer()
        lanes = slice(n * 256, (n + 1) * 256)
        moved = dot(work[...].reshape(8 * C, 1024), e_ref[:, lanes])
        grid[:, :, lanes] = moved.astype(BF16).reshape(8, C, 256)


def to_blocks(grid, e_ref, blocks):
    for n in range(4):
        rows = slice(n * 256, (n + 1) * 256)
        moved = dot_t(grid[...].reshape(8 * C, 1024), e_ref[rows, :])
        moved = moved.astype(BF16).reshape(8, C, 256)
        for pair in range(4):
            for k in range(4):
                low = moved[2 * pair, :, 64 * k : 64 * k + 64]
                high = moved[2 * pair + 1, :, 64 * k : 64 * k + 64]
                blocks[4 * n + k, :, pair * LANE : (pair + 1) * LANE] = jnp.concatenate(
                    [low, high], axis=1
                )


def pack_edges(grid, depth, t_ref, packed):
    edges = dot(grid.reshape(depth * C, grid.shape[2]), t_ref[...]).reshape(depth, C, LANE)
    total = edges[0]
    for z in range(1, depth):
        total = total + pltpu.roll(edges[z], 16 * z, 1)
    packed[...] = total.astype(BF16)


def unpack_edges(received, row, left_ok, right_ok, depth):
    lane = iota((C, LANE), 1) % 16
    left = jnp.where(left_ok, received[2 * row].astype(F32), 0.0)
    right = jnp.where(right_ok, received[2 * row + 1].astype(F32), 0.0)
    both = jnp.where(lane < 8, left, right)
    parts = [both] + [pltpu.roll(both, LANE - 16 * z, 1) for z in range(1, depth)]
    return jnp.stack(parts, axis=0).astype(BF16).reshape(depth * C, LANE)


def widen(grid, sides, received, s_ref, wide, count, depth, place):
    gx, gy = place
    low_ok, high_ok = gx > 0, gx < NX - 1
    left_ok, right_ok = gy > 0, gy < NY - 1

    def put(rows, halo, x, lanes):
        moved = dot(jnp.concatenate([rows, halo], axis=1), s_ref[x]).astype(BF16)
        wide[:, 0:C, lanes] = moved[:, :LANE].reshape(depth, C, LANE)
        wide[:, C : 2 * C, lanes] = rows.reshape(depth, C, LANE)
        wide[:, 2 * C : 3 * C, lanes] = moved[:, LANE:].reshape(depth, C, LANE)

    zero = jnp.zeros((depth * C, LANE), BF16)
    halo = unpack_edges(received, 0, left_ok & low_ok, right_ok & low_ok, depth)
    rows = jnp.where(low_ok, sides[0].reshape(depth * C, LANE), zero)
    put(rows, halo, count - 1, pl.ds(0, LANE))
    halo = unpack_edges(received, 2, left_ok & high_ok, right_ok & high_ok, depth)
    rows = jnp.where(high_ok, sides[1].reshape(depth * C, LANE), zero)
    put(rows, halo, 0, pl.ds((count + 1) * LANE, LANE))
    halo = unpack_edges(received, 1, left_ok, right_ok, depth)

    for x in range(count):
        rows = grid[:, :, x * LANE : (x + 1) * LANE].reshape(depth * C, LANE)
        put(rows, halo, x, pl.ds((x + 1) * LANE, LANE))


def coarse_halos(received, place):
    gx, gy = place
    left_ok, right_ok = gy > 0, gy < NY - 1
    low_ok, high_ok = gx > 0, gx < NX - 1
    return (
        unpack_edges(received, 0, left_ok & low_ok, right_ok & low_ok, 4),
        unpack_edges(received, 1, left_ok, right_ok, 4),
        unpack_edges(received, 2, left_ok & high_ok, right_ok & high_ok, 4),
    )


def widen_coarse(grid, sides, received, s_ref, wide, place):
    gx = place[0]
    halos = coarse_halos(received, place)
    zero = jnp.zeros((4 * C, LANE), BF16)
    halves = []
    for side, inside in ((0, gx > 0), (1, gx < NX - 1)):
        rows = jnp.where(inside, sides[side].reshape(4 * C, LANE), zero)
        halves.append([rows, pltpu.roll(rows.astype(F32), 64, 1).astype(BF16)])
    for column in range(8):
        if column < 2:
            rows, halo, x = halves[0][column], halos[0], column + 2
        elif column < 6:
            x = column - 2
            rows = grid[:, :, x * LANE : (x + 1) * LANE].reshape(4 * C, LANE)
            halo = halos[1]
        else:
            x = column - 6
            rows, halo = halves[1][x], halos[2]
        moved = dot(jnp.concatenate([rows, halo], axis=1), s_ref[x]).astype(BF16)
        for t in range(3):
            part = moved[:, t * LANE : (t + 1) * LANE].reshape(4, C, LANE)
            wide[:, t * C : (t + 1) * C, column * LANE : (column + 1) * LANE] = part


def extend_grect(grect, sides, received, s_ref, wide, place):
    gx = place[0]
    halos = coarse_halos(received, place)
    zero = jnp.zeros((4 * C, LANE), F32)
    for column in range(6):
        if column == 0:
            rows = jnp.where(gx > 0, sides[0].reshape(4 * C, LANE).astype(F32), zero)
            halo, x = halos[0], 3
        elif column < 5:
            x = column - 1
            rows = grect[:, :, x * LANE : (x + 1) * LANE].reshape(4 * C, LANE)
            halo = halos[1]
        else:
            rows = jnp.where(gx < NX - 1, sides[1].reshape(4 * C, LANE).astype(F32), zero)
            halo, x = halos[2], 0
        total = rows + dot(halo, s_ref[x, LANE:, LANE : 2 * LANE])
        wide[:, :, column * LANE : (column + 1) * LANE] = total.reshape(4, C, LANE)


def roll_columns(grid, r_ref, wide):
    for column in range(6):
        lanes = slice(column * LANE, (column + 1) * LANE)
        rows = grid[:, :, lanes]
        moved = dot(rows.reshape(4 * C, LANE), r_ref[...]).astype(BF16)
        wide[:, 0:C, lanes] = moved[:, :LANE].reshape(4, C, LANE)
        wide[:, C : 2 * C, lanes] = rows
        wide[:, 2 * C : 3 * C, lanes] = moved[:, LANE:].reshape(4, C, LANE)


def window(wide, z, first, width):
    return jnp.concatenate(
        [wide[z, :, first + dx * LANE : first + dx * LANE + width] for dx in range(3)], axis=0
    )


def convolve(wide, weight, total, depth, width):
    total[...] = jnp.zeros_like(total)
    for z in range(depth):
        for first in range(0, width, 256):
            piece = dot(weight[...], window(wide, z, first, 256)).reshape(3, C, 256)
            lanes = slice(first, first + 256)
            total[z : z + 3, :, lanes] = total[z : z + 3, :, lanes] + piece


def kernel_terms(grad, wide, total, depth, width, start):
    ahead = [grad[z : z + 3].reshape(3 * C, width) for z in range(depth)]
    pieces = [window(wide, z, start, width) for z in range(depth)]
    total[...] = dot_t(jnp.concatenate(ahead, axis=1), jnp.concatenate(pieces, axis=1))


def quarters(grid, wz):
    columns = []
    for a in range(2):
        for b in range(2):
            columns.append(
                jnp.concatenate(
                    [
                        grid[2 * wz + a, :, (2 * wx + b) * LANE : (2 * wx + b + 1) * LANE]
                        for wx in range(4)
                    ],
                    axis=1,
                )
            )
    return jnp.concatenate(columns, axis=0)


def tile_lanes(mask, rows, width):
    return jnp.broadcast_to(jnp.concatenate([mask] * (width // LANE), axis=1)[0:1], (rows, width))


def roll_half(value):
    parts = [
        pltpu.roll(value[:, k * LANE : (k + 1) * LANE], 64, 1) for k in range(value.shape[1] // LANE)
    ]
    return jnp.concatenate(parts, axis=1)


def kernel_rows(weight, stack, eye, forward, backward):
    for dz in range(3):
        for k in range(9):
            block = weight[9 * dz + k]
            forward[(2 - dz) * C : (3 - dz) * C, k * C : (k + 1) * C] = block
            stack[(8 - k) * C : (9 - k) * C, :] = block
        backward[dz * C : (dz + 1) * C, :] = dot_t(eye[0:C, 0:C], stack[...]).astype(BF16)


def step_rows(down, up, stage, eye, ddn, dga, uup, ugr):
    for o in range(C):
        stage[8 * o : 8 * o + 8, 0:C] = down[o].astype(F32)
    for k in range(4):
        for e in range(2):
            q = 2 * k + e
            block = stage[pl.ds(q, C, stride=8), :].astype(BF16)[:, 0:C]
            ddn[e * C : (e + 1) * C, k * C : (k + 1) * C] = block
            uup[k * C : (k + 1) * C, e * C : (e + 1) * C] = up[q]
    dga[...] = dot_t(eye[...], ddn[...]).astype(BF16)
    ugr[...] = dot_t(eye[0 : 2 * C, 0 : 2 * C], uup[...]).astype(BF16)


def slope(value):
    sigma = jax.nn.sigmoid(value)
    return sigma * (1.0 + value * (1.0 - sigma))


def section(
    slots_ref,
    count_ref,
    feat_hbm,
    cot_hbm,
    fine_hbm,
    down_hbm,
    coarse_hbm,
    up_hbm,
    blocks_out,
    blocks_ig,
    sums_a,
    sums_b,
    feat,
    cot_in,
    fine_w,
    down_w,
    coarse_w,
    up_w,
    stage,
    stack,
    eye,
    wf,
    wfb,
    wc,
    wcb,
    ddn,
    dga,
    uup,
    ugr,
    work,
    places,
    shift_f,
    shift_c,
    roll_c,
    edge_f,
    edge_c,
    fine,
    cot,
    fine3,
    hidden,
    act,
    low,
    low3,
    coarse,
    coarse2,
    grect,
    grect_low,
    grect_wide,
    rect2,
    gcoarse,
    gcoarse_own,
    gcoarse3,
    gdown2,
    ghid,
    ghid3,
    result,
    term_f,
    term_c,
    packed,
    sides_f,
    outer,
    sides_c,
    sides_g,
    edges_in,
    grads_a,
    first_in_a,
    chunk_a,
    second_in_a,
    grads_b,
    first_in_b,
    chunk_b,
    second_in_b,
    local_sem,
    send_sem,
    recv_sem,
    sum_send,
    sum_recv,
):
    gx = lax.axis_index("gx")
    gy = lax.axis_index("gy")
    here = (gx, gy)

    load_feat = pltpu.make_async_copy(feat_hbm, feat, local_sem.at[5])
    load_feat.start()
    loads = [
        pltpu.make_async_copy(source, target, local_sem.at[k])
        for k, (source, target) in enumerate(
            (
                (fine_hbm, fine_w),
                (down_hbm, down_w),
                (coarse_hbm, coarse_w),
                (up_hbm, up_w),
                (cot_hbm, cot_in),
            )
        )
    ]
    for load in loads:
        load.start()

    barrier = pltpu.get_barrier_semaphore()

    @pl.loop(1, NX)
    def _(d):
        pl.semaphore_signal(
            barrier, inc=1, device_id=(lax.rem(gx + d, NX), gy), device_id_type=MESH
        )
        pl.semaphore_signal(
            barrier, inc=1, device_id=(gx, lax.rem(gy + d, NY)), device_id_type=MESH
        )

    for dx in (1, NX - 1):
        for dy in (1, NY - 1):
            pl.semaphore_signal(
                barrier,
                inc=1,
                device_id=(lax.rem(gx + dx, NX), lax.rem(gy + dy, NY)),
                device_id_type=MESH,
            )

    live_count = count_ref[0, 0]
    build_places(places, slots_ref, live_count)
    build_edges(edge_f, edge_c)
    live = live_lanes(slots_ref, live_count)
    half_live = jnp.where(iota((8, LANE), 1) < 64, live, 0.0)
    lower = jnp.where(iota((8, LANE), 1) < 64, 1.0, 0.0)

    def exchange_edges(step):
        copies = []
        for row in (0, 2, 1):
            for side in range(2):
                copies.append(
                    pltpu.make_async_remote_copy(
                        src_ref=packed.at[step],
                        dst_ref=edges_in.at[step, 2 * row + side],
                        send_sem=send_sem.at[step, 2 + 2 * row + side],
                        recv_sem=recv_sem.at[step, 2 + 2 * row + side],
                        device_id=(
                            lax.rem(gx + NX + 1 - row, NX),
                            lax.rem(gy + (1 if side == 0 else NY - 1), NY),
                        ),
                        device_id_type=MESH,
                    )
                )
        for copy in copies:
            copy.start()
        return copies

    def exchange_sides(step, sources, sides):
        copies = []
        for side in range(2):
            copies.append(
                pltpu.make_async_remote_copy(
                    src_ref=sources[side],
                    dst_ref=sides.at[side],
                    send_sem=send_sem.at[step, side],
                    recv_sem=recv_sem.at[step, side],
                    device_id=(lax.rem(gx + (1 if side == 0 else NX - 1), NX), gy),
                    device_id_type=MESH,
                )
            )
        for copy in copies:
            copy.start()
        return copies

    def outer_columns(source, length):
        return [source.at[:, :, pl.ds(first, LANE)] for first in (length - LANE, 0)]

    def reduction(grads, first_in, chunk, second_in, sums, part, steps):
        rows = chunk.shape[1]

        def chunk_rows(index):
            return pl.ds(pl.multiple_of(index * rows, rows), rows)

        def first(d):
            peer = lax.rem(gy + d, NY)
            return pltpu.make_async_remote_copy(
                src_ref=grads.at[chunk_rows(peer)],
                dst_ref=first_in.at[d],
                send_sem=sum_send.at[part, 0, d],
                recv_sem=sum_recv.at[part, 0, d],
                device_id=(gx, peer),
                device_id_type=MESH,
            )

        def second(d):
            return pltpu.make_async_remote_copy(
                src_ref=chunk.at[0],
                dst_ref=second_in.at[d],
                send_sem=sum_send.at[part, 1, d],
                recv_sem=sum_recv.at[part, 1, d],
                device_id=(lax.rem(gx + d, NX), gy),
                device_id_type=MESH,
            )

        def second_x(d):
            x = lax.rem(gx, 4)
            return pltpu.make_async_remote_copy(
                src_ref=chunk.at[0],
                dst_ref=second_in.at[d],
                send_sem=sum_send.at[part, 1, d],
                recv_sem=sum_recv.at[part, 1, d],
                device_id=(gx - x + lax.rem(x + d, 4), gy),
                device_id_type=MESH,
            )

        def second_z(d):
            return pltpu.make_async_remote_copy(
                src_ref=chunk.at[2],
                dst_ref=second_in.at[4 + d],
                send_sem=sum_send.at[part, 1, 4 + d],
                recv_sem=sum_recv.at[part, 1, 4 + d],
                device_id=(lax.rem(gx + 4 * d, NX), gy),
                device_id_type=MESH,
            )

        def third(d):
            return pltpu.make_async_remote_copy(
                src_ref=chunk.at[1],
                dst_ref=sums.at[chunk_rows(gy)],
                send_sem=sum_send.at[part, 2, d],
                recv_sem=sum_recv.at[part, 2, d],
                device_id=(gx, lax.rem(gy + d, NY)),
                device_id_type=MESH,
            )

        def start_first():
            start_all(first)

        def start_second():
            wait_all(first)
            own = grads[chunk_rows(gy), :].astype(F32)
            for d in range(1, NY):
                own = own + first_in[d].astype(F32)
            chunk[0] = own.astype(BF16)
            if steps == 1:
                start_all(second)
            else:
                start_all(second_x, 4)
            return own

        def start_middle(own):
            wait_all(second_x, 4)
            for d in range(1, 4):
                own = own + second_in[d].astype(F32)
            chunk[2] = own.astype(BF16)
            start_all(second_z, 4)
            return own

        def start_third(own):
            if steps == 1:
                wait_all(second)
                received = range(1, NX)
            else:
                wait_all(second_z, 4)
                received = range(5, 8)
            for d in received:
                own = own + second_in[d].astype(F32)
            chunk[1] = own.astype(BF16)
            start_all(third)
            sums[chunk_rows(gy), :] = chunk[1]

        def finish():
            wait_all(third)

        return start_first, start_second, start_middle, start_third, finish

    def start_all(copy, count=NX):
        @pl.loop(1, count)
        def _(d):
            copy(d).start()

    def wait_all(copy, count=NX):
        @pl.loop(1, count)
        def _(d):
            copy(d).wait()

    def put_rows(grads, term):
        for k in range(3):
            grads[3 * C * k : 3 * C * (k + 1), :] = term[:, k * LANE : (k + 1) * LANE].astype(BF16)
        tail = term[:, 3 * LANE :]
        grads[9 * C : 9 * C + 72, 0:C] = tail[0:72].astype(BF16)
        grads[9 * C : 9 * C + 72, C : 2 * C] = tail[72:144].astype(BF16)

    load_feat.wait()
    copies = []

    def send_sides():
        pl.semaphore_wait(barrier, 2 * (NX - 1) + 4)
        copies.extend(exchange_sides(0, outer_columns(fine, 1024), sides_f.at[0]))

    to_grid(feat, work, places, fine, send_sides)
    pack_edges(fine[...], 8, edge_f, packed.at[0])
    copies = copies + exchange_edges(0)

    for load in loads:
        load.wait()
    build_shift_coarse(shift_c)
    to_grid(cot_in, work, places, cot)
    eye[...] = one_hot(iota((4 * C, 4 * C), 0) == iota((4 * C, 4 * C), 1))
    stage[...] = jnp.zeros_like(stage)
    step_rows(down_w, up_w, stage, eye, ddn, dga, uup, ugr)
    lower_mask = tile_lanes(lower, C, 512)
    for wz in range(4):
        both = dot(ugr[...], quarters(cot, wz))
        value = (both[:C] + roll_half(both[C:])) * lower_mask
        grect[wz] = value
        grect_low[wz] = value.astype(BF16)
    pack_edges(grect_low[...], 4, edge_c, packed.at[2])
    build_shift_fine(shift_f)
    kernel_rows(fine_w, stack, eye, wf, wfb)

    for copy in copies:
        copy.wait()
    grect_copies = exchange_edges(2) + exchange_sides(2, outer_columns(grect_low, 512), sides_g)
    widen(fine, sides_f.at[0], edges_in.at[0], shift_f, fine3, 8, 8, here)
    convolve(fine3, wf, hidden, 8, 1024)

    live_fine = tile_lanes(live, C, 1024)
    for z in range(8):
        value = hidden[z + 1] * live_fine
        hidden[z + 1] = value
        act[z] = (value * jax.nn.sigmoid(value)).astype(BF16)

    for wz in range(4):
        both = dot(ddn[...], quarters(act, wz))
        value = (both[:C] + roll_half(both[C:])) * lower_mask
        low[wz] = value.astype(BF16)
        for side, first in ((0, 2 * LANE), (1, 0)):
            second = pltpu.roll(value[:, first + LANE : first + 2 * LANE], 64, 1)
            outer[side, wz] = (value[:, first : first + LANE] + second).astype(BF16)

    copies = exchange_sides(1, [outer.at[0], outer.at[1]], sides_c)
    pack_edges(low[...], 4, edge_c, packed.at[1])
    copies = copies + exchange_edges(1)
    build_roll(roll_c)
    kernel_rows(coarse_w, stack, eye, wc, wcb)
    grads_a[...] = jnp.zeros_like(grads_a)
    grads_b[...] = jnp.zeros_like(grads_b)
    gcoarse_own[...] = jnp.zeros_like(gcoarse_own)
    for copy in grect_copies:
        copy.wait()
    extend_grect(grect, sides_g, edges_in.at[2], shift_c, grect_wide, here)
    for copy in copies:
        copy.wait()
    widen_coarse(low, sides_c, edges_in.at[1], shift_c, low3, here)
    convolve(low3, wc, coarse, 4, 768)

    for wz in range(4):
        value = coarse[wz + 1]
        grad = grect_wide[wz] * slope(value)
        gcoarse[wz] = grad.astype(BF16)
        gcoarse_own[wz + 1] = (grad[:, LANE : 5 * LANE] * lower_mask).astype(BF16)
        value = value[:, LANE : 5 * LANE]
        rect = value * jax.nn.sigmoid(value) * lower_mask
        rect2[wz, 0:C] = rect.astype(BF16)
        rect2[wz, C : 2 * C] = roll_half(rect).astype(BF16)

    roll_columns(gcoarse, roll_c, gcoarse3)
    convolve(gcoarse3, wcb, coarse2, 4, 512)

    live_coarse = tile_lanes(half_live, C, 512)
    ghid[0] = jnp.zeros((C, 1024), BF16)
    ghid[9] = jnp.zeros((C, 1024), BF16)
    for wz in range(4):
        value = coarse2[wz + 1] * live_coarse
        gdown2[wz, 0:C] = value.astype(BF16)
        gdown2[wz, C : 2 * C] = roll_half(value).astype(BF16)
        back = dot(dga[...], gdown2[wz])
        for a in range(2):
            for b in range(2):
                k = 2 * a + b
                for wx in range(4):
                    lanes = pl.ds((2 * wx + b) * LANE, LANE)
                    piece = back[k * C : (k + 1) * C, wx * LANE : (wx + 1) * LANE]
                    ghid[2 * wz + a + 1, :, lanes] = (
                        cot[2 * wz + a, :, lanes].astype(F32)
                        + piece * slope(hidden[2 * wz + a + 1, :, lanes])
                    ).astype(BF16)

    first_a, second_a, _, third_a, finish_a = reduction(
        grads_a, first_in_a, chunk_a, second_in_a, sums_a, 0, 1
    )
    first_b, second_b, middle_b, third_b, finish_b = reduction(
        grads_b, first_in_b, chunk_b, second_in_b, sums_b, 1, 2
    )
    kernel_terms(gcoarse_own, low3, term_c, 4, 512, LANE)
    total_u = jnp.zeros((4 * C, 2 * C), F32)
    total_d = jnp.zeros((2 * C, 4 * C), F32)
    for wz in range(4):
        total_u = total_u + dot_t(quarters(cot, wz), rect2[wz])
        total_d = total_d + dot_t(gdown2[wz], quarters(act, wz))
    put_rows(grads_b, term_c)
    low_d = total_d[:, 0:LANE].astype(BF16)
    high_d = total_d[:, LANE:192].astype(BF16)
    grads_b[512:704, 0 : 2 * C] = total_u.astype(BF16)
    grads_b[512:608, 96:LANE] = high_d[:, 0:32]
    grads_b[608:704, 96:LANE] = high_d[:, 32:64]
    grads_b[704:768, :] = low_d[0:64]
    grads_b[432:464, 96:LANE] = low_d[64:96, 0:32]
    grads_b[464:496, 96:LANE] = low_d[64:96, 32:64]
    grads_a[432:464, 96:LANE] = low_d[64:96, 64:96]
    grads_a[464:496, 96:LANE] = low_d[64:96, 96:LANE]
    first_b()
    kernel_terms(ghid, fine3, term_f, 8, 1024, 0)
    put_rows(grads_a, term_f)
    first_a()
    pack_edges(ghid[1:9], 8, edge_f, packed.at[3])
    copies = exchange_edges(3)
    copies = copies + exchange_sides(3, outer_columns(ghid.at[pl.ds(1, 8)], 1024), sides_f.at[1])

    for wz in range(4):
        upward = dot(uup[...], rect2[wz])
        for a in range(2):
            for b in range(2):
                k = 2 * a + b
                for wx in range(4):
                    lanes = pl.ds((2 * wx + b) * LANE, LANE)
                    piece = upward[k * C : (k + 1) * C, wx * LANE : (wx + 1) * LANE]
                    result[2 * wz + a, :, lanes] = (
                        hidden[2 * wz + a + 1, :, lanes] + piece
                    ).astype(BF16)
    to_blocks(result, places, blocks_out)
    own_b = second_b()
    own_a = second_a()
    own_b = middle_b(own_b)

    for copy in copies:
        copy.wait()
    widen(ghid.at[pl.ds(1, 8)], sides_f.at[1], edges_in.at[3], shift_f, ghid3, 8, 8, here)
    convolve(ghid3, wfb, hidden, 8, 1024)
    for z in range(8):
        result[z] = hidden[z + 1].astype(BF16)
    to_blocks(result, places, blocks_ig)

    third_b(own_b)
    third_a(own_a)
    finish_b()
    finish_a()


def unpack(
    sums_a,
    sums_b,
    out_in,
    ig_in,
    out_hbm,
    ig_hbm,
    gf_hbm,
    gd_hbm,
    gc_hbm,
    gu_hbm,
    gf,
    gd,
    gc,
    gu,
    stage,
    sem,
):
    copies = [
        pltpu.make_async_copy(source, target, sem.at[k])
        for k, (source, target) in enumerate(
            (
                (gf, gf_hbm),
                (gc, gc_hbm),
                (gu, gu_hbm),
                (gd, gd_hbm),
                (out_in, out_hbm),
                (ig_in, ig_hbm),
            )
        )
    ]
    copies[4].start()
    copies[5].start()
    scale = 1.0 / math.sqrt(SLOTS * 512 * NX * NY)

    for part, (sums, target) in enumerate(((sums_a, gf), (sums_b, gc))):
        tail = sums[9 * C : 9 * C + 80, :].astype(F32)
        tail = jnp.concatenate([tail[0:72, 0:C], tail[0:72, C : 2 * C]], axis=0)
        rows = jnp.concatenate(
            [sums[3 * C * k : 3 * C * (k + 1), :].astype(F32) for k in range(3)] + [tail], axis=1
        )
        rows = rows * scale
        for dz in range(3):
            for k in range(9):
                block = rows[(2 - dz) * C : (3 - dz) * C, k * C : (k + 1) * C]
                target[9 * dz + k] = block
        copies[part].start()
    for k in range(4):
        for e in range(2):
            block = sums_b[512 + k * C : 512 + (k + 1) * C, e * C : (e + 1) * C]
            gu[2 * k + e] = block.astype(F32) * scale
    copies[2].start()
    last = jnp.concatenate(
        [
            sums[first : first + 32, 96:LANE].astype(F32)
            for sums in (sums_b, sums_a)
            for first in (432, 464)
        ],
        axis=1,
    )
    low = jnp.concatenate([sums_b[704:768, :].astype(F32), last], axis=0)
    high = jnp.concatenate(
        [sums_b[512:608, 96:LANE].astype(F32), sums_b[608:704, 96:LANE].astype(F32)], axis=1
    )
    rows = jnp.concatenate([low, high], axis=1) * scale
    for k in range(4):
        for e in range(2):
            block = rows[e * C : (e + 1) * C, k * C : (k + 1) * C]
            stage[pl.ds(2 * k + e, C, stride=8), :] = jnp.concatenate(
                [block, jnp.zeros((C, LANE - C), F32)], axis=1
            )
    for o in range(C):
        gd[o] = stage[8 * o : 8 * o + 8, 0:C]
    copies[3].start()
    for copy in copies:
        copy.wait()


def on_device(
    features, block_slots, block_count, cotangent, fine_weight, down_weight, coarse_weight, up_weight
):
    vmem = pl.BlockSpec(memory_space=pltpu.VMEM)
    smem = pl.BlockSpec(memory_space=pltpu.SMEM)
    hbm = pl.BlockSpec(memory_space=pltpu.HBM)
    blocks = (SLOTS, C, 512)
    kernel_shape = (27, C, C)
    block_shape = jax.ShapeDtypeStruct(blocks, BF16)
    out, ig, sums_a, sums_b = pl.pallas_call(
        section,
        out_shape=(
            block_shape,
            block_shape,
            jax.ShapeDtypeStruct((ROWS_A, LANE), BF16),
            jax.ShapeDtypeStruct((ROWS_B, LANE), BF16),
        ),
        in_specs=[smem, smem] + [hbm] * 6,
        out_specs=(vmem, vmem, vmem, vmem),
        scratch_shapes=[
            pltpu.VMEM(blocks, BF16),
            pltpu.VMEM(blocks, BF16),
            pltpu.VMEM(kernel_shape, BF16),
            pltpu.VMEM((C, 8, C), BF16),
            pltpu.VMEM(kernel_shape, BF16),
            pltpu.VMEM((8, C, C), BF16),
            pltpu.VMEM((8 * C, LANE), F32),
            pltpu.VMEM((9 * C, C), BF16),
            pltpu.VMEM((4 * C, 4 * C), BF16),
            pltpu.VMEM((3 * C, 9 * C), BF16),
            pltpu.VMEM((3 * C, 9 * C), BF16),
            pltpu.VMEM((3 * C, 9 * C), BF16),
            pltpu.VMEM((3 * C, 9 * C), BF16),
            pltpu.VMEM((2 * C, 4 * C), BF16),
            pltpu.VMEM((4 * C, 2 * C), BF16),
            pltpu.VMEM((4 * C, 2 * C), BF16),
            pltpu.VMEM((2 * C, 4 * C), BF16),
            pltpu.VMEM((8, C, 1024), BF16),
            pltpu.VMEM((1024, 1024), BF16),
            pltpu.VMEM((8, 256, 256), BF16),
            pltpu.VMEM((4, 256, 384), BF16),
            pltpu.VMEM((LANE, 256), BF16),
            pltpu.VMEM((1024, LANE), BF16),
            pltpu.VMEM((512, LANE), BF16),
            pltpu.VMEM((8, C, 1024), BF16),
            pltpu.VMEM((8, C, 1024), BF16),
            pltpu.VMEM((8, 3 * C, 1280), BF16),
            pltpu.VMEM((10, C, 1024), F32),
            pltpu.VMEM((8, C, 1024), BF16),
            pltpu.VMEM((4, C, 512), BF16),
            pltpu.VMEM((4, 3 * C, 1024), BF16),
            pltpu.VMEM((6, C, 768), F32),
            pltpu.VMEM((6, C, 512), F32),
            pltpu.VMEM((4, C, 512), F32),
            pltpu.VMEM((4, C, 512), BF16),
            pltpu.VMEM((4, C, 768), F32),
            pltpu.VMEM((4, 2 * C, 512), BF16),
            pltpu.VMEM((4, C, 768), BF16),
            pltpu.VMEM((6, C, 512), BF16),
            pltpu.VMEM((4, 3 * C, 768), BF16),
            pltpu.VMEM((4, 2 * C, 512), BF16),
            pltpu.VMEM((10, C, 1024), BF16),
            pltpu.VMEM((8, 3 * C, 1280), BF16),
            pltpu.VMEM((8, C, 1024), BF16),
            pltpu.VMEM((3 * C, 9 * C), F32),
            pltpu.VMEM((3 * C, 9 * C), F32),
            pltpu.VMEM((4, C, LANE), BF16),
            pltpu.VMEM((2, 2, 8, C, LANE), BF16),
            pltpu.VMEM((2, 4, C, LANE), BF16),
            pltpu.VMEM((2, 4, C, LANE), BF16),
            pltpu.VMEM((2, 4, C, LANE), BF16),
            pltpu.VMEM((4, 6, C, LANE), BF16),
            pltpu.VMEM((ROWS_A, LANE), BF16),
            pltpu.VMEM((NY, ROWS_A // NY, LANE), BF16),
            pltpu.VMEM((2, ROWS_A // NY, LANE), BF16),
            pltpu.VMEM((NX, ROWS_A // NY, LANE), BF16),
            pltpu.VMEM((ROWS_B, LANE), BF16),
            pltpu.VMEM((NY, ROWS_B // NY, LANE), BF16),
            pltpu.VMEM((3, ROWS_B // NY, LANE), BF16),
            pltpu.VMEM((NX, ROWS_B // NY, LANE), BF16),
            pltpu.SemaphoreType.DMA((6,)),
            pltpu.SemaphoreType.DMA((4, 8)),
            pltpu.SemaphoreType.DMA((4, 8)),
            pltpu.SemaphoreType.DMA((2, 3, NX)),
            pltpu.SemaphoreType.DMA((2, 3, NX)),
        ],
        compiler_params=pltpu.CompilerParams(
            collective_id=0, has_side_effects=True, vmem_limit_bytes=50 * 1024 * 1024
        ),
        name="section",
    )(
        pltpu.with_memory_space_constraint(block_slots.reshape(1, SLOTS), pltpu.HBM),
        block_count.reshape(1, 1),
        *(
            pltpu.with_memory_space_constraint(value, pltpu.HBM)
            for value in (
                features.reshape(blocks),
                cotangent.reshape(blocks),
                fine_weight.transpose(1, 0, 2),
                down_weight,
                coarse_weight.transpose(1, 0, 2),
                up_weight,
            )
        ),
    )
    out, ig, gf, gd, gc, gu = pl.pallas_call(
        unpack,
        out_shape=(
            block_shape,
            block_shape,
            jax.ShapeDtypeStruct(kernel_shape, F32),
            jax.ShapeDtypeStruct((C, 8, C), F32),
            jax.ShapeDtypeStruct(kernel_shape, F32),
            jax.ShapeDtypeStruct((8, C, C), F32),
        ),
        in_specs=[vmem, vmem, vmem, vmem],
        out_specs=(hbm,) * 6,
        scratch_shapes=[
            pltpu.VMEM(kernel_shape, F32),
            pltpu.VMEM((C, 8, C), F32),
            pltpu.VMEM(kernel_shape, F32),
            pltpu.VMEM((8, C, C), F32),
            pltpu.VMEM((8 * C, LANE), F32),
            pltpu.SemaphoreType.DMA((6,)),
        ],
        compiler_params=pltpu.CompilerParams(vmem_limit_bytes=8 * 1024 * 1024),
        name="unpack",
    )(sums_a, sums_b, out, ig)
    shape_out = (1, 1) + blocks
    gf, gc = gf.transpose(1, 0, 2), gc.transpose(1, 0, 2)
    return out.reshape(shape_out), ig.reshape(shape_out), gf, gd, gc, gu


def solution(mesh):
    split = P("gx", "gy", None, None, None)
    return jax.shard_map(
        on_device,
        mesh=mesh,
        in_specs=(split, P("gx", "gy", None), P("gx", "gy"), split, P(), P(), P(), P()),
        out_specs=(split, split, P(), P(), P(), P()),
        check_vma=False,
    )
```

```python
import math

import jax
import jax.numpy as jnp
from jax import lax
from jax.experimental import pallas as pl
from jax.experimental.pallas import tpu as pltpu
from jax.sharding import PartitionSpec as P

C = 48
SLOTS = 16
LANE = 128
NX = 16
NY = 16
ROWS_A = 512
ROWS_B = 768
F32 = jnp.float32
BF16 = jnp.bfloat16
MESH = pl.DeviceIdType.MESH


def dot(a, b):
    return jnp.dot(a, b, preferred_element_type=F32)


def dot_t(a, b):
    return lax.dot_general(a, b, (((1,), (1,)), ((), ())), preferred_element_type=F32)


def iota(shape, dim):
    return lax.broadcasted_iota(jnp.int32, shape, dim)


def one_hot(cond):
    return jnp.where(cond, 1.0, 0.0).astype(BF16)


def build_shift_fine(s_ref):
    row = iota((256, 256), 0)
    col = iota((256, 256), 1)
    lane = col % LANE
    right = col >= LANE
    before = jnp.where(lane < 64, lane + 63, lane - 64)
    after = jnp.where(lane < 64, lane + 64, lane - 63)
    before = jnp.where(lane == 0, -1, before)
    after = jnp.where(lane == 127, -1, after)
    source = jnp.where(right, after, before)
    place = jnp.where(lane == jnp.where(right, 127, 0), jnp.where(right, LANE + 8, LANE), -512)

    @pl.loop(0, 8)
    def _(x):
        s_ref[x] = one_hot((row == source) | (row == place + x))


def coarse_edge(group):
    return jnp.where(
        group == 0, 63, jnp.where(group == 1, 62, jnp.where(group == 2, 0, jnp.where(group == 3, 1, -1)))
    )


def build_shift_coarse(s_ref):
    row = iota((256, 384), 0)
    col = iota((256, 384), 1)
    source = (col % LANE + col // LANE + LANE - 1) % LANE
    halo = row - LANE
    spot = jnp.where(
        halo < 4, 127, jnp.where(halo < 8, 126, jnp.where(halo < 12, 64, jnp.where(halo < 16, 65, -1)))
    )
    own = (row < 64) & (row == source)
    other = (halo >= 0) & (spot == source)

    @pl.loop(0, 4)
    def _(x):
        s_ref[x] = one_hot(own | (other & (halo % 4 == x)))


def build_roll(r_ref):
    row = iota((LANE, 256), 0)
    col = iota((LANE, 256), 1)
    r_ref[...] = one_hot(row == (col % LANE + 2 * (col // LANE) + LANE - 1) % LANE)


def build_edges(fine_ref, coarse_ref):
    row = iota((1024, LANE), 0)
    col = iota((1024, LANE), 1)
    lane = row % LANE
    x = row // LANE
    fine_ref[...] = one_hot(((lane == 127) & (col == x)) | ((lane == 0) & (col == x + 8)))
    row = iota((512, LANE), 0)
    col = iota((512, LANE), 1)
    coarse_ref[...] = one_hot((row % LANE == coarse_edge(col // 4)) & (row // LANE == col % 4))


def build_places(e_ref, slots_ref, live_count):
    e_ref[...] = jnp.zeros_like(e_ref)
    row = iota((16, 256), 0)
    col = iota((16, 256), 1)
    y = row % 8
    own = (row // 8) == (col // LANE)
    spot = col % LANE - 64 * (y % 2) - y // 2

    @pl.loop(0, SLOTS)
    def _(s):
        place = jnp.where(s < live_count, slots_ref[0, s], 4096)
        tile = one_hot(own & (spot == 4 * place))
        for j in range(4):
            e_ref[pl.ds(pl.multiple_of(64 * s + 16 * j, 16), 16), 256 * j : 256 * j + 256] = tile


def live_lanes(slots_ref, live_count):
    spot = (iota((8, LANE), 1) % 64) // 4

    def step(s, total):
        place = jnp.where(s < live_count, slots_ref[0, s], 4096)
        return total + jnp.where(spot == place, 1.0, 0.0)

    return lax.fori_loop(0, SLOTS, step, jnp.zeros((8, LANE), F32))


def to_grid(blocks, work, e_ref, grid, after_outer=None):
    for t in range(8):
        lanes = slice(t * LANE, (t + 1) * LANE)
        for pair in range(4):
            one = blocks[2 * t, :, pair * LANE : (pair + 1) * LANE]
            two = blocks[2 * t + 1, :, pair * LANE : (pair + 1) * LANE]
            work[2 * pair, :, lanes] = jnp.concatenate([one[:, :64], two[:, :64]], axis=1)
            work[2 * pair + 1, :, lanes] = jnp.concatenate([one[:, 64:], two[:, 64:]], axis=1)

    for n in (0, 3, 1, 2):
        if n == 1 and after_outer is not None:
            after_outer()
        lanes = slice(n * 256, (n + 1) * 256)
        moved = dot(work[...].reshape(8 * C, 1024), e_ref[:, lanes])
        grid[:, :, lanes] = moved.astype(BF16).reshape(8, C, 256)


def to_blocks(grid, e_ref, blocks):
    for n in range(4):
        rows = slice(n * 256, (n + 1) * 256)
        moved = dot_t(grid[...].reshape(8 * C, 1024), e_ref[rows, :])
        moved = moved.astype(BF16).reshape(8, C, 256)
        for pair in range(4):
            for k in range(4):
                low = moved[2 * pair, :, 64 * k : 64 * k + 64]
                high = moved[2 * pair + 1, :, 64 * k : 64 * k + 64]
                blocks[4 * n + k, :, pair * LANE : (pair + 1) * LANE] = jnp.concatenate(
                    [low, high], axis=1
                )


def pack_edges(grid, depth, t_ref, packed):
    edges = dot(grid.reshape(depth * C, grid.shape[2]), t_ref[...]).reshape(depth, C, LANE)
    total = edges[0]
    for z in range(1, depth):
        total = total + pltpu.roll(edges[z], 16 * z, 1)
    packed[...] = total.astype(BF16)


def unpack_edges(received, row, left_ok, right_ok, depth):
    lane = iota((C, LANE), 1) % 16
    left = jnp.where(left_ok, received[2 * row].astype(F32), 0.0)
    right = jnp.where(right_ok, received[2 * row + 1].astype(F32), 0.0)
    both = jnp.where(lane < 8, left, right)
    parts = [both] + [pltpu.roll(both, LANE - 16 * z, 1) for z in range(1, depth)]
    return jnp.stack(parts, axis=0).astype(BF16).reshape(depth * C, LANE)


def widen(grid, sides, received, s_ref, wide, count, depth, place):
    gx, gy = place
    low_ok, high_ok = gx > 0, gx < NX - 1
    left_ok, right_ok = gy > 0, gy < NY - 1

    def put(rows, halo, x, lanes):
        moved = dot(jnp.concatenate([rows, halo], axis=1), s_ref[x]).astype(BF16)
        wide[:, 0:C, lanes] = moved[:, :LANE].reshape(depth, C, LANE)
        wide[:, C : 2 * C, lanes] = rows.reshape(depth, C, LANE)
        wide[:, 2 * C : 3 * C, lanes] = moved[:, LANE:].reshape(depth, C, LANE)

    zero = jnp.zeros((depth * C, LANE), BF16)
    halo = unpack_edges(received, 0, left_ok & low_ok, right_ok & low_ok, depth)
    rows = jnp.where(low_ok, sides[0].reshape(depth * C, LANE), zero)
    put(rows, halo, count - 1, pl.ds(0, LANE))
    halo = unpack_edges(received, 2, left_ok & high_ok, right_ok & high_ok, depth)
    rows = jnp.where(high_ok, sides[1].reshape(depth * C, LANE), zero)
    put(rows, halo, 0, pl.ds((count + 1) * LANE, LANE))
    halo = unpack_edges(received, 1, left_ok, right_ok, depth)

    for x in range(count):
        rows = grid[:, :, x * LANE : (x + 1) * LANE].reshape(depth * C, LANE)
        put(rows, halo, x, pl.ds((x + 1) * LANE, LANE))


def coarse_halos(received, place):
    gx, gy = place
    left_ok, right_ok = gy > 0, gy < NY - 1
    low_ok, high_ok = gx > 0, gx < NX - 1
    return (
        unpack_edges(received, 0, left_ok & low_ok, right_ok & low_ok, 4),
        unpack_edges(received, 1, left_ok, right_ok, 4),
        unpack_edges(received, 2, left_ok & high_ok, right_ok & high_ok, 4),
    )


def widen_coarse(grid, sides, received, s_ref, wide, place):
    gx = place[0]
    halos = coarse_halos(received, place)
    zero = jnp.zeros((4 * C, LANE), BF16)
    halves = []
    for side, inside in ((0, gx > 0), (1, gx < NX - 1)):
        rows = jnp.where(inside, sides[side].reshape(4 * C, LANE), zero)
        halves.append([rows, pltpu.roll(rows.astype(F32), 64, 1).astype(BF16)])
    for column in range(8):
        if column < 2:
            rows, halo, x = halves[0][column], halos[0], column + 2
        elif column < 6:
            x = column - 2
            rows = grid[:, :, x * LANE : (x + 1) * LANE].reshape(4 * C, LANE)
            halo = halos[1]
        else:
            x = column - 6
            rows, halo = halves[1][x], halos[2]
        moved = dot(jnp.concatenate([rows, halo], axis=1), s_ref[x]).astype(BF16)
        for t in range(3):
            part = moved[:, t * LANE : (t + 1) * LANE].reshape(4, C, LANE)
            wide[:, t * C : (t + 1) * C, column * LANE : (column + 1) * LANE] = part


def extend_grect(grect, sides, received, s_ref, wide, place):
    gx = place[0]
    halos = coarse_halos(received, place)
    zero = jnp.zeros((4 * C, LANE), F32)
    for column in range(6):
        if column == 0:
            rows = jnp.where(gx > 0, sides[0].reshape(4 * C, LANE).astype(F32), zero)
            halo, x = halos[0], 3
        elif column < 5:
            x = column - 1
            rows = grect[:, :, x * LANE : (x + 1) * LANE].reshape(4 * C, LANE)
            halo = halos[1]
        else:
            rows = jnp.where(gx < NX - 1, sides[1].reshape(4 * C, LANE).astype(F32), zero)
            halo, x = halos[2], 0
        total = rows + dot(halo, s_ref[x, LANE:, LANE : 2 * LANE])
        wide[:, :, column * LANE : (column + 1) * LANE] = total.reshape(4, C, LANE)


def roll_columns(grid, r_ref, wide):
    for column in range(6):
        lanes = slice(column * LANE, (column + 1) * LANE)
        rows = grid[:, :, lanes]
        moved = dot(rows.reshape(4 * C, LANE), r_ref[...]).astype(BF16)
        wide[:, 0:C, lanes] = moved[:, :LANE].reshape(4, C, LANE)
        wide[:, C : 2 * C, lanes] = rows
        wide[:, 2 * C : 3 * C, lanes] = moved[:, LANE:].reshape(4, C, LANE)


def window(wide, z, first, width):
    return jnp.concatenate(
        [wide[z, :, first + dx * LANE : first + dx * LANE + width] for dx in range(3)], axis=0
    )


def convolve(wide, weight, total, depth, width):
    for z in range(depth):
        for first in range(0, width, 256):
            piece = dot(weight[...], window(wide, z, first, 256)).reshape(3, C, 256)
            lanes = slice(first, first + 256)
            total[z : z + 3, :, lanes] = total[z : z + 3, :, lanes] + piece


def kernel_terms(grad, wide, total, depth, width, start):
    ahead = [grad[z : z + 3].reshape(3 * C, width) for z in range(depth)]
    pieces = [window(wide, z, start, width) for z in range(depth)]
    total[...] = dot_t(jnp.concatenate(ahead, axis=1), jnp.concatenate(pieces, axis=1))


def quarters(grid, wz):
    columns = []
    for a in range(2):
        for b in range(2):
            columns.append(
                jnp.concatenate(
                    [
                        grid[2 * wz + a, :, (2 * wx + b) * LANE : (2 * wx + b + 1) * LANE]
                        for wx in range(4)
                    ],
                    axis=1,
                )
            )
    return jnp.concatenate(columns, axis=0)


def tile_lanes(mask, rows, width):
    return jnp.broadcast_to(jnp.concatenate([mask] * (width // LANE), axis=1)[0:1], (rows, width))


def roll_half(value):
    parts = [
        pltpu.roll(value[:, k * LANE : (k + 1) * LANE], 64, 1) for k in range(value.shape[1] // LANE)
    ]
    return jnp.concatenate(parts, axis=1)


def kernel_rows(weight, stack, eye, forward, backward):
    for dz in range(3):
        for k in range(9):
            block = weight[9 * dz + k]
            forward[(2 - dz) * C : (3 - dz) * C, k * C : (k + 1) * C] = block
            stack[(8 - k) * C : (9 - k) * C, :] = block
        backward[dz * C : (dz + 1) * C, :] = dot_t(eye[0:C, 0:C], stack[...]).astype(BF16)


def step_rows(down, up, stage, eye, ddn, dga, uup, ugr):
    for o in range(C):
        stage[8 * o : 8 * o + 8, 0:C] = down[o].astype(F32)
    for k in range(4):
        for e in range(2):
            q = 2 * k + e
            block = stage[pl.ds(q, C, stride=8), :].astype(BF16)[:, 0:C]
            ddn[e * C : (e + 1) * C, k * C : (k + 1) * C] = block
            uup[k * C : (k + 1) * C, e * C : (e + 1) * C] = up[q]
    dga[...] = dot_t(eye[...], ddn[...]).astype(BF16)
    ugr[...] = dot_t(eye[0 : 2 * C, 0 : 2 * C], uup[...]).astype(BF16)


def slope(value):
    sigma = jax.nn.sigmoid(value)
    return sigma * (1.0 + value * (1.0 - sigma))


def section(
    slots_ref,
    count_ref,
    feat_hbm,
    cot_hbm,
    fine_hbm,
    down_hbm,
    coarse_hbm,
    up_hbm,
    blocks_out,
    blocks_ig,
    sums_a,
    sums_b,
    feat,
    cot_in,
    fine_w,
    down_w,
    coarse_w,
    up_w,
    stage,
    stack,
    eye,
    wf,
    wfb,
    wc,
    wcb,
    ddn,
    dga,
    uup,
    ugr,
    work,
    places,
    shift_f,
    shift_c,
    roll_c,
    edge_f,
    edge_c,
    fine,
    cot,
    fine3,
    hidden,
    act,
    low,
    low3,
    coarse,
    coarse2,
    grect,
    grect_low,
    grect_wide,
    rect2,
    gcoarse,
    gcoarse_own,
    gcoarse3,
    gdown2,
    ghid,
    ghid3,
    result,
    term_f,
    term_c,
    packed,
    sides_f,
    outer,
    sides_c,
    sides_g,
    edges_in,
    grads_a,
    first_in_a,
    chunk_a,
    second_in_a,
    grads_b,
    first_in_b,
    chunk_b,
    second_in_b,
    local_sem,
    send_sem,
    recv_sem,
    sum_send,
    sum_recv,
):
    gx = lax.axis_index("gx")
    gy = lax.axis_index("gy")
    here = (gx, gy)

    load_feat = pltpu.make_async_copy(feat_hbm, feat, local_sem.at[5])
    load_feat.start()
    loads = [
        pltpu.make_async_copy(source, target, local_sem.at[k])
        for k, (source, target) in enumerate(
            (
                (fine_hbm, fine_w),
                (down_hbm, down_w),
                (coarse_hbm, coarse_w),
                (up_hbm, up_w),
                (cot_hbm, cot_in),
            )
        )
    ]
    for load in loads:
        load.start()

    barrier = pltpu.get_barrier_semaphore()

    for d in (8, 7, 9, 6, 10, 5, 11, 4, 12, 3, 13, 2, 14, 1, 15):
        pl.semaphore_signal(
            barrier, inc=1, device_id=(lax.rem(gx + d, NX), gy), device_id_type=MESH
        )
        pl.semaphore_signal(
            barrier, inc=1, device_id=(gx, lax.rem(gy + d, NY)), device_id_type=MESH
        )

    for dx in (1, NX - 1):
        for dy in (1, NY - 1):
            pl.semaphore_signal(
                barrier,
                inc=1,
                device_id=(lax.rem(gx + dx, NX), lax.rem(gy + dy, NY)),
                device_id_type=MESH,
            )

    live_count = count_ref[0, 0]
    build_places(places, slots_ref, live_count)
    build_edges(edge_f, edge_c)
    live = live_lanes(slots_ref, live_count)
    half_live = jnp.where(iota((8, LANE), 1) < 64, live, 0.0)
    lower = jnp.where(iota((8, LANE), 1) < 64, 1.0, 0.0)

    def exchange_edges(step):
        copies = []
        for row in (0, 2, 1):
            for side in range(2):
                copies.append(
                    pltpu.make_async_remote_copy(
                        src_ref=packed.at[step],
                        dst_ref=edges_in.at[step, 2 * row + side],
                        send_sem=send_sem.at[step, 2 + 2 * row + side],
                        recv_sem=recv_sem.at[step, 2 + 2 * row + side],
                        device_id=(
                            lax.rem(gx + NX + 1 - row, NX),
                            lax.rem(gy + (1 if side == 0 else NY - 1), NY),
                        ),
                        device_id_type=MESH,
                    )
                )
        for copy in copies:
            copy.start()
        return copies

    def exchange_sides(step, sources, sides):
        copies = []
        for side in range(2):
            copies.append(
                pltpu.make_async_remote_copy(
                    src_ref=sources[side],
                    dst_ref=sides.at[side],
                    send_sem=send_sem.at[step, side],
                    recv_sem=recv_sem.at[step, side],
                    device_id=(lax.rem(gx + (1 if side == 0 else NX - 1), NX), gy),
                    device_id_type=MESH,
                )
            )
        for copy in copies:
            copy.start()
        return copies

    def outer_columns(source, length):
        return [source.at[:, :, pl.ds(first, LANE)] for first in (length - LANE, 0)]

    def reduction(grads, first_in, chunk, second_in, sums, part, steps):
        rows = chunk.shape[1]

        def chunk_rows(index):
            return pl.ds(pl.multiple_of(index * rows, rows), rows)

        def first(d):
            peer = lax.rem(gy + d, NY)
            return pltpu.make_async_remote_copy(
                src_ref=grads.at[chunk_rows(peer)],
                dst_ref=first_in.at[d],
                send_sem=sum_send.at[part, 0, d],
                recv_sem=sum_recv.at[part, 0, d],
                device_id=(gx, peer),
                device_id_type=MESH,
            )

        def second(d):
            return pltpu.make_async_remote_copy(
                src_ref=chunk.at[0],
                dst_ref=second_in.at[d],
                send_sem=sum_send.at[part, 1, d],
                recv_sem=sum_recv.at[part, 1, d],
                device_id=(lax.rem(gx + d, NX), gy),
                device_id_type=MESH,
            )

        def second_x(d):
            x = lax.rem(gx, 4)
            return pltpu.make_async_remote_copy(
                src_ref=chunk.at[0],
                dst_ref=second_in.at[d],
                send_sem=sum_send.at[part, 1, d],
                recv_sem=sum_recv.at[part, 1, d],
                device_id=(gx - x + lax.rem(x + d, 4), gy),
                device_id_type=MESH,
            )

        def second_z(d):
            return pltpu.make_async_remote_copy(
                src_ref=chunk.at[2],
                dst_ref=second_in.at[4 + d],
                send_sem=sum_send.at[part, 1, 4 + d],
                recv_sem=sum_recv.at[part, 1, 4 + d],
                device_id=(lax.rem(gx + 4 * d, NX), gy),
                device_id_type=MESH,
            )

        def third(d):
            return pltpu.make_async_remote_copy(
                src_ref=chunk.at[1],
                dst_ref=sums.at[chunk_rows(gy)],
                send_sem=sum_send.at[part, 2, d],
                recv_sem=sum_recv.at[part, 2, d],
                device_id=(gx, lax.rem(gy + d, NY)),
                device_id_type=MESH,
            )

        flying = {}

        def start_first():
            flying["first"] = start_all(first)

        def start_second():
            wait_all(flying["first"])
            own = grads[chunk_rows(gy), :].astype(F32)
            for d in range(1, NY):
                own = own + first_in[d].astype(F32)
            chunk[0] = own.astype(BF16)
            flying["second"] = start_all(second) if steps == 1 else start_all(second_x, 4)
            return own

        def start_middle(own):
            wait_all(flying["second"])
            for d in range(1, 4):
                own = own + second_in[d].astype(F32)
            chunk[2] = own.astype(BF16)
            flying["second"] = start_all(second_z, 4)
            return own

        def start_third(own):
            wait_all(flying["second"])
            for d in range(1, NX) if steps == 1 else range(5, 8):
                own = own + second_in[d].astype(F32)
            chunk[1] = own.astype(BF16)
            flying["third"] = start_all(third)
            sums[chunk_rows(gy), :] = chunk[1]

        def finish():
            wait_all(flying["third"])

        return start_first, start_second, start_middle, start_third, finish

    sent = []

    def start_all(copy, count=NX):
        started = [copy(d) for d in range(1, count)]
        for one in started:
            one.start()
        sent.extend(started)
        return started

    def wait_all(started):
        for one in started:
            one.wait_recv()

    def put_rows(grads, term):
        for k in range(3):
            grads[3 * C * k : 3 * C * (k + 1), :] = term[:, k * LANE : (k + 1) * LANE].astype(BF16)
        tail = term[:, 3 * LANE :]
        grads[9 * C : 9 * C + 72, 0:C] = tail[0:72].astype(BF16)
        grads[9 * C : 9 * C + 72, C : 2 * C] = tail[72:144].astype(BF16)

    load_feat.wait()
    copies = []

    def send_sides():
        pl.semaphore_wait(barrier, 2 * (NX - 1) + 4)
        copies.extend(exchange_sides(0, outer_columns(fine, 1024), sides_f.at[0]))

    to_grid(feat, work, places, fine, send_sides)
    pack_edges(fine[...], 8, edge_f, packed.at[0])
    copies = copies + exchange_edges(0)

    for load in loads:
        load.wait()
    build_shift_coarse(shift_c)
    to_grid(cot_in, work, places, cot)
    eye[...] = one_hot(iota((4 * C, 4 * C), 0) == iota((4 * C, 4 * C), 1))
    stage[...] = jnp.zeros_like(stage)
    step_rows(down_w, up_w, stage, eye, ddn, dga, uup, ugr)
    lower_mask = tile_lanes(lower, C, 512)
    for wz in range(4):
        both = dot(ugr[...], quarters(cot, wz))
        value = (both[:C] + roll_half(both[C:])) * lower_mask
        grect[wz] = value
        grect_low[wz] = value.astype(BF16)
    pack_edges(grect_low[...], 4, edge_c, packed.at[2])
    build_shift_fine(shift_f)
    kernel_rows(fine_w, stack, eye, wf, wfb)
    hidden[...] = jnp.zeros_like(hidden)

    for copy in copies:
        copy.wait()
    grect_copies = exchange_edges(2) + exchange_sides(2, outer_columns(grect_low, 512), sides_g)
    widen(fine, sides_f.at[0], edges_in.at[0], shift_f, fine3, 8, 8, here)
    convolve(fine3, wf, hidden, 8, 1024)

    live_fine = tile_lanes(live, C, 1024)
    for z in range(8):
        value = hidden[z + 1] * live_fine
        hidden[z + 1] = value
        act[z] = (value * jax.nn.sigmoid(value)).astype(BF16)

    for wz in range(4):
        both = dot(ddn[...], quarters(act, wz))
        value = (both[:C] + roll_half(both[C:])) * lower_mask
        low[wz] = value.astype(BF16)
        for side, first in ((0, 2 * LANE), (1, 0)):
            second = pltpu.roll(value[:, first + LANE : first + 2 * LANE], 64, 1)
            outer[side, wz] = (value[:, first : first + LANE] + second).astype(BF16)

    copies = exchange_sides(1, [outer.at[0], outer.at[1]], sides_c)
    pack_edges(low[...], 4, edge_c, packed.at[1])
    copies = copies + exchange_edges(1)
    build_roll(roll_c)
    kernel_rows(coarse_w, stack, eye, wc, wcb)
    grads_a[...] = jnp.zeros_like(grads_a)
    grads_b[...] = jnp.zeros_like(grads_b)
    gcoarse_own[...] = jnp.zeros_like(gcoarse_own)
    coarse[...] = jnp.zeros_like(coarse)
    ghid[0] = jnp.zeros((C, 1024), BF16)
    ghid[9] = jnp.zeros((C, 1024), BF16)
    coarse2[...] = jnp.zeros_like(coarse2)
    for copy in grect_copies:
        copy.wait()
    extend_grect(grect, sides_g, edges_in.at[2], shift_c, grect_wide, here)
    for copy in copies:
        copy.wait()
    widen_coarse(low, sides_c, edges_in.at[1], shift_c, low3, here)
    convolve(low3, wc, coarse, 4, 768)

    for wz in range(4):
        value = coarse[wz + 1]
        grad = grect_wide[wz] * slope(value)
        gcoarse[wz] = grad.astype(BF16)
        gcoarse_own[wz + 1] = (grad[:, LANE : 5 * LANE] * lower_mask).astype(BF16)
        value = value[:, LANE : 5 * LANE]
        rect = value * jax.nn.sigmoid(value) * lower_mask
        rect2[wz, 0:C] = rect.astype(BF16)
        rect2[wz, C : 2 * C] = roll_half(rect).astype(BF16)

    roll_columns(gcoarse, roll_c, gcoarse3)
    convolve(gcoarse3, wcb, coarse2, 4, 512)

    live_coarse = tile_lanes(half_live, C, 512)
    for wz in range(4):
        value = coarse2[wz + 1] * live_coarse
        gdown2[wz, 0:C] = value.astype(BF16)
        gdown2[wz, C : 2 * C] = roll_half(value).astype(BF16)
        back = dot(dga[...], gdown2[wz])
        for a in range(2):
            for b in range(2):
                k = 2 * a + b
                for wx in range(4):
                    lanes = pl.ds((2 * wx + b) * LANE, LANE)
                    piece = back[k * C : (k + 1) * C, wx * LANE : (wx + 1) * LANE]
                    ghid[2 * wz + a + 1, :, lanes] = (
                        cot[2 * wz + a, :, lanes].astype(F32)
                        + piece * slope(hidden[2 * wz + a + 1, :, lanes])
                    ).astype(BF16)

    first_a, second_a, _, third_a, finish_a = reduction(
        grads_a, first_in_a, chunk_a, second_in_a, sums_a, 0, 1
    )
    first_b, second_b, middle_b, third_b, finish_b = reduction(
        grads_b, first_in_b, chunk_b, second_in_b, sums_b, 1, 2
    )
    kernel_terms(gcoarse_own, low3, term_c, 4, 512, LANE)
    total_u = jnp.zeros((4 * C, 2 * C), F32)
    total_d = jnp.zeros((2 * C, 4 * C), F32)
    for wz in range(4):
        total_u = total_u + dot_t(quarters(cot, wz), rect2[wz])
        total_d = total_d + dot_t(gdown2[wz], quarters(act, wz))
    put_rows(grads_b, term_c)
    low_d = total_d[:, 0:LANE].astype(BF16)
    high_d = total_d[:, LANE:192].astype(BF16)
    grads_b[512:704, 0 : 2 * C] = total_u.astype(BF16)
    grads_b[512:608, 96:LANE] = high_d[:, 0:32]
    grads_b[608:704, 96:LANE] = high_d[:, 32:64]
    grads_b[704:768, :] = low_d[0:64]
    grads_b[432:464, 96:LANE] = low_d[64:96, 0:32]
    grads_b[464:496, 96:LANE] = low_d[64:96, 32:64]
    grads_a[432:464, 96:LANE] = low_d[64:96, 64:96]
    grads_a[464:496, 96:LANE] = low_d[64:96, 96:LANE]
    first_b()
    kernel_terms(ghid, fine3, term_f, 8, 1024, 0)
    put_rows(grads_a, term_f)
    first_a()
    pack_edges(ghid[1:9], 8, edge_f, packed.at[3])
    copies = exchange_edges(3)
    copies = copies + exchange_sides(3, outer_columns(ghid.at[pl.ds(1, 8)], 1024), sides_f.at[1])

    for wz in range(4):
        upward = dot(uup[...], rect2[wz])
        for a in range(2):
            for b in range(2):
                k = 2 * a + b
                for wx in range(4):
                    lanes = pl.ds((2 * wx + b) * LANE, LANE)
                    piece = upward[k * C : (k + 1) * C, wx * LANE : (wx + 1) * LANE]
                    result[2 * wz + a, :, lanes] = (
                        hidden[2 * wz + a + 1, :, lanes] + piece
                    ).astype(BF16)
    to_blocks(result, places, blocks_out)
    hidden[...] = jnp.zeros_like(hidden)
    own_b = second_b()
    own_a = second_a()
    own_b = middle_b(own_b)

    for copy in copies:
        copy.wait()
    widen(ghid.at[pl.ds(1, 8)], sides_f.at[1], edges_in.at[3], shift_f, ghid3, 8, 8, here)
    convolve(ghid3, wfb, hidden, 8, 1024)
    for z in range(8):
        result[z] = hidden[z + 1].astype(BF16)
    to_blocks(result, places, blocks_ig)

    third_b(own_b)
    third_a(own_a)
    finish_b()
    finish_a()
    for one in sent:
        one.wait_send()


def unpack(
    sums_a,
    sums_b,
    out_in,
    ig_in,
    out_hbm,
    ig_hbm,
    gf_hbm,
    gd_hbm,
    gc_hbm,
    gu_hbm,
    gf,
    gd,
    gc,
    gu,
    stage,
    sem,
):
    copies = [
        pltpu.make_async_copy(source, target, sem.at[k])
        for k, (source, target) in enumerate(
            (
                (gf, gf_hbm),
                (gc, gc_hbm),
                (gu, gu_hbm),
                (gd, gd_hbm),
                (out_in, out_hbm),
                (ig_in, ig_hbm),
            )
        )
    ]
    copies[4].start()
    copies[5].start()
    scale = 1.0 / math.sqrt(SLOTS * 512 * NX * NY)

    for part, (sums, target) in enumerate(((sums_a, gf), (sums_b, gc))):
        tail = sums[9 * C : 9 * C + 80, :].astype(F32)
        tail = jnp.concatenate([tail[0:72, 0:C], tail[0:72, C : 2 * C]], axis=0)
        rows = jnp.concatenate(
            [sums[3 * C * k : 3 * C * (k + 1), :].astype(F32) for k in range(3)] + [tail], axis=1
        )
        rows = rows * scale
        for dz in range(3):
            for k in range(9):
                block = rows[(2 - dz) * C : (3 - dz) * C, k * C : (k + 1) * C]
                target[9 * dz + k] = block
        copies[part].start()
    for k in range(4):
        for e in range(2):
            block = sums_b[512 + k * C : 512 + (k + 1) * C, e * C : (e + 1) * C]
            gu[2 * k + e] = block.astype(F32) * scale
    copies[2].start()
    last = jnp.concatenate(
        [
            sums[first : first + 32, 96:LANE].astype(F32)
            for sums in (sums_b, sums_a)
            for first in (432, 464)
        ],
        axis=1,
    )
    low = jnp.concatenate([sums_b[704:768, :].astype(F32), last], axis=0)
    high = jnp.concatenate(
        [sums_b[512:608, 96:LANE].astype(F32), sums_b[608:704, 96:LANE].astype(F32)], axis=1
    )
    rows = jnp.concatenate([low, high], axis=1) * scale
    for k in range(4):
        for e in range(2):
            block = rows[e * C : (e + 1) * C, k * C : (k + 1) * C]
            stage[pl.ds(2 * k + e, C, stride=8), :] = jnp.concatenate(
                [block, jnp.zeros((C, LANE - C), F32)], axis=1
            )
    for o in range(C):
        gd[o] = stage[8 * o : 8 * o + 8, 0:C]
    copies[3].start()
    for copy in copies:
        copy.wait()


def on_device(
    features, block_slots, block_count, cotangent, fine_weight, down_weight, coarse_weight, up_weight
):
    vmem = pl.BlockSpec(memory_space=pltpu.VMEM)
    smem = pl.BlockSpec(memory_space=pltpu.SMEM)
    hbm = pl.BlockSpec(memory_space=pltpu.HBM)
    blocks = (SLOTS, C, 512)
    kernel_shape = (27, C, C)
    block_shape = jax.ShapeDtypeStruct(blocks, BF16)
    out, ig, sums_a, sums_b = pl.pallas_call(
        section,
        out_shape=(
            block_shape,
            block_shape,
            jax.ShapeDtypeStruct((ROWS_A, LANE), BF16),
            jax.ShapeDtypeStruct((ROWS_B, LANE), BF16),
        ),
        in_specs=[smem, smem] + [hbm] * 6,
        out_specs=(vmem, vmem, vmem, vmem),
        scratch_shapes=[
            pltpu.VMEM(blocks, BF16),
            pltpu.VMEM(blocks, BF16),
            pltpu.VMEM(kernel_shape, BF16),
            pltpu.VMEM((C, 8, C), BF16),
            pltpu.VMEM(kernel_shape, BF16),
            pltpu.VMEM((8, C, C), BF16),
            pltpu.VMEM((8 * C, LANE), F32),
            pltpu.VMEM((9 * C, C), BF16),
            pltpu.VMEM((4 * C, 4 * C), BF16),
            pltpu.VMEM((3 * C, 9 * C), BF16),
            pltpu.VMEM((3 * C, 9 * C), BF16),
            pltpu.VMEM((3 * C, 9 * C), BF16),
            pltpu.VMEM((3 * C, 9 * C), BF16),
            pltpu.VMEM((2 * C, 4 * C), BF16),
            pltpu.VMEM((4 * C, 2 * C), BF16),
            pltpu.VMEM((4 * C, 2 * C), BF16),
            pltpu.VMEM((2 * C, 4 * C), BF16),
            pltpu.VMEM((8, C, 1024), BF16),
            pltpu.VMEM((1024, 1024), BF16),
            pltpu.VMEM((8, 256, 256), BF16),
            pltpu.VMEM((4, 256, 384), BF16),
            pltpu.VMEM((LANE, 256), BF16),
            pltpu.VMEM((1024, LANE), BF16),
            pltpu.VMEM((512, LANE), BF16),
            pltpu.VMEM((8, C, 1024), BF16),
            pltpu.VMEM((8, C, 1024), BF16),
            pltpu.VMEM((8, 3 * C, 1280), BF16),
            pltpu.VMEM((10, C, 1024), F32),
            pltpu.VMEM((8, C, 1024), BF16),
            pltpu.VMEM((4, C, 512), BF16),
            pltpu.VMEM((4, 3 * C, 1024), BF16),
            pltpu.VMEM((6, C, 768), F32),
            pltpu.VMEM((6, C, 512), F32),
            pltpu.VMEM((4, C, 512), F32),
            pltpu.VMEM((4, C, 512), BF16),
            pltpu.VMEM((4, C, 768), F32),
            pltpu.VMEM((4, 2 * C, 512), BF16),
            pltpu.VMEM((4, C, 768), BF16),
            pltpu.VMEM((6, C, 512), BF16),
            pltpu.VMEM((4, 3 * C, 768), BF16),
            pltpu.VMEM((4, 2 * C, 512), BF16),
            pltpu.VMEM((10, C, 1024), BF16),
            pltpu.VMEM((8, 3 * C, 1280), BF16),
            pltpu.VMEM((8, C, 1024), BF16),
            pltpu.VMEM((3 * C, 9 * C), F32),
            pltpu.VMEM((3 * C, 9 * C), F32),
            pltpu.VMEM((4, C, LANE), BF16),
            pltpu.VMEM((2, 2, 8, C, LANE), BF16),
            pltpu.VMEM((2, 4, C, LANE), BF16),
            pltpu.VMEM((2, 4, C, LANE), BF16),
            pltpu.VMEM((2, 4, C, LANE), BF16),
            pltpu.VMEM((4, 6, C, LANE), BF16),
            pltpu.VMEM((ROWS_A, LANE), BF16),
            pltpu.VMEM((NY, ROWS_A // NY, LANE), BF16),
            pltpu.VMEM((2, ROWS_A // NY, LANE), BF16),
            pltpu.VMEM((NX, ROWS_A // NY, LANE), BF16),
            pltpu.VMEM((ROWS_B, LANE), BF16),
            pltpu.VMEM((NY, ROWS_B // NY, LANE), BF16),
            pltpu.VMEM((3, ROWS_B // NY, LANE), BF16),
            pltpu.VMEM((NX, ROWS_B // NY, LANE), BF16),
            pltpu.SemaphoreType.DMA((6,)),
            pltpu.SemaphoreType.DMA((4, 8)),
            pltpu.SemaphoreType.DMA((4, 8)),
            pltpu.SemaphoreType.DMA((2, 3, NX)),
            pltpu.SemaphoreType.DMA((2, 3, NX)),
        ],
        compiler_params=pltpu.CompilerParams(
            collective_id=0, has_side_effects=True, vmem_limit_bytes=50 * 1024 * 1024
        ),
        name="section",
    )(
        pltpu.with_memory_space_constraint(block_slots.reshape(1, SLOTS), pltpu.HBM),
        block_count.reshape(1, 1),
        *(
            pltpu.with_memory_space_constraint(value, pltpu.HBM)
            for value in (
                features.reshape(blocks),
                cotangent.reshape(blocks),
                fine_weight.transpose(1, 0, 2),
                down_weight,
                coarse_weight.transpose(1, 0, 2),
                up_weight,
            )
        ),
    )
    out, ig, gf, gd, gc, gu = pl.pallas_call(
        unpack,
        out_shape=(
            block_shape,
            block_shape,
            jax.ShapeDtypeStruct(kernel_shape, F32),
            jax.ShapeDtypeStruct((C, 8, C), F32),
            jax.ShapeDtypeStruct(kernel_shape, F32),
            jax.ShapeDtypeStruct((8, C, C), F32),
        ),
        in_specs=[vmem, vmem, vmem, vmem],
        out_specs=(hbm,) * 6,
        scratch_shapes=[
            pltpu.VMEM(kernel_shape, F32),
            pltpu.VMEM((C, 8, C), F32),
            pltpu.VMEM(kernel_shape, F32),
            pltpu.VMEM((8, C, C), F32),
            pltpu.VMEM((8 * C, LANE), F32),
            pltpu.SemaphoreType.DMA((6,)),
        ],
        compiler_params=pltpu.CompilerParams(vmem_limit_bytes=8 * 1024 * 1024),
        name="unpack",
    )(sums_a, sums_b, out, ig)
    shape_out = (1, 1) + blocks
    gf, gc = gf.transpose(1, 0, 2), gc.transpose(1, 0, 2)
    return out.reshape(shape_out), ig.reshape(shape_out), gf, gd, gc, gu


def solution(mesh):
    split = P("gx", "gy", None, None, None)
    return jax.shard_map(
        on_device,
        mesh=mesh,
        in_specs=(split, P("gx", "gy", None), P("gx", "gy"), split, P(), P(), P(), P()),
        out_specs=(split, split, P(), P(), P(), P()),
        check_vma=False,
    )
```
